32 devices in a mesh: dp: 4 (over y, core), ctx: 8 (over z, x).
Axes of the slice: x: 2, y: 2, z: 4, core: 2. Of those that a mesh axis runs over, the one named last changes fastest.
Arguments:
- tokens: bfloat16 [4, 1024, 1024], P('dp', 'ctx'), may hold values from -8 to 8
- lengths: int32 [4], P('dp'), may hold values from 256 to 1024, as said below
- attn_gain: float32 [1024], replicated, may hold values from 0.25 to 1.75
- q_gain: float32 [64], replicated, may hold values from 0.25 to 1.75
- k_gain: float32 [64], replicated, may hold values from 0.25 to 1.75
- w_query: bfloat16 [1024, 1024], replicated, may hold values from -0.1875 to 0.1875
- w_key: bfloat16 [1024, 512], replicated, may hold values from -0.1875 to 0.1875
- w_value: bfloat16 [1024, 512], replicated, may hold values from -0.1875 to 0.1875
- w_out: bfloat16 [1024, 1024], replicated, may hold values from -3 to 3
- ffn_gain: float32 [1024], replicated, may hold values from 0.25 to 1.75
- w_gate: bfloat16 [1024, 4608], replicated, may hold values from -0.1875 to 0.1875
- w_up: bfloat16 [1024, 4608], replicated, may hold values from -0.1875 to 0.1875
- w_down: bfloat16 [4608, 1024], replicated, may hold values from -0.09375 to 0.09375
- cotangent: bfloat16 [4, 1024, 1024], P('dp', 'ctx'), may hold values from -8 to 8
Outputs:
- result: bfloat16 [4, 1024, 1024], P('dp', 'ctx')
- grad_tokens: float32 [4, 1024, 1024], P('dp', 'ctx')
- attn_gain_grad: float32 [1024], replicated
- q_gain_grad: float32 [64], replicated
- k_gain_grad: float32 [64], replicated
- query_grad: float32 [1024, 1024], P(('dp', 'ctx'))
- key_grad: float32 [1024, 512], P(('dp', 'ctx'))
- value_grad: float32 [1024, 512], P(('dp', 'ctx'))
- out_grad: float32 [1024, 1024], P(None, ('dp', 'ctx'))
- ffn_gain_grad: float32 [1024], replicated
- gate_grad: float32 [1024, 4608], P(('dp', 'ctx'))
- up_grad: float32 [1024, 4608], P(('dp', 'ctx'))
- down_grad: float32 [4608, 1024], P(None, ('dp', 'ctx'))
The draws below stay inside these ranges and needn't reach their ends.
Inputs may be any that keep to these rules, and one draw needn't show every extreme that they name: `lengths`: each sequence's true length; at least one sequence fills all 1024 slots.
All inputs are finite; a program needn't handle non-finite values.
Results may differ from the reference program's by a relative error of at most 0.018.
Values may be sent and summed in bfloat16 or wider, within the bound.
No kernel may reach another device: no remote copies, remote signals or barrier semaphores. Data moves between devices by JAX's collectives and lax.ppermute only.
A program may use at most 320 MiB of HBM per device.

```python
import math
import jax
import jax.numpy as jnp
from jax import lax

D = 1024
HEADS = 16
KV_HEADS = 8
HEAD_DIM = 64
FF = 4608
SEQS = 4
SEQ_LEN = 1024


def draw_lengths(key, part):
    first_key, second_key = jax.random.split(key)
    drawn = jax.random.randint(first_key, (SEQS,), SEQ_LEN // 4, SEQ_LEN + 1)
    full_index = jax.random.randint(second_key, (), 0, SEQS)
    return jnp.where(jnp.arange(SEQS) == full_index, SEQ_LEN, drawn).astype(jnp.int32)


def strengthened(result, own_key, source, target, parts, factor):
    def block_of(position):
        return (jnp.arange(result.shape[position]) // (result.shape[position] // parts)).reshape((-1,) + (1,) * (result.ndim - 1 - position))

    one_side = jax.random.permutation(own_key, parts)[block_of(target)]
    second = (block_of(target) + parts // 2) % parts
    return jnp.where((block_of(source) == one_side) | (block_of(source) == second), factor * result, result)


def steps_of(key, shape, shards, low, largest):
    loudness = 1.0
    for axis_at, blocks in shards:
        steps = jax.random.uniform(jax.random.fold_in(jax.random.fold_in(key, 6), axis_at), (blocks,), jnp.float32, low / len(shards), largest / len(shards))
        loudness = loudness * jnp.repeat(jnp.exp(steps), shape[axis_at] // blocks).reshape((-1,) + (1,) * (len(shape) - 1 - axis_at))
    return loudness


def centred(own_key, extent, scale, limit, pieces=(), held_as=jnp.bfloat16):
    array = jax.random.normal(own_key, extent, jnp.float32) * scale
    if len(pieces) > 0:
        array = steps_of(own_key, extent, pieces, -0.22, 0.18) * array
    return jnp.clip(array, min=-limit, max=limit).astype(held_as)


def heavy_noise(stream_key, shape, scale, reach, shards, heavy, held_as=jnp.bfloat16):
    values = scale * jax.random.normal(stream_key, shape, jnp.float32)
    if shards:
        values = values * steps_of(stream_key, shape, shards, -0.22, 0.18)
    return jnp.clip(strengthened(values, jax.random.fold_in(stream_key, 3), *heavy), -reach, reach).astype(held_as)


def setup_inputs(seed: int = 0) -> dict:
    arg_keys = jax.random.split(jax.random.key(seed), 15)
    return {
        "tokens": heavy_noise(arg_keys[0], (SEQS, SEQ_LEN, D), 1.0, 8.0, ((0, 4), (1, 8)), (1, 2, 8, 2.0)),
        "lengths": draw_lengths(jax.random.fold_in(arg_keys[14], 71), 0),
        "attn_gain": jnp.clip(1.0 + 0.15 * jax.random.normal(arg_keys[2], (D,), jnp.float32), 0.25, 1.75),
        "q_gain": jnp.clip(1.0 + 0.15 * jax.random.normal(arg_keys[3], (HEAD_DIM,), jnp.float32), 0.25, 1.75),
        "k_gain": jnp.clip(1.0 + 0.15 * jax.random.normal(arg_keys[4], (HEAD_DIM,), jnp.float32), 0.25, 1.75),
        "w_query": centred(arg_keys[5], (D, HEADS * HEAD_DIM), D ** -0.5, 0.1875),
        "w_key": centred(arg_keys[6], (D, KV_HEADS * HEAD_DIM), D ** -0.5, 0.1875),
        "w_value": centred(arg_keys[7], (D, KV_HEADS * HEAD_DIM), D ** -0.5, 0.1875),
        "w_out": centred(arg_keys[8], (HEADS * HEAD_DIM, D), (max(1, HEADS * HEAD_DIM // 256)) ** -0.5, 3.0),
        "ffn_gain": jnp.clip(1.0 + 0.15 * jax.random.normal(arg_keys[9], (D,), jnp.float32), 0.25, 1.75),
        "w_gate": centred(arg_keys[10], (D, FF), D ** -0.5, 0.1875),
        "w_up": centred(arg_keys[11], (D, FF), D ** -0.5, 0.1875),
        "w_down": centred(arg_keys[12], (FF, D), FF ** -0.5, 0.09375),
        "cotangent": heavy_noise(arg_keys[13], (SEQS, SEQ_LEN, D), 1.0, 8.0, ((0, 4), (1, 8)), (1, 2, 8, 2.0)),
    }


EPS = 1e-05
THETA = 1000000.0
MASKED = -1e+30
HIGHEST = lax.Precision.HIGHEST

@jax.custom_vjp
def low(v):
    return lax.optimization_barrier(v.astype(jnp.bfloat16)).astype(jnp.float32)

@jax.custom_vjp
def low_back(v):
    return v

def low_keep(v):
    return (low(v), None)

def low_pass(kept, grad):
    return (grad,)

def back_keep(v):
    return (v, None)

def back_low(kept, grad):
    return (low(grad),)
low.defvjp(low_keep, low_pass)
low_back.defvjp(back_keep, back_low)

def root_norm(values, gain):
    return values * lax.rsqrt(lax.optimization_barrier(jnp.mean(values * values, axis=-1, keepdims=True)) + EPS) * gain

def rotate(values, cosine, sine):
    half = values.shape[-1] // 2
    first_half = values[..., :half]
    second_half = values[..., half:]
    return jnp.concatenate([first_half * cosine - second_half * sine, second_half * cosine + first_half * sine], axis=-1)

def angles(positions, width):
    freqs = THETA ** (-(jnp.arange(width // 2, dtype=jnp.float32) * 2.0 / width))
    turned = positions.astype(jnp.float32)[:, None] * freqs[None, :]
    return (jnp.cos(turned), jnp.sin(turned))

def seq_forward(params, inputs, length):
    attn_gain, q_gain, k_gain, w_query, w_key, w_value, w_out, ffn_gain, w_gate, w_up, w_down = params
    head_dim = q_gain.shape[0]
    heads = w_query.shape[1] // head_dim
    kv_heads = w_key.shape[1] // head_dim
    groups = heads // kv_heads
    positions = jnp.arange(SEQ_LEN, dtype=jnp.int32)
    cosine, sine = angles(positions, head_dim)
    cosine = cosine[:, None, :]
    sine = sine[:, None, :]
    acts = low(root_norm(inputs, attn_gain))
    qproj = low_back(jnp.dot(acts, w_query, precision=HIGHEST))
    kproj = low_back(jnp.dot(acts, w_key, precision=HIGHEST))
    vproj = low_back(jnp.dot(acts, w_value, precision=HIGHEST))
    queries = low(rotate(root_norm(qproj.reshape(SEQ_LEN, heads, head_dim), q_gain), cosine, sine))
    queries = queries.reshape(SEQ_LEN, kv_heads, groups, head_dim)
    keys = low(rotate(root_norm(kproj.reshape(SEQ_LEN, kv_heads, head_dim), k_gain), cosine, sine))
    values = low(vproj.reshape(SEQ_LEN, kv_heads, head_dim))
    span = math.gcd(512, SEQ_LEN)

    def attend(item):
        query_block, query_pos = item
        scores = low_back(0.125 * jnp.einsum('tcgd,ucd->cgtu', query_block, keys, precision=HIGHEST))
        counted = ((positions[None, :] <= query_pos[:, None]) & (positions[None, :] < length))[None, None]
        masked = jnp.where(counted, scores, MASKED)
        top_row = lax.optimization_barrier(jnp.max(masked, axis=-1, keepdims=True))
        weights = jnp.where(counted, jnp.exp(masked - top_row), 0.0)
        row_total = lax.optimization_barrier(jnp.sum(weights, axis=-1, keepdims=True))
        attended = jnp.einsum('cgtu,ucd->cgtd', low(weights), values, precision=HIGHEST) / row_total
        return attended.transpose(2, 0, 1, 3)
    blocks = lax.map(jax.checkpoint(attend), (queries.reshape(SEQ_LEN // span, span, kv_heads, groups, head_dim), positions.reshape(SEQ_LEN // span, span)))
    attn_low = low(low_back(blocks.reshape(SEQ_LEN, heads * head_dim)))
    middle = inputs + low_back(jnp.dot(attn_low, w_out, precision=HIGHEST))
    inner = low(root_norm(middle, ffn_gain))
    gate_proj = low_back(jnp.dot(inner, w_gate, precision=HIGHEST))
    up_proj = low_back(jnp.dot(inner, w_up, precision=HIGHEST))
    hidden = low(jax.nn.silu(gate_proj) * up_proj)
    return middle + low_back(jnp.dot(hidden, w_down, precision=HIGHEST))

def reference(tokens, lengths, attn_gain, q_gain, k_gain, w_query, w_key, w_value, w_out, ffn_gain, w_gate, w_up, w_down, cotangent):
    params = tuple((item.astype(jnp.float32) for item in (attn_gain, q_gain, k_gain, w_query, w_key, w_value, w_out, ffn_gain, w_gate, w_up, w_down)))

    def per_sequence(totals, item):
        inputs, incoming, length = item
        valid = (jnp.arange(SEQ_LEN, dtype=jnp.int32) < length).astype(jnp.float32)
        output, pull_back = jax.vjp(lambda weights, rows_in: seq_forward(weights, rows_in, length), params, inputs)
        grads, grad_inputs = pull_back(incoming * valid[:, None])
        totals = jax.tree.map(lambda left, right: left + right, totals, grads)
        return (totals, (output.astype(jnp.bfloat16), grad_inputs))
    start_sums = tuple((jnp.zeros(item.shape, jnp.float32) for item in params))
    sums, (outputs, grad_inputs) = lax.scan(per_sequence, start_sums, (tokens.astype(jnp.float32), cotangent.astype(jnp.float32), lengths))
    return (outputs, grad_inputs, sums[0], sums[1], sums[2], sums[3], sums[4], sums[5], sums[6], sums[7], sums[8], sums[9], sums[10])
```

```python
import jax
import jax.numpy as jnp
from jax import lax
from jax.sharding import PartitionSpec as P

EPS = 1e-05
THETA = 1000000.0
MASKED = -1e30


def passed_along(shard, axis, by):
    count = lax.axis_size(axis)
    pairs = [(i, i + by) for i in range(count) if 0 <= i + by < count]
    return lax.ppermute(shard, axis, pairs)


def from_behind(value, axis, steps):
    count = lax.axis_size(axis)
    pairs = [(source, (source + steps) % count) for source in range(count)]
    return lax.ppermute(value, axis, pairs)


def root_norm(values, gain):
    return values * lax.rsqrt(jnp.mean(values * values, axis=-1, keepdims=True) + EPS) * gain


def rotate(values, cosine, sine):
    half = values.shape[-1] // 2
    first_half = values[..., :half]
    second_half = values[..., half:]
    return jnp.concatenate(
        [first_half * cosine - second_half * sine, second_half * cosine + first_half * sine],
        axis=-1,
    )


def angles(positions, width):
    freqs = THETA ** (-(jnp.arange(width // 2, dtype=jnp.float32) * 2.0 / width))
    turned = positions.astype(jnp.float32)[:, None] * freqs[None, :]
    return (jnp.cos(turned), jnp.sin(turned))


def query_form(flat, gain, cosine, sine, groups):
    seq_count, row_count, width = flat.shape
    head_dim = gain.shape[0]
    normed = root_norm(flat.reshape(seq_count, row_count, width // head_dim, head_dim), gain)
    turned = rotate(normed, cosine, sine)
    return turned.reshape(seq_count, row_count, -1, groups, head_dim).transpose(0, 2, 3, 1, 4)


def key_form(flat, gain, cosine, sine):
    seq_count, row_count, width = flat.shape
    head_dim = gain.shape[0]
    normed = root_norm(flat.reshape(seq_count, row_count, width // head_dim, head_dim), gain)
    return rotate(normed, cosine, sine)


def ring_form(
    tokens,
    lengths,
    attn_gain,
    q_gain,
    k_gain,
    w_query,
    w_key,
    w_value,
    w_out,
    ffn_gain,
    w_gate,
    w_up,
    w_down,
    cotangent,
):
    seq_count, row_count, width = tokens.shape
    head_dim = q_gain.shape[0]
    heads = w_query.shape[1] // head_dim
    kv_heads = w_key.shape[1] // head_dim
    groups = heads // kv_heads
    loop_size = lax.axis_size("ctx")
    my_place = lax.axis_index("ctx")
    query_start = my_place * row_count
    query_pos = query_start + jnp.arange(row_count, dtype=jnp.int32)
    longest = jnp.max(lengths)
    cosine, sine = angles(query_pos, head_dim)
    cosine = cosine[None, :, None, :]
    sine = sine[None, :, None, :]
    inputs = tokens.astype(jnp.float32)
    acts = root_norm(inputs, attn_gain).astype(jnp.bfloat16).reshape(-1, width)
    qproj = jnp.dot(acts, w_query, preferred_element_type=jnp.float32).reshape(
        seq_count, row_count, -1
    )
    kproj = jnp.dot(acts, w_key, preferred_element_type=jnp.float32).reshape(
        seq_count, row_count, -1
    )
    vproj = jnp.dot(acts, w_value, preferred_element_type=jnp.float32)
    queries = query_form(qproj, q_gain, cosine, sine, groups).astype(jnp.bfloat16)
    keys = key_form(kproj, k_gain, cosine, sine).astype(jnp.bfloat16)
    values = vproj.astype(jnp.bfloat16).reshape(seq_count, row_count, kv_heads, head_dim)
    key_values = jnp.stack([keys, values])

    def block_mask(key_start, count):
        key_pos = key_start + jnp.arange(count, dtype=jnp.int32)
        causal = key_pos[None, None, :] <= query_pos[None, :, None]
        inside = key_pos[None, None, :] < lengths[:, None, None]
        return (causal & inside)[:, None, None, :, :]

    def needed(key_start):
        return (key_start < query_start + row_count) & (key_start < longest)

    def scores_of(key_piece):
        return 0.125 * jnp.einsum(
            "scgtd,sucd->scgtu", queries, key_piece, preferred_element_type=jnp.float32
        )

    def absorb(state, pair, key_start):

        def absorb_work(current):
            top_row, row_total, summed = current
            counted = block_mask(key_start, pair.shape[2])
            masked = jnp.where(counted, scores_of(pair[0]), MASKED)
            top_new = jnp.maximum(top_row, jnp.max(masked, axis=-1))
            weights = jnp.where(counted, jnp.exp(masked - top_new[..., None]), 0.0)
            factor = jnp.exp(top_row - top_new)
            row_total = row_total * factor + jnp.sum(weights, axis=-1)
            summed = summed * factor[..., None] + jnp.einsum(
                "scgtu,sucd->scgtd",
                weights.astype(jnp.bfloat16),
                pair[1],
                preferred_element_type=jnp.float32,
            )
            return (top_new, row_total, summed)

        return lax.cond(needed(key_start), absorb_work, lambda current: current, state)

    stat_shape = (seq_count, kv_heads, groups, row_count)
    start_state = (
        jnp.full(stat_shape, MASKED, jnp.float32),
        jnp.zeros(stat_shape, jnp.float32),
        jnp.zeros(stat_shape + (head_dim,), jnp.float32),
    )
    first_state = absorb(start_state, key_values, query_start)

    def forward_turn(step, carry):
        held, state = carry
        held = passed_along(held, "ctx", 1)
        source = (my_place - step) % loop_size
        return (held, absorb(state, held, source * row_count))

    _, (top_row, row_total, summed) = lax.fori_loop(
        1, loop_size, forward_turn, (key_values, first_state)
    )
    attended = summed / row_total[..., None]
    attn_low = attended.astype(jnp.bfloat16)
    out_heads = w_out.reshape(kv_heads, groups, head_dim, width)
    attn_branch = jnp.einsum(
        "scgtd,cgde->ste", attn_low, out_heads, preferred_element_type=jnp.float32
    )
    middle = inputs + attn_branch
    inner = root_norm(middle, ffn_gain).astype(jnp.bfloat16).reshape(-1, width)
    gate_proj = jnp.dot(inner, w_gate, preferred_element_type=jnp.float32)
    up_proj = jnp.dot(inner, w_up, preferred_element_type=jnp.float32)
    hidden = (jax.nn.silu(gate_proj) * up_proj).astype(jnp.bfloat16)
    output = middle + jnp.dot(hidden, w_down, preferred_element_type=jnp.float32).reshape(
        seq_count, row_count, width
    )
    result = output.astype(jnp.bfloat16)
    valid = (query_pos[None, :] < lengths[:, None]).astype(jnp.float32)
    grad_out = cotangent.astype(jnp.float32) * valid[..., None]
    grad_low = grad_out.astype(jnp.bfloat16).reshape(-1, width)
    down_turned = jnp.einsum("nd,nf->df", grad_low, hidden, preferred_element_type=jnp.float32)
    grad_hidden = jnp.einsum("nd,fd->nf", grad_low, w_down, preferred_element_type=jnp.float32)
    _, pull_gate = jax.vjp(lambda gate_in, up_in: jax.nn.silu(gate_in) * up_in, gate_proj, up_proj)
    grad_gate, grad_up = pull_gate(grad_hidden)
    gate_low = grad_gate.astype(jnp.bfloat16)
    up_low = grad_up.astype(jnp.bfloat16)
    gate_local = jnp.einsum("nd,nf->df", inner, gate_low, preferred_element_type=jnp.float32)
    up_local = jnp.einsum("nd,nf->df", inner, up_low, preferred_element_type=jnp.float32)
    grad_inner = jnp.einsum("nf,df->nd", gate_low, w_gate, preferred_element_type=jnp.float32)
    grad_inner = grad_inner + jnp.einsum(
        "nf,df->nd", up_low, w_up, preferred_element_type=jnp.float32
    )
    _, pull_second = jax.vjp(root_norm, middle, ffn_gain)
    grad_middle, ffn_local = pull_second(grad_inner.reshape(seq_count, row_count, width))
    grad_middle = grad_middle + grad_out
    branch_low = grad_middle.astype(jnp.bfloat16)
    out_turned = jnp.einsum(
        "std,scgte->dcge", branch_low, attn_low, preferred_element_type=jnp.float32
    ).reshape(width, -1)
    grad_attended = jnp.einsum(
        "ste,cgde->scgtd", branch_low, out_heads, preferred_element_type=jnp.float32
    ).astype(jnp.bfloat16)
    grad_wide = grad_attended.astype(jnp.float32)
    delta = jnp.sum(grad_wide * attended, axis=-1)
    grad_scaled = grad_wide / row_total[..., None]

    def block_back(pair, key_start):
        counted = block_mask(key_start, pair.shape[2])
        weights = jnp.where(counted, jnp.exp(scores_of(pair[0]) - top_row[..., None]), 0.0)
        probs = weights / row_total[..., None]
        grad_values = jnp.einsum(
            "scgtu,scgtd->sucd",
            weights.astype(jnp.bfloat16),
            grad_scaled,
            preferred_element_type=jnp.float32,
        )
        grad_probs = jnp.einsum(
            "scgtd,sucd->scgtu", grad_attended, pair[1], preferred_element_type=jnp.float32
        )
        grad_scores = (probs * (grad_probs - delta[..., None])).astype(jnp.bfloat16)
        more_queries = 0.125 * jnp.einsum(
            "scgtu,sucd->scgtd", grad_scores, pair[0], preferred_element_type=jnp.float32
        )
        grad_keys = 0.125 * jnp.einsum(
            "scgtu,scgtd->sucd", grad_scores, queries, preferred_element_type=jnp.float32
        )
        return (more_queries, jnp.stack([grad_keys, grad_values]))

    start_queries = jnp.zeros(stat_shape + (head_dim,), jnp.float32)

    def backward_turn(step, carry):
        held, held_grads, grad_queries = carry
        key_start = (my_place - step) % loop_size * row_count

        def backward_work(current):
            query_acc, pair_acc = current
            more_queries, more_pair = block_back(held, key_start)
            return (query_acc + more_queries, pair_acc + more_pair)

        grad_queries, held_grads = lax.cond(
            needed(key_start), backward_work, lambda current: current, (grad_queries, held_grads)
        )
        held = passed_along(held, "ctx", 1)
        held_grads = from_behind(held_grads.astype(jnp.bfloat16), "ctx", 1).astype(held_grads.dtype)
        return (held, held_grads, grad_queries)

    start_grads = jnp.zeros((2, seq_count, row_count, kv_heads, head_dim), jnp.float32)
    _, pair_grads, grad_queries = lax.fori_loop(
        0, loop_size, backward_turn, (key_values, start_grads, start_queries)
    )
    _, pull_query = jax.vjp(
        lambda proj_in, gain_in: query_form(proj_in, gain_in, cosine, sine, groups), qproj, q_gain
    )
    grad_qproj, q_local = pull_query(grad_queries)
    _, pull_key = jax.vjp(
        lambda proj_in, gain_in: key_form(proj_in, gain_in, cosine, sine), kproj, k_gain
    )
    grad_kproj, k_local = pull_key(pair_grads[0])
    query_low = grad_qproj.reshape(-1, heads * head_dim).astype(jnp.bfloat16)
    key_low = grad_kproj.reshape(-1, kv_heads * head_dim).astype(jnp.bfloat16)
    value_low = pair_grads[1].reshape(-1, kv_heads * head_dim).astype(jnp.bfloat16)
    query_local = jnp.einsum("nd,ne->de", acts, query_low, preferred_element_type=jnp.float32)
    key_local = jnp.einsum("nd,ne->de", acts, key_low, preferred_element_type=jnp.float32)
    value_local = jnp.einsum("nd,ne->de", acts, value_low, preferred_element_type=jnp.float32)
    grad_acts = jnp.einsum("ne,de->nd", query_low, w_query, preferred_element_type=jnp.float32)
    grad_acts = grad_acts + jnp.einsum(
        "ne,de->nd", key_low, w_key, preferred_element_type=jnp.float32
    )
    grad_acts = grad_acts + jnp.einsum(
        "ne,de->nd", value_low, w_value, preferred_element_type=jnp.float32
    )
    _, pull_first = jax.vjp(root_norm, inputs, attn_gain)
    grad_inputs, attn_local = pull_first(grad_acts.reshape(seq_count, row_count, width))
    grad_inputs = grad_inputs + grad_middle
    query_sum, key_sum, value_sum, out_sum, gate_sum, up_sum, down_sum = (
        lax.psum_scatter(query_local, ("dp", "ctx"), scatter_dimension=0, tiled=True),
        lax.psum_scatter(key_local, ("dp", "ctx"), scatter_dimension=0, tiled=True),
        lax.psum_scatter(value_local, ("dp", "ctx"), scatter_dimension=0, tiled=True),
        lax.psum_scatter(out_turned, ("dp", "ctx"), scatter_dimension=0, tiled=True),
        lax.psum_scatter(gate_local, ("dp", "ctx"), scatter_dimension=0, tiled=True),
        lax.psum_scatter(up_local, ("dp", "ctx"), scatter_dimension=0, tiled=True),
        lax.psum_scatter(down_turned, ("dp", "ctx"), scatter_dimension=0, tiled=True),
    )
    attn_sum, q_sum, k_sum, ffn_sum = lax.psum(
        (attn_local, q_local, k_local, ffn_local), ("dp", "ctx")
    )
    return (
        result,
        grad_inputs,
        attn_sum,
        q_sum,
        k_sum,
        query_sum,
        key_sum,
        value_sum,
        out_sum.T,
        ffn_sum,
        gate_sum,
        up_sum,
        down_sum.T,
    )


def gathered(shard, axis):
    return lax.all_gather(shard, axis, axis=0, tiled=True)


def bf16_dot(left, right, dims):
    return lax.dot_general(left, right, (dims, ((), ())), preferred_element_type=jnp.float32)


def split_form(
    tokens,
    lengths,
    attn_gain,
    q_gain,
    k_gain,
    w_query,
    w_key,
    w_value,
    w_out,
    ffn_gain,
    w_gate,
    w_up,
    w_down,
    cotangent,
):
    _, row_count, width = tokens.shape
    head_dim = q_gain.shape[0]
    heads = w_query.shape[1] // head_dim
    kv_heads = w_key.shape[1] // head_dim
    groups = heads // kv_heads
    hidden_width = w_gate.shape[1]
    parts = lax.axis_size("ctx")
    sums = lax.axis_size("dp")
    place = lax.axis_index("ctx")
    seq_len = row_count * parts
    length = lengths[0]
    own_pos = place * row_count + jnp.arange(row_count, dtype=jnp.int32)
    all_pos = jnp.arange(seq_len, dtype=jnp.int32)
    cosine, sine = angles(all_pos, head_dim)
    cosine = cosine[:, None, :]
    sine = sine[:, None, :]
    own_cosine = lax.dynamic_slice_in_dim(cosine, place * row_count, row_count, 0)
    own_sine = lax.dynamic_slice_in_dim(sine, place * row_count, row_count, 0)

    def form(flat, gain, cosine_at, sine_at):
        split = flat.reshape(flat.shape[0], -1, head_dim)
        return rotate(root_norm(split, gain), cosine_at, sine_at)

    x_all = gathered(tokens[0], "ctx").astype(jnp.float32)
    cot_all = gathered(cotangent[0], "ctx")
    x_own = tokens[0].astype(jnp.float32)
    acts_all = root_norm(x_all, attn_gain).astype(jnp.bfloat16)
    acts_own = root_norm(x_own, attn_gain).astype(jnp.bfloat16)
    kproj_all = jnp.dot(acts_all, w_key, preferred_element_type=jnp.float32)
    vproj_all = jnp.dot(acts_all, w_value, preferred_element_type=jnp.float32)
    qproj_own = jnp.dot(acts_own, w_query, preferred_element_type=jnp.float32)
    keys = form(kproj_all, k_gain, cosine, sine).astype(jnp.bfloat16)
    values = vproj_all.astype(jnp.bfloat16).reshape(seq_len, kv_heads, head_dim)
    queries = form(qproj_own, q_gain, own_cosine, own_sine).astype(jnp.bfloat16)
    queries = queries.reshape(row_count, kv_heads, groups, head_dim)
    counted = ((all_pos[None, :] <= own_pos[:, None]) & (all_pos[None, :] < length))[None, None]
    scores = 0.125 * jnp.einsum(
        "tcgd,ucd->cgtu", queries, keys, preferred_element_type=jnp.float32
    )
    masked = jnp.where(counted, scores, MASKED)
    top = jnp.max(masked, axis=-1, keepdims=True)
    weights = jnp.where(counted, jnp.exp(masked - top), 0.0)
    total = jnp.sum(weights, axis=-1, keepdims=True)
    attended = (
        jnp.einsum(
            "cgtu,ucd->cgtd", weights.astype(jnp.bfloat16), values, preferred_element_type=jnp.float32
        )
        / total
    )
    attn_low = attended.astype(jnp.bfloat16).transpose(2, 0, 1, 3).reshape(row_count, -1)
    att_all = gathered(attn_low, "ctx")

    middle = x_own + jnp.dot(attn_low, w_out, preferred_element_type=jnp.float32)
    inner = root_norm(middle, ffn_gain).astype(jnp.bfloat16)
    valid_own = (own_pos < length).astype(jnp.float32)[:, None]
    grad_out = cotangent[0].astype(jnp.float32) * valid_own
    grad_low = grad_out.astype(jnp.bfloat16)

    def ffn(inner_at, grad_at, gate_w, up_w, down_w):
        gate = jnp.dot(inner_at, gate_w, preferred_element_type=jnp.float32)
        up = jnp.dot(inner_at, up_w, preferred_element_type=jnp.float32)
        grad_hidden = bf16_dot(grad_at, down_w, ((1,), (1,)))
        sig = jax.nn.sigmoid(gate)
        hidden = (gate * sig * up).astype(jnp.bfloat16)
        grad_gate = (grad_hidden * up * (sig * (1.0 + gate * (1.0 - sig)))).astype(jnp.bfloat16)
        grad_up = (grad_hidden * (gate * sig)).astype(jnp.bfloat16)
        return hidden, grad_gate, grad_up

    hidden, grad_gate, grad_up = ffn(inner, grad_low, w_gate, w_up, w_down)
    output = middle + jnp.dot(hidden, w_down, preferred_element_type=jnp.float32)
    result = output.astype(jnp.bfloat16)
    grad_inner = bf16_dot(grad_gate, w_gate, ((1,), (1,))) + bf16_dot(grad_up, w_up, ((1,), (1,)))
    _, pull_second = jax.vjp(root_norm, middle, ffn_gain)
    grad_middle, ffn_local = pull_second(grad_inner)
    grad_middle = grad_middle + grad_out
    branch_low = grad_middle.astype(jnp.bfloat16)
    grad_att = bf16_dot(branch_low, w_out, ((1,), (1,))).astype(jnp.bfloat16)

    rows_each = width // (sums * parts)
    branch_cols = branch_low.reshape(row_count, sums, parts, rows_each).transpose(2, 0, 1, 3)
    branch_cols = branch_cols.reshape(parts, row_count, sums * rows_each)
    head_cols = grad_att.reshape(row_count, parts, -1).transpose(1, 0, 2)
    sent = jnp.concatenate([head_cols, branch_cols], axis=-1)
    came = lax.all_to_all(sent, "ctx", 0, 0, tiled=True).reshape(seq_len, -1)
    q_width = heads * head_dim // parts
    kv_width = kv_heads * head_dim // parts
    grad_att_h = came[:, :q_width]
    branch_c = came[:, q_width:]

    wq_h = lax.dynamic_slice_in_dim(w_query, place * q_width, q_width, 1)
    qproj_h = jnp.dot(acts_all, wq_h, preferred_element_type=jnp.float32)
    kproj_h = lax.dynamic_slice_in_dim(kproj_all, place * kv_width, kv_width, 1)
    value_h = lax.dynamic_slice_in_dim(vproj_all, place * kv_width, kv_width, 1).astype(jnp.bfloat16)
    value_h = value_h.reshape(seq_len, -1, head_dim)

    def q_form(flat, gain):
        return form(flat, gain, cosine, sine)

    q_h, pull_q = jax.vjp(q_form, qproj_h, q_gain)
    k_h, pull_k = jax.vjp(q_form, kproj_h, k_gain)
    q_h = q_h.astype(jnp.bfloat16).reshape(seq_len, -1, groups, head_dim)
    k_h = k_h.astype(jnp.bfloat16)
    counted_all = ((all_pos[None, :] <= all_pos[:, None]) & (all_pos[None, :] < length))[None, None]
    scores = 0.125 * jnp.einsum("tcgd,ucd->cgtu", q_h, k_h, preferred_element_type=jnp.float32)
    masked = jnp.where(counted_all, scores, MASKED)
    top = jnp.max(masked, axis=-1, keepdims=True)
    weights = jnp.where(counted_all, jnp.exp(masked - top), 0.0)
    total = jnp.sum(weights, axis=-1, keepdims=True)
    attended_h = (
        jnp.einsum(
            "cgtu,ucd->cgtd", weights.astype(jnp.bfloat16), value_h, preferred_element_type=jnp.float32
        )
        / total
    )
    grad_att_h = grad_att_h.reshape(seq_len, -1, groups, head_dim).transpose(1, 2, 0, 3)
    grad_wide = grad_att_h.astype(jnp.float32)
    delta = jnp.sum(grad_wide * attended_h, axis=-1, keepdims=True)
    grad_values = jnp.einsum(
        "cgtu,cgtd->ucd",
        weights.astype(jnp.bfloat16),
        (grad_wide / total).astype(jnp.bfloat16),
        preferred_element_type=jnp.float32,
    )
    grad_probs = jnp.einsum("cgtd,ucd->cgtu", grad_att_h, value_h, preferred_element_type=jnp.float32)
    grad_scores = (weights / total * (grad_probs - delta)).astype(jnp.bfloat16)
    grad_q = 0.125 * jnp.einsum(
        "cgtu,ucd->tcgd", grad_scores, k_h, preferred_element_type=jnp.float32
    )
    grad_k = 0.125 * jnp.einsum(
        "cgtu,tcgd->ucd", grad_scores, q_h, preferred_element_type=jnp.float32
    )
    grad_qproj, q_local = pull_q(grad_q.reshape(seq_len, -1, head_dim))
    grad_kproj, k_local = pull_k(grad_k)
    proj_low = jnp.concatenate(
        [grad_qproj, grad_kproj, grad_values.reshape(seq_len, -1)], axis=-1
    ).astype(jnp.bfloat16)
    proj_local = bf16_dot(acts_all, proj_low, ((0,), (0,)))
    out_local = bf16_dot(branch_c, att_all, ((0,), (0,)))

    back = lax.all_to_all(
        proj_low.reshape(parts, row_count, -1), "ctx", 0, 0, tiled=True
    )
    query_low = back[:, :, :q_width].transpose(1, 0, 2).reshape(row_count, -1)
    key_low = back[:, :, q_width : q_width + kv_width].transpose(1, 0, 2).reshape(row_count, -1)
    value_low = back[:, :, q_width + kv_width :].transpose(1, 0, 2).reshape(row_count, -1)
    grad_acts = (
        bf16_dot(query_low, w_query, ((1,), (1,)))
        + bf16_dot(key_low, w_key, ((1,), (1,)))
        + bf16_dot(value_low, w_value, ((1,), (1,)))
    )
    _, pull_first = jax.vjp(root_norm, x_own, attn_gain)
    grad_inputs, attn_local = pull_first(grad_acts)
    grad_inputs = grad_inputs + grad_middle

    columns = hidden_width // parts
    gate_c = lax.dynamic_slice_in_dim(w_gate, place * columns, columns, 1)
    up_c = lax.dynamic_slice_in_dim(w_up, place * columns, columns, 1)
    down_c = lax.dynamic_slice_in_dim(w_down, place * columns, columns, 0)
    middle_all = x_all + jnp.dot(att_all, w_out, preferred_element_type=jnp.float32)
    inner_all = root_norm(middle_all, ffn_gain).astype(jnp.bfloat16)
    grad_all = jnp.where((all_pos < length)[:, None], cot_all, 0).astype(jnp.bfloat16)
    hidden_c, grad_gate_c, grad_up_c = ffn(inner_all, grad_all, gate_c, up_c, down_c)
    wide = jnp.concatenate(
        [
            bf16_dot(inner_all, grad_gate_c, ((0,), (0,))).astype(jnp.bfloat16),
            bf16_dot(inner_all, grad_up_c, ((0,), (0,))).astype(jnp.bfloat16),
            bf16_dot(grad_all, hidden_c, ((0,), (0,))).astype(jnp.bfloat16),
            proj_local.astype(jnp.bfloat16),
        ],
        axis=-1,
    )

    def halves(array, own_bit, by):
        half = array.shape[0] // 2
        kept = lax.dynamic_slice_in_dim(array, own_bit * half, half, 0)
        given = lax.dynamic_slice_in_dim(array, (1 - own_bit) * half, half, 0)
        pairs = [(i, i ^ by) for i in range(sums)]
        got = lax.ppermute(given, "dp", pairs)
        return (kept.astype(jnp.float32) + got.astype(jnp.float32)).astype(array.dtype)

    row = lax.axis_index("dp")

    def dp_sum(array):
        blocks = array.reshape(2, 2, array.shape[0] // 4, -1).transpose(1, 0, 2, 3)
        blocks = halves(blocks, row % 2, 1)[0]
        return halves(blocks, row // 2, 2)[0]

    wide_sum = dp_sum(wide)
    out_sum = dp_sum(out_local.astype(jnp.bfloat16)).astype(jnp.float32)
    spread = lax.all_to_all(
        wide_sum.reshape(parts, rows_each, -1), "ctx", 0, 0, tiled=True
    ).transpose(1, 0, 2)
    spread = spread.astype(jnp.float32)

    def taken(start, size):
        return spread[:, :, start : start + size].reshape(rows_each, -1)

    gate_sum = taken(0, columns)
    up_sum = taken(columns, columns)
    down_sum = taken(2 * columns, columns)
    query_sum = taken(3 * columns, q_width)
    key_sum = taken(3 * columns + q_width, kv_width)
    value_sum = taken(3 * columns + q_width + kv_width, kv_width)
    attn_sum, q_sum, k_sum, ffn_sum = lax.psum(
        (attn_local, q_local, k_local, ffn_local), ("dp", "ctx")
    )
    return (
        result[None],
        grad_inputs[None],
        attn_sum,
        q_sum,
        k_sum,
        query_sum,
        key_sum,
        value_sum,
        out_sum.T,
        ffn_sum,
        gate_sum,
        up_sum,
        down_sum.T,
    )


def per_device(*arguments):
    tokens, q_gain, w_key, w_gate = arguments[0], arguments[3], arguments[6], arguments[10]
    parts = lax.axis_size("ctx")
    kv_heads = w_key.shape[1] // q_gain.shape[0]
    fits = (
        tokens.shape[0] == 1
        and lax.axis_size("dp") == 4
        and kv_heads % parts == 0
        and w_gate.shape[1] % (64 * parts) == 0
        and tokens.shape[2] % (8 * 4 * parts) == 0
    )
    return (split_form if fits else ring_form)(*arguments)


def solution(mesh):
    placed = (
        P("dp", "ctx", None),
        P("dp"),
        P(),
        P(),
        P(),
        P(),
        P(),
        P(),
        P(),
        P(),
        P(),
        P(),
        P(),
        P("dp", "ctx", None),
    )
    return jax.shard_map(
        per_device,
        mesh=mesh,
        in_specs=placed,
        out_specs=(
            P("dp", "ctx", None),
            P("dp", "ctx", None),
            P(),
            P(),
            P(),
            P(("dp", "ctx"), None),
            P(("dp", "ctx"), None),
            P(("dp", "ctx"), None),
            P(None, ("dp", "ctx")),
            P(),
            P(("dp", "ctx"), None),
            P(("dp", "ctx"), None),
            P(None, ("dp", "ctx")),
        ),
        check_vma=False,
    )
```

```python
import jax
import jax.numpy as jnp
from jax import lax
from jax.experimental import pallas as pl
from jax.experimental.pallas import tpu as pltpu
from jax.sharding import PartitionSpec as P

EPS = 1e-05
THETA = 1000000.0
MASKED = -1e30


def passed_along(shard, axis, by):
    count = lax.axis_size(axis)
    pairs = [(i, i + by) for i in range(count) if 0 <= i + by < count]
    return lax.ppermute(shard, axis, pairs)


def from_behind(value, axis, steps):
    count = lax.axis_size(axis)
    pairs = [(source, (source + steps) % count) for source in range(count)]
    return lax.ppermute(value, axis, pairs)


def root_norm(values, gain):
    return values * lax.rsqrt(jnp.mean(values * values, axis=-1, keepdims=True) + EPS) * gain


def rotate(values, cosine, sine):
    half = values.shape[-1] // 2
    first_half = values[..., :half]
    second_half = values[..., half:]
    return jnp.concatenate(
        [first_half * cosine - second_half * sine, second_half * cosine + first_half * sine],
        axis=-1,
    )


def angles(positions, width):
    freqs = THETA ** (-(jnp.arange(width // 2, dtype=jnp.float32) * 2.0 / width))
    turned = positions.astype(jnp.float32)[:, None] * freqs[None, :]
    return (jnp.cos(turned), jnp.sin(turned))


def query_form(flat, gain, cosine, sine, groups):
    seq_count, row_count, width = flat.shape
    head_dim = gain.shape[0]
    normed = root_norm(flat.reshape(seq_count, row_count, width // head_dim, head_dim), gain)
    turned = rotate(normed, cosine, sine)
    return turned.reshape(seq_count, row_count, -1, groups, head_dim).transpose(0, 2, 3, 1, 4)


def key_form(flat, gain, cosine, sine):
    seq_count, row_count, width = flat.shape
    head_dim = gain.shape[0]
    normed = root_norm(flat.reshape(seq_count, row_count, width // head_dim, head_dim), gain)
    return rotate(normed, cosine, sine)


def ring_form(
    tokens,
    lengths,
    attn_gain,
    q_gain,
    k_gain,
    w_query,
    w_key,
    w_value,
    w_out,
    ffn_gain,
    w_gate,
    w_up,
    w_down,
    cotangent,
):
    seq_count, row_count, width = tokens.shape
    head_dim = q_gain.shape[0]
    heads = w_query.shape[1] // head_dim
    kv_heads = w_key.shape[1] // head_dim
    groups = heads // kv_heads
    loop_size = lax.axis_size("ctx")
    my_place = lax.axis_index("ctx")
    query_start = my_place * row_count
    query_pos = query_start + jnp.arange(row_count, dtype=jnp.int32)
    longest = jnp.max(lengths)
    cosine, sine = angles(query_pos, head_dim)
    cosine = cosine[None, :, None, :]
    sine = sine[None, :, None, :]
    inputs = tokens.astype(jnp.float32)
    acts = root_norm(inputs, attn_gain).astype(jnp.bfloat16).reshape(-1, width)
    qproj = jnp.dot(acts, w_query, preferred_element_type=jnp.float32).reshape(
        seq_count, row_count, -1
    )
    kproj = jnp.dot(acts, w_key, preferred_element_type=jnp.float32).reshape(
        seq_count, row_count, -1
    )
    vproj = jnp.dot(acts, w_value, preferred_element_type=jnp.float32)
    queries = query_form(qproj, q_gain, cosine, sine, groups).astype(jnp.bfloat16)
    keys = key_form(kproj, k_gain, cosine, sine).astype(jnp.bfloat16)
    values = vproj.astype(jnp.bfloat16).reshape(seq_count, row_count, kv_heads, head_dim)
    key_values = jnp.stack([keys, values])

    def block_mask(key_start, count):
        key_pos = key_start + jnp.arange(count, dtype=jnp.int32)
        causal = key_pos[None, None, :] <= query_pos[None, :, None]
        inside = key_pos[None, None, :] < lengths[:, None, None]
        return (causal & inside)[:, None, None, :, :]

    def needed(key_start):
        return (key_start < query_start + row_count) & (key_start < longest)

    def scores_of(key_piece):
        return 0.125 * jnp.einsum(
            "scgtd,sucd->scgtu", queries, key_piece, preferred_element_type=jnp.float32
        )

    def absorb(state, pair, key_start):

        def absorb_work(current):
            top_row, row_total, summed = current
            counted = block_mask(key_start, pair.shape[2])
            masked = jnp.where(counted, scores_of(pair[0]), MASKED)
            top_new = jnp.maximum(top_row, jnp.max(masked, axis=-1))
            weights = jnp.where(counted, jnp.exp(masked - top_new[..., None]), 0.0)
            factor = jnp.exp(top_row - top_new)
            row_total = row_total * factor + jnp.sum(weights, axis=-1)
            summed = summed * factor[..., None] + jnp.einsum(
                "scgtu,sucd->scgtd",
                weights.astype(jnp.bfloat16),
                pair[1],
                preferred_element_type=jnp.float32,
            )
            return (top_new, row_total, summed)

        return lax.cond(needed(key_start), absorb_work, lambda current: current, state)

    stat_shape = (seq_count, kv_heads, groups, row_count)
    start_state = (
        jnp.full(stat_shape, MASKED, jnp.float32),
        jnp.zeros(stat_shape, jnp.float32),
        jnp.zeros(stat_shape + (head_dim,), jnp.float32),
    )
    first_state = absorb(start_state, key_values, query_start)

    def forward_turn(step, carry):
        held, state = carry
        held = passed_along(held, "ctx", 1)
        source = (my_place - step) % loop_size
        return (held, absorb(state, held, source * row_count))

    _, (top_row, row_total, summed) = lax.fori_loop(
        1, loop_size, forward_turn, (key_values, first_state)
    )
    attended = summed / row_total[..., None]
    attn_low = attended.astype(jnp.bfloat16)
    out_heads = w_out.reshape(kv_heads, groups, head_dim, width)
    attn_branch = jnp.einsum(
        "scgtd,cgde->ste", attn_low, out_heads, preferred_element_type=jnp.float32
    )
    middle = inputs + attn_branch
    inner = root_norm(middle, ffn_gain).astype(jnp.bfloat16).reshape(-1, width)
    gate_proj = jnp.dot(inner, w_gate, preferred_element_type=jnp.float32)
    up_proj = jnp.dot(inner, w_up, preferred_element_type=jnp.float32)
    hidden = (jax.nn.silu(gate_proj) * up_proj).astype(jnp.bfloat16)
    output = middle + jnp.dot(hidden, w_down, preferred_element_type=jnp.float32).reshape(
        seq_count, row_count, width
    )
    result = output.astype(jnp.bfloat16)
    valid = (query_pos[None, :] < lengths[:, None]).astype(jnp.float32)
    grad_out = cotangent.astype(jnp.float32) * valid[..., None]
    grad_low = grad_out.astype(jnp.bfloat16).reshape(-1, width)
    down_turned = jnp.einsum("nd,nf->df", grad_low, hidden, preferred_element_type=jnp.float32)
    grad_hidden = jnp.einsum("nd,fd->nf", grad_low, w_down, preferred_element_type=jnp.float32)
    _, pull_gate = jax.vjp(lambda gate_in, up_in: jax.nn.silu(gate_in) * up_in, gate_proj, up_proj)
    grad_gate, grad_up = pull_gate(grad_hidden)
    gate_low = grad_gate.astype(jnp.bfloat16)
    up_low = grad_up.astype(jnp.bfloat16)
    gate_local = jnp.einsum("nd,nf->df", inner, gate_low, preferred_element_type=jnp.float32)
    up_local = jnp.einsum("nd,nf->df", inner, up_low, preferred_element_type=jnp.float32)
    grad_inner = jnp.einsum("nf,df->nd", gate_low, w_gate, preferred_element_type=jnp.float32)
    grad_inner = grad_inner + jnp.einsum(
        "nf,df->nd", up_low, w_up, preferred_element_type=jnp.float32
    )
    _, pull_second = jax.vjp(root_norm, middle, ffn_gain)
    grad_middle, ffn_local = pull_second(grad_inner.reshape(seq_count, row_count, width))
    grad_middle = grad_middle + grad_out
    branch_low = grad_middle.astype(jnp.bfloat16)
    out_turned = jnp.einsum(
        "std,scgte->dcge", branch_low, attn_low, preferred_element_type=jnp.float32
    ).reshape(width, -1)
    grad_attended = jnp.einsum(
        "ste,cgde->scgtd", branch_low, out_heads, preferred_element_type=jnp.float32
    ).astype(jnp.bfloat16)
    grad_wide = grad_attended.astype(jnp.float32)
    delta = jnp.sum(grad_wide * attended, axis=-1)
    grad_scaled = grad_wide / row_total[..., None]

    def block_back(pair, key_start):
        counted = block_mask(key_start, pair.shape[2])
        weights = jnp.where(counted, jnp.exp(scores_of(pair[0]) - top_row[..., None]), 0.0)
        probs = weights / row_total[..., None]
        grad_values = jnp.einsum(
            "scgtu,scgtd->sucd",
            weights.astype(jnp.bfloat16),
            grad_scaled,
            preferred_element_type=jnp.float32,
        )
        grad_probs = jnp.einsum(
            "scgtd,sucd->scgtu", grad_attended, pair[1], preferred_element_type=jnp.float32
        )
        grad_scores = (probs * (grad_probs - delta[..., None])).astype(jnp.bfloat16)
        more_queries = 0.125 * jnp.einsum(
            "scgtu,sucd->scgtd", grad_scores, pair[0], preferred_element_type=jnp.float32
        )
        grad_keys = 0.125 * jnp.einsum(
            "scgtu,scgtd->sucd", grad_scores, queries, preferred_element_type=jnp.float32
        )
        return (more_queries, jnp.stack([grad_keys, grad_values]))

    start_queries = jnp.zeros(stat_shape + (head_dim,), jnp.float32)

    def backward_turn(step, carry):
        held, held_grads, grad_queries = carry
        key_start = (my_place - step) % loop_size * row_count

        def backward_work(current):
            query_acc, pair_acc = current
            more_queries, more_pair = block_back(held, key_start)
            return (query_acc + more_queries, pair_acc + more_pair)

        grad_queries, held_grads = lax.cond(
            needed(key_start), backward_work, lambda current: current, (grad_queries, held_grads)
        )
        held = passed_along(held, "ctx", 1)
        held_grads = from_behind(held_grads.astype(jnp.bfloat16), "ctx", 1).astype(held_grads.dtype)
        return (held, held_grads, grad_queries)

    start_grads = jnp.zeros((2, seq_count, row_count, kv_heads, head_dim), jnp.float32)
    _, pair_grads, grad_queries = lax.fori_loop(
        0, loop_size, backward_turn, (key_values, start_grads, start_queries)
    )
    _, pull_query = jax.vjp(
        lambda proj_in, gain_in: query_form(proj_in, gain_in, cosine, sine, groups), qproj, q_gain
    )
    grad_qproj, q_local = pull_query(grad_queries)
    _, pull_key = jax.vjp(
        lambda proj_in, gain_in: key_form(proj_in, gain_in, cosine, sine), kproj, k_gain
    )
    grad_kproj, k_local = pull_key(pair_grads[0])
    query_low = grad_qproj.reshape(-1, heads * head_dim).astype(jnp.bfloat16)
    key_low = grad_kproj.reshape(-1, kv_heads * head_dim).astype(jnp.bfloat16)
    value_low = pair_grads[1].reshape(-1, kv_heads * head_dim).astype(jnp.bfloat16)
    query_local = jnp.einsum("nd,ne->de", acts, query_low, preferred_element_type=jnp.float32)
    key_local = jnp.einsum("nd,ne->de", acts, key_low, preferred_element_type=jnp.float32)
    value_local = jnp.einsum("nd,ne->de", acts, value_low, preferred_element_type=jnp.float32)
    grad_acts = jnp.einsum("ne,de->nd", query_low, w_query, preferred_element_type=jnp.float32)
    grad_acts = grad_acts + jnp.einsum(
        "ne,de->nd", key_low, w_key, preferred_element_type=jnp.float32
    )
    grad_acts = grad_acts + jnp.einsum(
        "ne,de->nd", value_low, w_value, preferred_element_type=jnp.float32
    )
    _, pull_first = jax.vjp(root_norm, inputs, attn_gain)
    grad_inputs, attn_local = pull_first(grad_acts.reshape(seq_count, row_count, width))
    grad_inputs = grad_inputs + grad_middle
    query_sum, key_sum, value_sum, out_sum, gate_sum, up_sum, down_sum = (
        lax.psum_scatter(query_local, ("dp", "ctx"), scatter_dimension=0, tiled=True),
        lax.psum_scatter(key_local, ("dp", "ctx"), scatter_dimension=0, tiled=True),
        lax.psum_scatter(value_local, ("dp", "ctx"), scatter_dimension=0, tiled=True),
        lax.psum_scatter(out_turned, ("dp", "ctx"), scatter_dimension=0, tiled=True),
        lax.psum_scatter(gate_local, ("dp", "ctx"), scatter_dimension=0, tiled=True),
        lax.psum_scatter(up_local, ("dp", "ctx"), scatter_dimension=0, tiled=True),
        lax.psum_scatter(down_turned, ("dp", "ctx"), scatter_dimension=0, tiled=True),
    )
    attn_sum, q_sum, k_sum, ffn_sum = lax.psum(
        (attn_local, q_local, k_local, ffn_local), ("dp", "ctx")
    )
    return (
        result,
        grad_inputs,
        attn_sum,
        q_sum,
        k_sum,
        query_sum,
        key_sum,
        value_sum,
        out_sum.T,
        ffn_sum,
        gate_sum,
        up_sum,
        down_sum.T,
    )


LANES = 128
VMEM_LIMIT = 60 << 20
NN = ((1,), (0,))
NT = ((1,), (1,))
TN = ((0,), (0,))


def bf16_dot(left, right, dims):
    return lax.dot_general(left, right, (dims, ((), ())), preferred_element_type=jnp.float32)


def inverse_root(values):
    return lax.rsqrt(jnp.mean(values * values, axis=-1, keepdims=True) + EPS)


def lane_of(shape):
    return lax.broadcasted_iota(jnp.int32, shape, len(shape) - 1)


def head_mean(values, head_dim):
    rows = lax.broadcasted_iota(jnp.int32, (LANES, LANES), 0) // head_dim
    columns = lane_of((LANES, LANES)) // head_dim
    spread = jnp.where(rows == columns, 1.0 / head_dim, 0.0).astype(jnp.bfloat16)
    high = values.astype(jnp.bfloat16)
    low = (values - high.astype(jnp.float32)).astype(jnp.bfloat16)
    return bf16_dot(high, spread, NN) + bf16_dot(low, spread, NN)


def partner(values, head_dim):
    half = head_dim // 2
    first = lane_of(values.shape) % head_dim < half
    return jnp.where(
        first, pltpu.roll(values, LANES - half, axis=1), pltpu.roll(values, half, axis=1)
    )


def head_turn(flat, gain, cosine, sine, head_dim):
    normed = flat * lax.rsqrt(head_mean(flat * flat, head_dim) + EPS) * gain
    return normed * cosine + partner(normed, head_dim) * sine


def head_turn_back(grad, flat, gain, cosine, sine, head_dim):
    back = grad * cosine + partner(grad * sine, head_dim)
    root = lax.rsqrt(head_mean(flat * flat, head_dim) + EPS)
    scaled = gain * back
    mean = head_mean(scaled * flat, head_dim)
    return (
        root * scaled - flat * (root * root * root * mean),
        jnp.sum(back * flat * root, axis=0, keepdims=True),
    )


def turns(freq, start, rows):
    pos = (start + lax.broadcasted_iota(jnp.int32, (rows, 1), 0)).astype(jnp.float32)
    angle = pos * freq[0:1, :]
    return jnp.cos(angle), jnp.sin(angle) * freq[1:2, :]


def whole_spec(shape):
    return pl.BlockSpec(shape, lambda *_: (0,) * len(shape))


def cost_of(inputs, outs, flops):
    moved = sum(item.size * item.dtype.itemsize for item in (*inputs, *outs))
    return pl.CostEstimate(flops=flops, bytes_accessed=moved, transcendentals=0)


class Arriving:
    def __init__(self, source, ref, signal):
        self.copy, self.ref, self.shape = pltpu.make_async_copy(source, ref, signal), ref, ref.shape
        self.copy.start()

    def ready(self):
        if self.copy is not None:
            self.copy.wait()
            self.copy = None
        return self.ref

    def __getitem__(self, at):
        return self.ready()[at]


class Leaving:
    def __init__(self, ref, target, signal):
        self.ref, self.target, self.signal, self.shape = ref, target, signal, ref.shape
        self.copy = None

    def __setitem__(self, at, value):
        self.ref[at] = value

    def __getitem__(self, at):
        return self.ref[at]

    def leave(self):
        if self.copy is None:
            self.copy = pltpu.make_async_copy(self.ref, self.target, self.signal)
            self.copy.start()


class Rows:
    def __init__(self, array, scalar, rows=0):
        self.array, self.scalar, self.rows = array, scalar, rows
        self.shape = (rows,) + array.shape[1:] if rows else array.shape[1:]
        self.dtype, self.size = array.dtype, array.size

    def of(self, ref, scalars):
        at = scalars[self.scalar]
        if not self.rows:
            return ref.at[at]
        return ref.at[pl.ds(pl.multiple_of(at * self.rows, self.rows), self.rows)]


def kernel_call(body, scalars, inputs, outs, scratch, flops, name, held=(), stacks=()):
    count, kept = len(inputs), len(held)

    def run(scalars_ref, *refs):
        given, refs = refs[:count], refs[count + kept :]
        targets, refs = refs[: len(outs)], refs[len(outs) :]
        stack_refs, refs = refs[: len(stacks)], refs[len(stacks) :]
        buffers, refs = refs[:count], refs[count:]
        results, refs = refs[: len(outs)], refs[len(outs) :]
        signals, own = refs[0], refs[1:]
        arriving = []
        for at, item in enumerate(inputs):
            source = item.of(given[at], scalars_ref) if isinstance(item, Rows) else given[at]
            arriving.append(Arriving(source, buffers[at], signals.at[at]))
        leaving = [
            Leaving(result, target, signals.at[count + at])
            for at, (result, target) in enumerate(zip(results, targets))
        ]
        body(scalars_ref, *arriving, *leaving, *stack_refs, *own)
        for item in arriving:
            item.ready()
        for item in leaving:
            item.leave()
        for item in leaving:
            item.copy.wait()

    near = pl.BlockSpec(memory_space=pl.ANY)
    far = pl.BlockSpec(memory_space=pltpu.HBM)
    arrays = [item.array if isinstance(item, Rows) else item for item in inputs]
    return pl.pallas_call(
        run,
        in_specs=[pl.BlockSpec(memory_space=pltpu.SMEM)] + [near] * count + [far] * kept,
        out_specs=[far] * (len(outs) + len(stacks)),
        out_shape=[*outs, *stacks],
        scratch_shapes=[pltpu.VMEM(item.shape, item.dtype) for item in (*inputs, *outs)]
        + [pltpu.SemaphoreType.DMA((count + len(outs),))]
        + list(scratch),
        input_output_aliases={1 + count + at: len(outs) + at for at in range(kept)},
        cost_estimate=cost_of(inputs, (*outs, *stacks), flops),
        compiler_params=pltpu.CompilerParams(vmem_limit_bytes=VMEM_LIMIT),
        name=name,
    )(scalars, *arrays, *held)


def shape_of(shape, dtype):
    return jax.ShapeDtypeStruct(shape, dtype)


def stacked(values):
    return jnp.concatenate(
        [values[:, at : at + LANES] for at in range(0, values.shape[1], LANES)], axis=0
    )


def key_value_rows(scalars, shard_refs, wk_ref, wv_ref, gain_ref, k_gain_ref, freq, acts, kv, head_dim):
    count, rows = len(shard_refs), shard_refs[0].shape[0]
    for at, ref in enumerate(shard_refs):
        values = ref[...].astype(jnp.float32)
        acts[at] = (values * inverse_root(values) * gain_ref[...]).astype(jnp.bfloat16)
    tables = [turns(freq, scalars[at] * rows, rows) for at in range(count)]
    cosine, sine = (jnp.concatenate(table, axis=0) for table in zip(*tables))
    flat = acts[...].reshape(count * rows, -1)
    left = lane_of((count * rows, LANES)) < head_dim
    keys = bf16_dot(flat, wk_ref[...], NN)
    values = bf16_dot(flat, wv_ref[...], NN)
    for chunk in range(wk_ref.shape[1] // LANES):
        at = slice(chunk * LANES, (chunk + 1) * LANES)
        turned = head_turn(keys[:, at], k_gain_ref[...], cosine, sine, head_dim)
        value = values[:, at]
        for odd in range(2):
            pair = jnp.where(
                left,
                pltpu.roll(turned, head_dim, axis=1) if odd else turned,
                value if odd else pltpu.roll(value, head_dim, axis=1),
            )
            start = (2 * chunk + odd) * LANES
            kv[:, :, start : start + LANES] = pair.astype(jnp.bfloat16).reshape(count, rows, LANES)


def key_value_body(count, head_dim, scalars, *refs):
    acts_out, kv_out, acts, kv, signals = refs[count + 5 :]
    key_value_rows(scalars, refs[:count], *refs[count : count + 4], refs[count + 4][...], acts, kv, head_dim)
    leaving = [
        pltpu.make_async_copy(buffer.at[at], out.at[scalars[at]], signals.at[2 * at + turn])
        for at in range(count)
        for turn, (buffer, out) in enumerate(((acts, acts_out), (kv, kv_out)))
    ]
    for copy in leaving:
        copy.start()
    for copy in leaving:
        copy.wait()


def key_value_part(scalars, shards, w_key, w_value, attn_gain, k_gain, freq, parts, head_dim):
    rows, width = shards[0].shape
    kv_width = 2 * w_key.shape[1]
    count = len(shards)
    return kernel_call(
        lambda *refs: key_value_body(count, head_dim, *refs),
        scalars,
        [*shards, w_key, w_value, attn_gain, k_gain, freq],
        [],
        [
            pltpu.VMEM((count, rows, width), jnp.bfloat16),
            pltpu.VMEM((count, rows, kv_width), jnp.bfloat16),
            pltpu.SemaphoreType.DMA((2 * count,)),
        ],
        2 * count * rows * width * kv_width,
        "key_value_part",
        (),
        [
            shape_of((parts, rows, width), jnp.bfloat16),
            shape_of((parts, rows, kv_width), jnp.bfloat16),
        ],
    )


def attend_body(known, fresh, head_dim, scalars, *refs):
    shard_refs, refs = refs[:fresh], refs[fresh:]
    wk_ref, wv_ref, gain_ref, k_gain_ref, freq_ref, x_ref, wq_ref, q_gain_ref = refs[:8]
    kv_refs, refs = refs[8 : 8 + known], refs[8 + known :]
    out_ref, acts_out, acts, kv, bias, turned, signals = refs
    place, length = scalars[known + fresh], scalars[known + fresh + 1]
    rows = x_ref.shape[0]
    count = (known + fresh) * rows
    chunks = wq_ref.shape[1] // LANES
    freq = freq_ref[...]
    key_value_rows(
        [scalars[known + at] for at in range(fresh)],
        shard_refs,
        wk_ref,
        wv_ref,
        gain_ref,
        k_gain_ref,
        freq,
        acts,
        kv.at[pl.ds(known, fresh)],
        head_dim,
    )
    leaving = [
        pltpu.make_async_copy(acts.at[at], acts_out.at[scalars[known + at]], signals.at[at])
        for at in range(fresh)
    ]
    for copy in leaving:
        copy.start()
    values = x_ref[...].astype(jnp.float32)
    own = (values * inverse_root(values) * gain_ref[...]).astype(jnp.bfloat16)
    tables = turns(freq, place * rows, rows)
    cosine, sine = (jnp.concatenate([table] * chunks, axis=0) for table in tables)
    flat = stacked(bf16_dot(own, wq_ref[...], NN))
    turned[...] = (0.125 * head_turn(flat, q_gain_ref[...], cosine, sine, head_dim)).reshape(
        chunks, rows, LANES
    )
    query_pos = place * rows + lane_of((rows, 2 * rows)) % rows
    for slot in range(known + fresh):
        key_pos = scalars[slot] * rows + lax.broadcasted_iota(jnp.int32, (rows, 2 * rows), 0)
        bias[slot * rows : (slot + 1) * rows, :] = jnp.where(
            (key_pos <= query_pos) & (key_pos < length), 0.0, MASKED
        )
        if slot < known:
            kv[slot] = kv_refs[slot][...]
    left = lane_of((rows, LANES)) < head_dim

    def one_head(index, carry):
        at = pl.ds(pl.multiple_of(index * LANES, LANES), LANES)
        mine = turned[index]
        both = jnp.concatenate(
            [jnp.where(left, mine, 0.0), jnp.where(left, pltpu.roll(mine, head_dim, axis=1), 0.0)],
            axis=0,
        ).astype(jnp.bfloat16)
        head_kv = kv[:, :, at].reshape(count, LANES)
        scores = bf16_dot(head_kv, both, NT) + bias[...]
        top = jnp.max(scores, axis=0, keepdims=True)
        weights = jnp.exp(scores - top)
        total = jnp.sum(weights, axis=0, keepdims=True)
        summed = bf16_dot(head_kv, weights.astype(jnp.bfloat16), TN)[head_dim:] / total
        heads = jnp.concatenate([summed[:, :rows], summed[:, rows:]], axis=0)
        out_ref[:, at] = heads.T.astype(jnp.bfloat16)
        return carry

    lax.fori_loop(0, chunks, one_head, 0, unroll=2)
    for copy in leaving:
        copy.wait()


def attend(scalars, shards, x_own, early, w_key, w_value, w_query, attn_gain, q_gain, k_gain, freq, head_dim):
    parts, rows, width = early[0].shape
    q_width, kv_width = w_query.shape[1], 2 * w_key.shape[1]
    fresh = len(shards)
    known = parts - fresh
    blocks = [Rows(early[1], at) for at in range(known)]
    return kernel_call(
        lambda *refs: attend_body(known, fresh, head_dim, *refs),
        scalars,
        [*shards, w_key, w_value, attn_gain, k_gain, freq, x_own, w_query, q_gain, *blocks],
        [shape_of((rows, q_width), jnp.bfloat16)],
        [
            pltpu.VMEM((fresh, rows, width), jnp.bfloat16),
            pltpu.VMEM((parts, rows, kv_width), jnp.bfloat16),
            pltpu.VMEM((parts * rows, 2 * rows), jnp.float32),
            pltpu.VMEM((q_width // LANES, rows, LANES), jnp.float32),
            pltpu.SemaphoreType.DMA((fresh,)),
        ],
        2 * rows * width * (q_width + fresh * kv_width) + 4 * rows * parts * rows * q_width,
        "attend",
        [early[0]],
        [shape_of((parts, rows, width), jnp.bfloat16)],
    )


def ffn_terms(gate, up, grad_hidden):
    sig = 1.0 / (1.0 + jnp.exp(-gate))
    swish = gate * sig
    hidden = (swish * up).astype(jnp.bfloat16)
    grad_gate = (grad_hidden * up * (sig * (1.0 + gate * (1.0 - sig)))).astype(jnp.bfloat16)
    grad_up = (grad_hidden * swish).astype(jnp.bfloat16)
    return hidden, grad_gate, grad_up


def valid_rows(ref, start, length):
    pos = start + lax.broadcasted_iota(jnp.int32, (ref.shape[0], 1), 0)
    return jnp.where(pos < length, ref[...].astype(jnp.float32), 0.0).astype(jnp.bfloat16)


def ffn_body(
    sums,
    first,
    last,
    scalars,
    x_ref,
    att_ref,
    cot_ref,
    w_out_ref,
    gain_ref,
    gate_ref,
    up_ref,
    down_ref,
    *refs,
):
    if not first:
        before, refs = refs[:2], refs[2:]
    outs, (mid, inner, grad_low, out_acc, inner_acc) = refs[:-5], refs[-5:]
    step = pl.program_id(0)
    gain = gain_ref[...]
    rows = x_ref.shape[0]

    @pl.when(step == 0)
    def _():
        middle = x_ref[...].astype(jnp.float32) + bf16_dot(att_ref[...], w_out_ref[...], NN)
        mid[...] = middle
        inner[...] = (middle * inverse_root(middle) * gain).astype(jnp.bfloat16)
        grad_low[...] = valid_rows(cot_ref, scalars[0] * rows, scalars[1])
        out_acc[...] = middle if first else before[0][...]
        inner_acc[...] = jnp.zeros_like(inner_acc) if first else before[1][...]

    gate_w, up_w, down_w = gate_ref[...], up_ref[...], down_ref[...]
    hidden, grad_gate, grad_up = ffn_terms(
        bf16_dot(inner[...], gate_w, NN),
        bf16_dot(inner[...], up_w, NN),
        bf16_dot(grad_low[...], down_w, NT),
    )
    out_acc[...] += bf16_dot(hidden, down_w, NN)
    inner_acc[...] += bf16_dot(grad_gate, gate_w, NT) + bf16_dot(grad_up, up_w, NT)

    @pl.when(step == pl.num_programs(0) - 1)
    def _():
        if not last:
            outs[0][...] = out_acc[...]
            outs[1][...] = inner_acc[...]
            return
        result_ref, grad_mid_ref, sent_ref, gain_grad_ref = outs
        result_ref[...] = out_acc[...].astype(jnp.bfloat16)
        middle = mid[...]
        grad_inner = inner_acc[...]
        root = inverse_root(middle)
        scaled = grad_inner * gain
        mean = jnp.mean(scaled * middle, axis=-1, keepdims=True)
        grad_mid = (
            grad_low[...].astype(jnp.float32) + root * scaled - middle * (root * root * root * mean)
        )
        grad_mid_ref[...] = grad_mid
        gain_grad_ref[...] = jnp.sum(grad_inner * middle * root, axis=0, keepdims=True)
        branch = grad_mid.astype(jnp.bfloat16)
        grad_att = bf16_dot(branch, w_out_ref[...], NT)
        parts = sent_ref.shape[0]
        each = grad_mid.shape[1] // (parts * sums)
        lane = lane_of((rows, LANES))
        for part in range(parts):
            head_at = slice(part * LANES, (part + 1) * LANES)
            sent_ref[part, :, :LANES] = grad_att[:, head_at].astype(jnp.bfloat16)
            picked = jnp.zeros((rows, LANES), jnp.float32)
            for block in range(sums):
                start = (block * parts + part) * each
                chunk = grad_mid[:, start // LANES * LANES : start // LANES * LANES + LANES]
                turn = (block * each - start % LANES) % LANES
                moved = pltpu.roll(chunk, turn, axis=1) if turn else chunk
                picked = jnp.where(lane // each == block, moved, picked)
            sent_ref[part, :, LANES:] = picked.astype(jnp.bfloat16)


def ffn_part(scalars, own, weights, blocks, chunk, before, last, parts, sums):
    rows, width = own[0].shape
    low, high = blocks
    w_gate, w_up, w_down = weights
    inputs = [*own, *weights, *before]
    specs = [whole_spec(item.shape) for item in own] + [
        pl.BlockSpec((width, chunk), lambda i, s: (0, i + low)),
        pl.BlockSpec((width, chunk), lambda i, s: (0, i + low)),
        pl.BlockSpec((chunk, width), lambda i, s: (i + low, 0)),
    ]
    specs += [whole_spec(item.shape) for item in before]
    outs = [shape_of((rows, width), jnp.float32)] * 2
    if last:
        outs = [
            shape_of((rows, width), jnp.bfloat16),
            shape_of((rows, width), jnp.float32),
            shape_of((parts, rows, 2 * LANES), jnp.bfloat16),
            shape_of((1, width), jnp.float32),
        ]
    return pl.pallas_call(
        lambda *refs: ffn_body(sums, not before, last, *refs),
        grid_spec=pltpu.PrefetchScalarGridSpec(
            num_scalar_prefetch=1,
            grid=(high - low,),
            in_specs=specs,
            out_specs=[whole_spec(item.shape) for item in outs],
            scratch_shapes=[
                pltpu.VMEM((rows, width), jnp.float32),
                pltpu.VMEM((rows, width), jnp.bfloat16),
                pltpu.VMEM((rows, width), jnp.bfloat16),
                pltpu.VMEM((rows, width), jnp.float32),
                pltpu.VMEM((rows, width), jnp.float32),
            ],
        ),
        out_shape=outs,
        cost_estimate=pl.CostEstimate(
            flops=12 * rows * width * chunk * (high - low),
            bytes_accessed=6 * width * chunk * (high - low),
            transcendentals=0,
        ),
        compiler_params=pltpu.CompilerParams(vmem_limit_bytes=VMEM_LIMIT),
        name="ffn_part",
    )(scalars, *inputs)


def factor_rows(slots, columns, scalars, x_refs, att_refs, cot_refs, w_out_ref, gain_ref, gate_up_ref, down_ref):
    rows = x_refs[0].shape[0]

    def all_rows(refs):
        return jnp.concatenate([ref[...] for ref in refs], axis=0)

    middle = all_rows(x_refs).astype(jnp.float32) + bf16_dot(all_rows(att_refs), w_out_ref[...], NN)
    inner = (middle * inverse_root(middle) * gain_ref[...]).astype(jnp.bfloat16)
    grad_low = jnp.concatenate(
        [
            valid_rows(ref, scalars[slot] * rows, scalars[-1 + slots[2]])
            for ref, slot in zip(cot_refs, range(slots[0], slots[1]))
        ],
        axis=0,
    )
    both = bf16_dot(inner, gate_up_ref[...], NN)
    grad_hidden = bf16_dot(grad_low, down_ref[...], NT)
    hidden, grad_gate, grad_up = ffn_terms(both[:, :columns], both[:, columns:], grad_hidden)
    return inner, grad_low, grad_gate, grad_up, hidden


def factor_body(slots, columns, scalars, *refs):
    count = slots[1] - slots[0]
    x_refs, att_refs, cot_refs = refs[:count], refs[count : 2 * count], refs[2 * count : 3 * count]
    weights, outs = refs[3 * count : 3 * count + 4], refs[3 * count + 4 :]
    found = factor_rows(slots, columns, scalars, x_refs, att_refs, cot_refs, *weights)
    for out, value in zip(outs, found):
        out[...] = value
        out.leave()


def factor_part(scalars, x_shards, att_shards, cot_shards, weights, slots):
    rows, width = x_shards[0].shape
    columns = weights[-1].shape[0]
    low, high = slots
    count = high - low
    outs = [shape_of((count * rows, width), jnp.bfloat16)] * 2
    outs += [shape_of((count * rows, columns), jnp.bfloat16)] * 3
    return kernel_call(
        lambda *refs: factor_body((low, high, scalars.shape[0]), columns, *refs),
        scalars,
        [
            *x_shards[low:high],
            *att_shards[low:high],
            *cot_shards[low:high],
            *weights,
        ],
        outs,
        [],
        2 * count * rows * width * (width + 3 * columns),
        "factor_part",
    )


def cut_rows(kept_ref, given_ref, values, start, core):
    size = values.shape[0] // 4
    columns = slice(start, start + values.shape[1])
    for block in range(4):
        piece = values[block * size : (block + 1) * size]
        rows = slice(block // 2 * size, (block // 2 + 1) * size)

        @pl.when(core == block % 2)
        def _(piece=piece, rows=rows):
            kept_ref[rows, columns] = piece

        @pl.when(core != block % 2)
        def _(piece=piece, rows=rows):
            given_ref[rows, columns] = piece


def turned_product(rights, lefts, columns):
    total = None
    for right, left in zip(rights, lefts):
        term = bf16_dot(right, left, TN)
        total = term if total is None else total + term
    return total.T[:, :columns].astype(jnp.bfloat16)


def last_body(slots, known, padded, columns, scalars, *refs):
    count = slots[1] - slots[0]
    x_refs, att_refs, cot_refs = refs[:count], refs[count : 2 * count], refs[2 * count : 3 * count]
    weights, refs = refs[3 * count : 3 * count + 4], refs[3 * count + 4 :]
    before, (kept_ref, given_ref, grad_ref, hidden_ref) = refs[: 3 * known], refs[3 * known :]
    inner, grad_low, grad_gate, grad_up, hidden = factor_rows(
        slots, padded, scalars, x_refs, att_refs, cot_refs, *weights
    )
    grad_ref[...] = grad_low
    grad_ref.leave()
    hidden_ref[...] = hidden
    hidden_ref.leave()
    core = scalars[slots[2] - 2]
    for index, now in enumerate((grad_gate, grad_up)):
        found = turned_product(
            [before[3 * at + 1 + index][...] for at in range(known)] + [now],
            [before[3 * at][...] for at in range(known)] + [inner],
            columns,
        )
        cut_rows(kept_ref, given_ref, found, index * columns, core)


def last_products(scalars, x_shards, att_shards, cot_shards, weights, slots, before, columns):
    rows, width = x_shards[0].shape
    padded = weights[-1].shape[0]
    low, high = slots
    count = high - low
    return kernel_call(
        lambda *refs: last_body((low, high, scalars.shape[0]), len(before), padded, columns, *refs),
        scalars,
        [
            *x_shards[low:high],
            *att_shards[low:high],
            *cot_shards[low:high],
            *weights,
            *[item for factors in before for item in (factors[0], factors[2], factors[3])],
        ],
        [
            shape_of((width // 2, 2 * columns), jnp.bfloat16),
            shape_of((width // 2, 2 * columns), jnp.bfloat16),
            shape_of((count * rows, width), jnp.bfloat16),
            shape_of((count * rows, padded), jnp.bfloat16),
        ],
        [],
        2 * count * rows * width * (width + 3 * padded) + 4 * len(x_shards) * rows * width * columns,
        "last_products",
    )


def head_body(head_dim, scalars, *refs):
    w_ref, q_gain_ref, k_gain_ref, freq_ref, acts_ref, came_ref, low_ref, gains_ref = refs
    parts, rows, width = acts_ref.shape
    count = parts * rows
    length = scalars[1]
    cosine, sine = turns(freq_ref[...], 0, count)
    flat = bf16_dot(acts_ref[...].reshape(count, width), w_ref[...], NN)
    flat_q, flat_kv = flat[:, :LANES], flat[:, LANES:]
    left = lane_of((count, LANES)) < head_dim
    queries = (0.125 * head_turn(flat_q, q_gain_ref[...], cosine, sine, head_dim)).astype(jnp.bfloat16)
    turned = head_turn(flat_kv, k_gain_ref[...], cosine, sine, head_dim)
    keys = jnp.where(left, turned, pltpu.roll(turned, head_dim, axis=1)).astype(jnp.bfloat16)
    values = jnp.where(left, pltpu.roll(flat_kv, head_dim, axis=1), flat_kv).astype(jnp.bfloat16)
    incoming = came_ref[:, :, :LANES].reshape(count, LANES)
    span = 2 * rows
    blocks = count // span
    key_grads = [jnp.zeros((span, LANES), jnp.float32)] * blocks
    value_grads = [jnp.zeros((span, LANES), jnp.float32)] * blocks
    query_grads = []
    nothing = jnp.zeros((span, LANES), jnp.bfloat16)
    for block in range(blocks):
        extent = (block + 1) * span
        at = slice(block * span, extent)
        key_pos = lax.broadcasted_iota(jnp.int32, (extent, span), 0)
        query_pos = block * span + lane_of((extent, span))
        counted = (key_pos <= query_pos) & (key_pos < length)
        turned = None
        for head in range(2):
            mine = (lane_of((span, LANES)) // head_dim) == head
            query = jnp.where(mine, queries[at], nothing)
            grad = jnp.where(mine, incoming[at], nothing)
            scores = jnp.where(counted, bf16_dot(keys[:extent], query, NT), MASKED)
            top = jnp.max(scores, axis=0, keepdims=True)
            weights = jnp.exp(scores - top)
            probs = weights * (1.0 / jnp.sum(weights, axis=0, keepdims=True))
            grad_probs = bf16_dot(values[:extent], grad, NT)
            delta = jnp.sum(probs * grad_probs, axis=0, keepdims=True)
            grad_scores = (probs * (grad_probs - delta)).astype(jnp.bfloat16)
            more_values = bf16_dot(probs.astype(jnp.bfloat16), grad, NN)
            more_keys = bf16_dot(grad_scores, query, NN)
            own = (lane_of((extent, LANES)) // head_dim) == head
            key = jnp.where(own, keys[:extent], jnp.zeros((extent, LANES), jnp.bfloat16))
            more = bf16_dot(key, grad_scores, TN)
            turned = more if turned is None else turned + more
            for low in range(block + 1):
                rows_at = slice(low * span, (low + 1) * span)
                key_grads[low] = key_grads[low] + more_keys[rows_at]
                value_grads[low] = value_grads[low] + more_values[rows_at]
        query_grads.append(0.125 * turned.T)
    query_grad = jnp.concatenate(query_grads, axis=0)
    key_grad = jnp.concatenate(key_grads, axis=0)
    value_grad = jnp.concatenate(value_grads, axis=0)
    key_grad = key_grad + pltpu.roll(key_grad, head_dim, axis=1)
    value_grad = value_grad + pltpu.roll(value_grad, head_dim, axis=1)
    query_low, q_part = head_turn_back(query_grad, flat_q, q_gain_ref[...], cosine, sine, head_dim)
    key_low, k_part = head_turn_back(key_grad, flat_kv, k_gain_ref[...], cosine, sine, head_dim)
    low_ref[:, :, :LANES] = query_low.astype(jnp.bfloat16).reshape(parts, rows, LANES)
    low_ref[:, :, LANES:] = (
        jnp.where(left, key_low, value_grad).astype(jnp.bfloat16).reshape(parts, rows, LANES)
    )
    gains_ref[0:1, :] = q_part
    gains_ref[1:2, :] = k_part


def head_gradients(scalars, acts, w_head, q_gain, k_gain, freq, came, head_dim):
    parts, rows, width = acts.shape
    count = parts * rows
    return kernel_call(
        lambda *refs: head_body(head_dim, *refs),
        scalars,
        [w_head, q_gain, k_gain, freq, acts, came],
        [
            shape_of((parts, rows, 2 * LANES), jnp.bfloat16),
            shape_of((8, LANES), jnp.float32),
        ],
        [],
        4 * count * width * LANES + 14 * count * count * head_dim,
        "head_gradients",
    )


def head_products_body(sources, scalars, *refs):
    low_ref, acts_ref, w_ref, came_ref = refs[:4]
    att_refs, (kept_ref, given_ref, out_kept_ref, out_given_ref, gain_ref) = refs[4:-5], refs[-5:]
    parts, rows, width = acts_ref.shape
    count = parts * rows
    core = scalars[sources]
    low = low_ref[...].reshape(count, 2 * LANES)
    turned = bf16_dot(low, acts_ref[...].reshape(count, width), TN).T
    cut_rows(kept_ref, given_ref, turned.astype(jnp.bfloat16), 0, core)
    gain_ref[...] = jnp.sum(turned * w_ref[...].astype(jnp.float32), axis=-1, keepdims=True)
    total = None
    came = came_ref.ready()
    for slot in range(sources):
        branch = came[scalars[slot], :, LANES:]
        term = bf16_dot(branch, att_refs[slot][...], TN)
        total = term if total is None else total + term
    cut_rows(out_kept_ref, out_given_ref, total.astype(jnp.bfloat16), 0, core)


def head_products(scalars, low, acts, came, w_head, att_shards):
    parts, rows, width = acts.shape
    out_width = att_shards[0].shape[1]
    return kernel_call(
        lambda *refs: head_products_body(len(att_shards), *refs),
        scalars,
        [low, acts, w_head, came, *att_shards],
        [
            shape_of((width // 2, 2 * LANES), jnp.bfloat16),
            shape_of((width // 2, 2 * LANES), jnp.bfloat16),
            shape_of((LANES // 2, out_width), jnp.bfloat16),
            shape_of((LANES // 2, out_width), jnp.bfloat16),
            shape_of((width, 1), jnp.float32),
        ],
        [],
        6 * parts * rows * width * LANES,
        "head_products",
    )


def down_body(pieces, columns, scalars, *refs):
    grad_refs, hidden_refs, (kept_ref, given_ref) = refs[:pieces], refs[pieces : 2 * pieces], refs[2 * pieces :]
    found = turned_product(
        [ref[...] for ref in hidden_refs], [ref[...] for ref in grad_refs], columns
    )
    cut_rows(kept_ref, given_ref, found, 0, scalars[0])


def down_product(scalars, grads, hiddens, columns):
    width = grads[0].shape[1]
    total = columns + -columns % LANES
    return kernel_call(
        lambda *refs: down_body(len(grads), columns, *refs),
        scalars,
        [*grads, *hiddens],
        [shape_of((width // 2, total), jnp.bfloat16)] * 2,
        [],
        2 * sum(item.shape[0] for item in grads) * width * columns,
        "down_product",
    )


def token_grad_body(head_dim, scalars, back_ref, wq_ref, wk_ref, wv_ref, x_ref, grad_mid_ref, gain_ref, out_ref):
    parts = back_ref.shape[0]
    back = back_ref.ready()
    left = lane_of((back.shape[1], LANES)) < head_dim
    keys, values = [], []
    for part in range(0, parts, 2):
        even = back[part, :, LANES:].astype(jnp.float32)
        odd = back[part + 1, :, LANES:].astype(jnp.float32)
        keys.append(jnp.where(left, even, pltpu.roll(odd, head_dim, axis=1)).astype(jnp.bfloat16))
        values.append(jnp.where(left, pltpu.roll(even, head_dim, axis=1), odd).astype(jnp.bfloat16))
    queries = [back[part, :, :LANES] for part in range(parts)]
    grad = (
        bf16_dot(jnp.concatenate(queries, axis=1), wq_ref[...], NT)
        + bf16_dot(jnp.concatenate(keys, axis=1), wk_ref[...], NT)
        + bf16_dot(jnp.concatenate(values, axis=1), wv_ref[...], NT)
    )
    values = x_ref[...].astype(jnp.float32)
    root = inverse_root(values)
    scaled = grad * gain_ref[...]
    mean = jnp.mean(scaled * values, axis=-1, keepdims=True)
    out_ref[...] = grad_mid_ref[...] + root * scaled - values * (root * root * root * mean)


def token_grad(scalars, back, w_query, w_key, w_value, x_own, grad_mid, attn_gain, head_dim):
    rows, width = x_own.shape
    inputs = [back, w_query, w_key, w_value, x_own, grad_mid, attn_gain]
    return kernel_call(
        lambda *refs: token_grad_body(head_dim, *refs),
        scalars,
        inputs,
        [shape_of((rows, width), jnp.float32)],
        [],
        4 * rows * width * width,
        "token_grad",
    )[0]


def spread_body(columns, count, head_dim, scalars, came_ref, *outs):
    parts = came_ref.shape[0]
    came = came_ref.ready()
    for part in range(parts):
        for index in range(count):
            piece = came[part, :, index * columns : (index + 1) * columns].astype(jnp.float32)
            outs[index][:, part * columns : (part + 1) * columns] = piece
    if not head_dim:
        return
    query_ref, key_ref, value_ref, gain_ref = outs[count:]
    start = count * columns
    for part in range(parts):
        piece = came[part, :, start : start + 2 * LANES].astype(jnp.float32)
        query_ref[:, part * LANES : (part + 1) * LANES] = piece[:, :LANES]
        at = slice(part * head_dim, (part + 1) * head_dim)
        key_ref[:, at] = piece[:, LANES : LANES + head_dim]
        value_ref[:, at] = piece[:, LANES + head_dim :]
    total = came[0, :, start + 2 * LANES :].astype(jnp.float32)
    for part in range(1, parts):
        total = total + came[part, :, start + 2 * LANES :].astype(jnp.float32)
    gain_ref[...] = total


def spread_out(scalars, came, columns, count, head_dim=0):
    parts, rows, width = came.shape
    outs = [shape_of((rows, parts * columns), jnp.float32)] * count
    if head_dim:
        outs += [shape_of((rows, parts * size), jnp.float32) for size in (LANES, head_dim, head_dim)]
        outs.append(shape_of((rows, width - count * columns - 2 * LANES), jnp.float32))
    return kernel_call(
        lambda *refs: spread_body(columns, count, head_dim, *refs),
        scalars,
        [came],
        outs,
        [],
        0,
        "spread_out",
    )


def swapped(value, axis, by):
    count = lax.axis_size(axis)
    return lax.ppermute(value, axis, [(i, i ^ by) for i in range(count)])


def after(value, *others):
    return lax.optimization_barrier((value, *others))[0]


def split_form(
    tokens,
    lengths,
    attn_gain,
    q_gain,
    k_gain,
    w_query,
    w_key,
    w_value,
    w_out,
    ffn_gain,
    w_gate,
    w_up,
    w_down,
    cotangent,
):
    _, rows, width = tokens.shape
    head_dim = q_gain.shape[0]
    hidden_width = w_gate.shape[1]
    parts = lax.axis_size("ctx")
    sums = lax.axis_size("dp")
    place = lax.axis_index("ctx").astype(jnp.int32)
    row = lax.axis_index("dp").astype(jnp.int32)
    core, line = row % 2, row // 2
    length = lengths[0]
    columns = hidden_width // parts
    each = width // (sums * parts)
    steps = parts // 2
    sources = [((place - 2 * (slot // 2)) % parts) ^ (slot % 2) for slot in range(parts)]
    freq = THETA ** (-(jnp.arange(head_dim // 2, dtype=jnp.float32) * 2.0 / head_dim))
    sign = jnp.ones_like(freq)
    freq = jnp.stack([jnp.concatenate([freq] * 4), jnp.concatenate([-sign, sign, -sign, sign])])
    attn_row, ffn_row = attn_gain[None], ffn_gain[None]
    q_row = jnp.concatenate([q_gain, q_gain])[None]
    k_row = jnp.concatenate([k_gain, k_gain])[None]
    x_own, cot_own = tokens[0], cotangent[0]

    def own_columns(weights, size, axis):
        return lax.dynamic_slice_in_dim(weights, place * size, size, axis)

    w_head = jnp.concatenate(
        [
            own_columns(w_query, LANES, 1),
            own_columns(w_key, head_dim, 1),
            own_columns(w_value, head_dim, 1),
        ],
        axis=-1,
    )
    spare = -columns % LANES
    wide = columns + spare
    gate_up = jnp.concatenate(
        [
            jnp.pad(own_columns(w_gate, columns, 1), ((0, 0), (0, spare))),
            jnp.pad(own_columns(w_up, columns, 1), ((0, 0), (0, spare))),
        ],
        axis=-1,
    )
    down = jnp.pad(own_columns(w_down, columns, 0), ((0, spare), (0, 0)))

    half = parts // 2
    held, x_shards, early = x_own, [], None
    for step in range(steps):
        if step:
            held = from_behind(held, "ctx", 2)
        other = held
        if step == steps - 1:
            early = key_value_part(
                jnp.stack(sources[:half]),
                x_shards[:half],
                w_key,
                w_value,
                attn_row,
                k_row,
                freq,
                parts,
                head_dim,
            )
            other = after(held, early[0], gate_up, down, w_head, x_shards[-1])
        x_shards += [held, swapped(other, "ctx", 1)]
    cot_shards = [cot_own]

    def spread_step(shards, source, count, *waits):
        source = after(source, *waits)
        shards.append(swapped(source, "ctx", 1))
        if count < steps:
            shards.append(from_behind(source, "ctx", 2))

    spread_step(cot_shards, cot_own, 1, *x_shards[-2:])
    where = jnp.stack([place, length])
    attn_low, acts = attend(
        jnp.stack(sources + [place, length]),
        x_shards[half:],
        x_own,
        early,
        w_key,
        w_value,
        w_query,
        attn_row,
        q_row,
        k_row,
        freq,
        head_dim,
    )

    chunk = next(c for c in (512, 384, 256, 128) if hidden_width % c == 0)
    slots = jnp.stack(sources + [core, length])
    weights = [w_out, ffn_row, gate_up, down]
    att_shards, factors, came = [after(attn_low, *cot_shards)], [], None
    result, grad_mid, sent, ffn_gain_part = ffn_part(
        where,
        [x_own, att_shards[0], cot_own, w_out, ffn_row],
        [w_gate, w_up, w_down],
        (0, hidden_width // chunk),
        chunk,
        [],
        True,
        parts,
        sums,
    )
    covers = [[sent]]
    for step in range(1, steps):
        waits = covers[-1] if step > 2 else []
        spread_step(att_shards, att_shards[-1], step, *waits)
        spread_step(cot_shards, cot_shards[-1], step + 1, *waits)
        if step == 1:
            came = lax.all_to_all(after(sent, *att_shards[1:], *cot_shards[3:]), "ctx", 0, 0, tiled=True)
            continue
        low = 2 * step - 4
        x_ready = list(x_shards)
        x_ready[low] = after(x_ready[low], covers[-1][0], *att_shards[low + 1 : low + 3], *cot_shards[low + 1 : low + 3])
        factors.append(
            factor_part(
                slots, x_ready, att_shards + [None] * parts, cot_shards + [None] * parts, weights, (low, low + 2)
            )
        )
        covers.append([factors[-1][0]])
    spread_step(att_shards, att_shards[-1], steps, *covers[-1], *att_shards, *cot_shards)
    low, head_gains = head_gradients(
        where, acts, w_head, q_row, k_row, freq, after(came, factors[-1][0]), head_dim
    )
    low = after(low, att_shards[-1])
    back = lax.all_to_all(low, "ctx", 0, 0, tiled=True)
    head_kept, head_given, out_kept, out_given, attn_part = head_products(
        slots, low, acts, came, w_head, att_shards
    )
    def core_sum(kept, given):
        total = kept.astype(jnp.float32) + swapped(given, "dp", 1).astype(jnp.float32)
        return total.astype(jnp.bfloat16)

    def line_halves(half):
        size = half.shape[0] // 2
        mine = lax.dynamic_slice_in_dim(half, line * size, size, 0)
        return mine, lax.dynamic_slice_in_dim(half, (1 - line) * size, size, 0)

    def line_sum(half):
        mine, other = line_halves(half)
        return mine.astype(jnp.float32) + swapped(other, "dp", 2).astype(jnp.float32)

    def split_pair(values):
        high = lax.reduce_precision(values, 8, 7)
        return jnp.concatenate([high, values - high]).astype(jnp.bfloat16)

    gains = jnp.concatenate(
        [
            attn_part[:, 0] / attn_gain,
            ffn_gain_part[0],
            head_gains[0, :head_dim] + head_gains[0, head_dim:],
            head_gains[1, :head_dim],
        ]
    )
    gain_count = gains.shape[0]
    gains = gains + swapped(gains, "dp", 1)
    gains = gains + swapped(gains, "dp", 2)
    pieces = split_pair(gains)
    room = -(-pieces.shape[0] // (each * 64)) * 64
    pieces = jnp.pad(pieces, (0, each * room - pieces.shape[0]))
    pieces = jnp.broadcast_to(pieces.reshape(1, each, room), (parts, each, room))
    head_half = core_sum(head_kept, head_given)
    out_half = core_sum(out_kept, out_given)
    start = 2 * len(factors)
    x_ready = x_shards[:start] + [after(x_shards[start], head_half)] + x_shards[start + 1 :]
    kept, given, late_grad, late_hidden = last_products(
        slots, x_ready, att_shards, cot_shards, weights, (start, parts), factors, columns
    )
    head_sum = line_sum(head_half)
    out_sum = line_sum(out_half)
    first_half = core_sum(kept, after(given, back, pieces, head_sum))
    down_kept, down_given = down_product(
        core[None],
        [item[1] for item in factors] + [after(late_grad, first_half)],
        [item[4] for item in factors] + [late_hidden],
        columns,
    )
    first_sum = line_sum(first_half)
    grad_tokens = token_grad(
        where, after(back, down_kept), w_query, w_key, w_value, x_own, grad_mid, attn_row, head_dim
    )
    down_half = core_sum(down_kept, after(down_given, first_sum, grad_tokens))[:, :columns]

    def exchanged(items):
        joined = jnp.concatenate(
            [item.astype(jnp.bfloat16).reshape(parts, each, -1) for item in items], axis=-1
        )
        return lax.all_to_all(joined, "ctx", 0, 0, tiled=True)

    first_came = exchanged([first_sum])
    down_sum = line_sum(down_half)
    last = exchanged([down_sum, head_sum, pieces])
    cut = core[None]

    gate_sum, up_sum = spread_out(cut, first_came, columns, 2)
    down_out, query_out, key_out, value_out, totals = spread_out(cut, last, columns, 1, head_dim)
    totals = totals.reshape(-1)
    totals = totals[:gain_count] + totals[gain_count : 2 * gain_count]
    return (
        result[None],
        grad_tokens[None],
        totals[:width],
        totals[2 * width : 2 * width + head_dim],
        totals[2 * width + head_dim :],
        query_out,
        key_out,
        value_out,
        out_sum.T,
        totals[width : 2 * width],
        gate_sum,
        up_sum,
        down_out.T,
    )


def per_device(*arguments):
    tokens, q_gain, w_query, w_key = (arguments[i] for i in (0, 3, 5, 6))
    parts = lax.axis_size("ctx")
    sums = lax.axis_size("dp")
    head_dim = q_gain.shape[0]
    fits = (
        tokens.shape[0] == 1
        and sums == 4
        and parts % 2 == 0
        and 2 * head_dim == LANES
        and w_query.shape[1] == parts * LANES
        and w_key.shape[1] == parts * head_dim
        and tokens.shape[2] == sums * parts * 32
        and tokens.shape[1] == LANES
        and parts <= 8
    )
    return (split_form if fits else ring_form)(*arguments)


def solution(mesh):
    placed = (
        P("dp", "ctx", None),
        P("dp"),
        P(),
        P(),
        P(),
        P(),
        P(),
        P(),
        P(),
        P(),
        P(),
        P(),
        P(),
        P("dp", "ctx", None),
    )
    return jax.shard_map(
        per_device,
        mesh=mesh,
        in_specs=placed,
        out_specs=(
            P("dp", "ctx", None),
            P("dp", "ctx", None),
            P(),
            P(),
            P(),
            P(("dp", "ctx"), None),
            P(("dp", "ctx"), None),
            P(("dp", "ctx"), None),
            P(None, ("dp", "ctx")),
            P(),
            P(("dp", "ctx"), None),
            P(("dp", "ctx"), None),
            P(None, ("dp", "ctx")),
        ),
        check_vma=False,
    )
```

```python
import jax
import jax.numpy as jnp
from jax import lax
from jax.experimental import pallas as pl
from jax.experimental.pallas import tpu as pltpu
from jax.sharding import PartitionSpec as P

EPS = 1e-05
THETA = 1000000.0
MASKED = -1e30


def passed_along(shard, axis, by):
    count = lax.axis_size(axis)
    pairs = [(i, i + by) for i in range(count) if 0 <= i + by < count]
    return lax.ppermute(shard, axis, pairs)


def from_behind(value, axis, steps):
    count = lax.axis_size(axis)
    pairs = [(source, (source + steps) % count) for source in range(count)]
    return lax.ppermute(value, axis, pairs)


def root_norm(values, gain):
    return values * lax.rsqrt(jnp.mean(values * values, axis=-1, keepdims=True) + EPS) * gain


def rotate(values, cosine, sine):
    half = values.shape[-1] // 2
    first_half = values[..., :half]
    second_half = values[..., half:]
    return jnp.concatenate(
        [first_half * cosine - second_half * sine, second_half * cosine + first_half * sine],
        axis=-1,
    )


def angles(positions, width):
    freqs = THETA ** (-(jnp.arange(width // 2, dtype=jnp.float32) * 2.0 / width))
    turned = positions.astype(jnp.float32)[:, None] * freqs[None, :]
    return (jnp.cos(turned), jnp.sin(turned))


def query_form(flat, gain, cosine, sine, groups):
    seq_count, row_count, width = flat.shape
    head_dim = gain.shape[0]
    normed = root_norm(flat.reshape(seq_count, row_count, width // head_dim, head_dim), gain)
    turned = rotate(normed, cosine, sine)
    return turned.reshape(seq_count, row_count, -1, groups, head_dim).transpose(0, 2, 3, 1, 4)


def key_form(flat, gain, cosine, sine):
    seq_count, row_count, width = flat.shape
    head_dim = gain.shape[0]
    normed = root_norm(flat.reshape(seq_count, row_count, width // head_dim, head_dim), gain)
    return rotate(normed, cosine, sine)


def ring_form(
    tokens,
    lengths,
    attn_gain,
    q_gain,
    k_gain,
    w_query,
    w_key,
    w_value,
    w_out,
    ffn_gain,
    w_gate,
    w_up,
    w_down,
    cotangent,
):
    seq_count, row_count, width = tokens.shape
    head_dim = q_gain.shape[0]
    heads = w_query.shape[1] // head_dim
    kv_heads = w_key.shape[1] // head_dim
    groups = heads // kv_heads
    loop_size = lax.axis_size("ctx")
    my_place = lax.axis_index("ctx")
    query_start = my_place * row_count
    query_pos = query_start + jnp.arange(row_count, dtype=jnp.int32)
    longest = jnp.max(lengths)
    cosine, sine = angles(query_pos, head_dim)
    cosine = cosine[None, :, None, :]
    sine = sine[None, :, None, :]
    inputs = tokens.astype(jnp.float32)
    acts = root_norm(inputs, attn_gain).astype(jnp.bfloat16).reshape(-1, width)
    qproj = jnp.dot(acts, w_query, preferred_element_type=jnp.float32).reshape(
        seq_count, row_count, -1
    )
    kproj = jnp.dot(acts, w_key, preferred_element_type=jnp.float32).reshape(
        seq_count, row_count, -1
    )
    vproj = jnp.dot(acts, w_value, preferred_element_type=jnp.float32)
    queries = query_form(qproj, q_gain, cosine, sine, groups).astype(jnp.bfloat16)
    keys = key_form(kproj, k_gain, cosine, sine).astype(jnp.bfloat16)
    values = vproj.astype(jnp.bfloat16).reshape(seq_count, row_count, kv_heads, head_dim)
    key_values = jnp.stack([keys, values])

    def block_mask(key_start, count):
        key_pos = key_start + jnp.arange(count, dtype=jnp.int32)
        causal = key_pos[None, None, :] <= query_pos[None, :, None]
        inside = key_pos[None, None, :] < lengths[:, None, None]
        return (causal & inside)[:, None, None, :, :]

    def needed(key_start):
        return (key_start < query_start + row_count) & (key_start < longest)

    def scores_of(key_piece):
        return 0.125 * jnp.einsum(
            "scgtd,sucd->scgtu", queries, key_piece, preferred_element_type=jnp.float32
        )

    def absorb(state, pair, key_start):

        def absorb_work(current):
            top_row, row_total, summed = current
            counted = block_mask(key_start, pair.shape[2])
            masked = jnp.where(counted, scores_of(pair[0]), MASKED)
            top_new = jnp.maximum(top_row, jnp.max(masked, axis=-1))
            weights = jnp.where(counted, jnp.exp(masked - top_new[..., None]), 0.0)
            factor = jnp.exp(top_row - top_new)
            row_total = row_total * factor + jnp.sum(weights, axis=-1)
            summed = summed * factor[..., None] + jnp.einsum(
                "scgtu,sucd->scgtd",
                weights.astype(jnp.bfloat16),
                pair[1],
                preferred_element_type=jnp.float32,
            )
            return (top_new, row_total, summed)

        return lax.cond(needed(key_start), absorb_work, lambda current: current, state)

    stat_shape = (seq_count, kv_heads, groups, row_count)
    start_state = (
        jnp.full(stat_shape, MASKED, jnp.float32),
        jnp.zeros(stat_shape, jnp.float32),
        jnp.zeros(stat_shape + (head_dim,), jnp.float32),
    )
    first_state = absorb(start_state, key_values, query_start)

    def forward_turn(step, carry):
        held, state = carry
        held = passed_along(held, "ctx", 1)
        source = (my_place - step) % loop_size
        return (held, absorb(state, held, source * row_count))

    _, (top_row, row_total, summed) = lax.fori_loop(
        1, loop_size, forward_turn, (key_values, first_state)
    )
    attended = summed / row_total[..., None]
    attn_low = attended.astype(jnp.bfloat16)
    out_heads = w_out.reshape(kv_heads, groups, head_dim, width)
    attn_branch = jnp.einsum(
        "scgtd,cgde->ste", attn_low, out_heads, preferred_element_type=jnp.float32
    )
    middle = inputs + attn_branch
    inner = root_norm(middle, ffn_gain).astype(jnp.bfloat16).reshape(-1, width)
    gate_proj = jnp.dot(inner, w_gate, preferred_element_type=jnp.float32)
    up_proj = jnp.dot(inner, w_up, preferred_element_type=jnp.float32)
    hidden = (jax.nn.silu(gate_proj) * up_proj).astype(jnp.bfloat16)
    output = middle + jnp.dot(hidden, w_down, preferred_element_type=jnp.float32).reshape(
        seq_count, row_count, width
    )
    result = output.astype(jnp.bfloat16)
    valid = (query_pos[None, :] < lengths[:, None]).astype(jnp.float32)
    grad_out = cotangent.astype(jnp.float32) * valid[..., None]
    grad_low = grad_out.astype(jnp.bfloat16).reshape(-1, width)
    down_turned = jnp.einsum("nd,nf->df", grad_low, hidden, preferred_element_type=jnp.float32)
    grad_hidden = jnp.einsum("nd,fd->nf", grad_low, w_down, preferred_element_type=jnp.float32)
    _, pull_gate = jax.vjp(lambda gate_in, up_in: jax.nn.silu(gate_in) * up_in, gate_proj, up_proj)
    grad_gate, grad_up = pull_gate(grad_hidden)
    gate_low = grad_gate.astype(jnp.bfloat16)
    up_low = grad_up.astype(jnp.bfloat16)
    gate_local = jnp.einsum("nd,nf->df", inner, gate_low, preferred_element_type=jnp.float32)
    up_local = jnp.einsum("nd,nf->df", inner, up_low, preferred_element_type=jnp.float32)
    grad_inner = jnp.einsum("nf,df->nd", gate_low, w_gate, preferred_element_type=jnp.float32)
    grad_inner = grad_inner + jnp.einsum(
        "nf,df->nd", up_low, w_up, preferred_element_type=jnp.float32
    )
    _, pull_second = jax.vjp(root_norm, middle, ffn_gain)
    grad_middle, ffn_local = pull_second(grad_inner.reshape(seq_count, row_count, width))
    grad_middle = grad_middle + grad_out
    branch_low = grad_middle.astype(jnp.bfloat16)
    out_turned = jnp.einsum(
        "std,scgte->dcge", branch_low, attn_low, preferred_element_type=jnp.float32
    ).reshape(width, -1)
    grad_attended = jnp.einsum(
        "ste,cgde->scgtd", branch_low, out_heads, preferred_element_type=jnp.float32
    ).astype(jnp.bfloat16)
    grad_wide = grad_attended.astype(jnp.float32)
    delta = jnp.sum(grad_wide * attended, axis=-1)
    grad_scaled = grad_wide / row_total[..., None]

    def block_back(pair, key_start):
        counted = block_mask(key_start, pair.shape[2])
        weights = jnp.where(counted, jnp.exp(scores_of(pair[0]) - top_row[..., None]), 0.0)
        probs = weights / row_total[..., None]
        grad_values = jnp.einsum(
            "scgtu,scgtd->sucd",
            weights.astype(jnp.bfloat16),
            grad_scaled,
            preferred_element_type=jnp.float32,
        )
        grad_probs = jnp.einsum(
            "scgtd,sucd->scgtu", grad_attended, pair[1], preferred_element_type=jnp.float32
        )
        grad_scores = (probs * (grad_probs - delta[..., None])).astype(jnp.bfloat16)
        more_queries = 0.125 * jnp.einsum(
            "scgtu,sucd->scgtd", grad_scores, pair[0], preferred_element_type=jnp.float32
        )
        grad_keys = 0.125 * jnp.einsum(
            "scgtu,scgtd->sucd", grad_scores, queries, preferred_element_type=jnp.float32
        )
        return (more_queries, jnp.stack([grad_keys, grad_values]))

    start_queries = jnp.zeros(stat_shape + (head_dim,), jnp.float32)

    def backward_turn(step, carry):
        held, held_grads, grad_queries = carry
        key_start = (my_place - step) % loop_size * row_count

        def backward_work(current):
            query_acc, pair_acc = current
            more_queries, more_pair = block_back(held, key_start)
            return (query_acc + more_queries, pair_acc + more_pair)

        grad_queries, held_grads = lax.cond(
            needed(key_start), backward_work, lambda current: current, (grad_queries, held_grads)
        )
        held = passed_along(held, "ctx", 1)
        held_grads = from_behind(held_grads.astype(jnp.bfloat16), "ctx", 1).astype(held_grads.dtype)
        return (held, held_grads, grad_queries)

    start_grads = jnp.zeros((2, seq_count, row_count, kv_heads, head_dim), jnp.float32)
    _, pair_grads, grad_queries = lax.fori_loop(
        0, loop_size, backward_turn, (key_values, start_grads, start_queries)
    )
    _, pull_query = jax.vjp(
        lambda proj_in, gain_in: query_form(proj_in, gain_in, cosine, sine, groups), qproj, q_gain
    )
    grad_qproj, q_local = pull_query(grad_queries)
    _, pull_key = jax.vjp(
        lambda proj_in, gain_in: key_form(proj_in, gain_in, cosine, sine), kproj, k_gain
    )
    grad_kproj, k_local = pull_key(pair_grads[0])
    query_low = grad_qproj.reshape(-1, heads * head_dim).astype(jnp.bfloat16)
    key_low = grad_kproj.reshape(-1, kv_heads * head_dim).astype(jnp.bfloat16)
    value_low = pair_grads[1].reshape(-1, kv_heads * head_dim).astype(jnp.bfloat16)
    query_local = jnp.einsum("nd,ne->de", acts, query_low, preferred_element_type=jnp.float32)
    key_local = jnp.einsum("nd,ne->de", acts, key_low, preferred_element_type=jnp.float32)
    value_local = jnp.einsum("nd,ne->de", acts, value_low, preferred_element_type=jnp.float32)
    grad_acts = jnp.einsum("ne,de->nd", query_low, w_query, preferred_element_type=jnp.float32)
    grad_acts = grad_acts + jnp.einsum(
        "ne,de->nd", key_low, w_key, preferred_element_type=jnp.float32
    )
    grad_acts = grad_acts + jnp.einsum(
        "ne,de->nd", value_low, w_value, preferred_element_type=jnp.float32
    )
    _, pull_first = jax.vjp(root_norm, inputs, attn_gain)
    grad_inputs, attn_local = pull_first(grad_acts.reshape(seq_count, row_count, width))
    grad_inputs = grad_inputs + grad_middle
    query_sum, key_sum, value_sum, out_sum, gate_sum, up_sum, down_sum = (
        lax.psum_scatter(query_local, ("dp", "ctx"), scatter_dimension=0, tiled=True),
        lax.psum_scatter(key_local, ("dp", "ctx"), scatter_dimension=0, tiled=True),
        lax.psum_scatter(value_local, ("dp", "ctx"), scatter_dimension=0, tiled=True),
        lax.psum_scatter(out_turned, ("dp", "ctx"), scatter_dimension=0, tiled=True),
        lax.psum_scatter(gate_local, ("dp", "ctx"), scatter_dimension=0, tiled=True),
        lax.psum_scatter(up_local, ("dp", "ctx"), scatter_dimension=0, tiled=True),
        lax.psum_scatter(down_turned, ("dp", "ctx"), scatter_dimension=0, tiled=True),
    )
    attn_sum, q_sum, k_sum, ffn_sum = lax.psum(
        (attn_local, q_local, k_local, ffn_local), ("dp", "ctx")
    )
    return (
        result,
        grad_inputs,
        attn_sum,
        q_sum,
        k_sum,
        query_sum,
        key_sum,
        value_sum,
        out_sum.T,
        ffn_sum,
        gate_sum,
        up_sum,
        down_sum.T,
    )


LANES = 128
VMEM_LIMIT = 60 << 20
NN = ((1,), (0,))
NT = ((1,), (1,))
TN = ((0,), (0,))


def bf16_dot(left, right, dims):
    return lax.dot_general(left, right, (dims, ((), ())), preferred_element_type=jnp.float32)


def inverse_root(values):
    return lax.rsqrt(jnp.mean(values * values, axis=-1, keepdims=True) + EPS)


def lane_of(shape):
    return lax.broadcasted_iota(jnp.int32, shape, len(shape) - 1)


def head_mean(values, head_dim):
    rows = lax.broadcasted_iota(jnp.int32, (LANES, LANES), 0) // head_dim
    columns = lane_of((LANES, LANES)) // head_dim
    spread = jnp.where(rows == columns, 1.0 / head_dim, 0.0).astype(jnp.bfloat16)
    return bf16_dot(values.astype(jnp.bfloat16), spread, NN)


def partner(values, head_dim):
    half = head_dim // 2
    first = lane_of(values.shape) % head_dim < half
    return jnp.where(
        first, pltpu.roll(values, LANES - half, axis=1), pltpu.roll(values, half, axis=1)
    )


def head_turn(flat, gain, cosine, sine, head_dim):
    normed = flat * lax.rsqrt(head_mean(flat * flat, head_dim) + EPS) * gain
    return normed * cosine + partner(normed, head_dim) * sine


def head_turn_back(grad, flat, gain, cosine, sine, head_dim):
    back = grad * cosine + partner(grad * sine, head_dim)
    root = lax.rsqrt(head_mean(flat * flat, head_dim) + EPS)
    scaled = gain * back
    mean = head_mean(scaled * flat, head_dim)
    return (
        root * scaled - flat * (root * root * root * mean),
        jnp.sum(back * flat * root, axis=0, keepdims=True),
    )


def turns(freq, base_ref, starts):
    base_cos, base_sin = base_ref[0], base_ref[1]
    cosines, sines = [], []
    for start in starts:
        angle = jnp.asarray(start, jnp.float32) * freq[0:1, :]
        cos, sin = jnp.cos(angle), jnp.sin(angle)
        cosines.append(base_cos * cos - base_sin * sin)
        sines.append((base_sin * cos + base_cos * sin) * freq[1:2, :])
    return jnp.concatenate(cosines, axis=0), jnp.concatenate(sines, axis=0)


def whole_spec(shape):
    return pl.BlockSpec(shape, lambda *_: (0,) * len(shape))


def cost_of(inputs, outs, flops):
    moved = sum(item.size * item.dtype.itemsize for item in (*inputs, *outs))
    return pl.CostEstimate(flops=flops, bytes_accessed=moved, transcendentals=0)


class Arriving:
    def __init__(self, sources, targets, signals, ref):
        self.copies = [pltpu.make_async_copy(*item) for item in zip(sources, targets, signals)]
        self.ref, self.shape = ref, ref.shape
        for copy in self.copies:
            copy.start()

    def ready(self):
        for copy in self.copies:
            copy.wait()
        self.copies = []
        return self.ref

    def __getitem__(self, at):
        return self.ready()[at]


class Leaving:
    def __init__(self, ref, target, signal):
        self.ref, self.target, self.signal, self.shape = ref, target, signal, ref.shape
        self.copy = None

    def __setitem__(self, at, value):
        self.ref[at] = value

    def __getitem__(self, at):
        return self.ref[at]

    def leave(self):
        if self.copy is None:
            self.copy = pltpu.make_async_copy(self.ref, self.target, self.signal)
            self.copy.start()


class Stack:
    def __init__(self, arrays):
        self.arrays, self.dtype = list(arrays), arrays[0].dtype
        self.shape = (len(arrays),) + arrays[0].shape
        self.size = len(arrays) * arrays[0].size


class Rows:
    def __init__(self, array, scalar, rows=0):
        self.array, self.scalar, self.rows = array, scalar, rows
        self.shape = (rows,) + array.shape[1:] if rows else array.shape[1:]
        self.dtype, self.size = array.dtype, array.size

    def of(self, ref, scalars):
        at = scalars[self.scalar]
        if not self.rows:
            return ref.at[at]
        return ref.at[pl.ds(pl.multiple_of(at * self.rows, self.rows), self.rows)]


def kernel_call(body, scalars, inputs, outs, scratch, flops, name, held=(), stacks=()):
    arrays = [item.arrays if isinstance(item, Stack) else [getattr(item, "array", item)] for item in inputs]
    count, kept = sum(map(len, arrays)), len(held)

    def run(scalars_ref, *refs):
        given, refs = refs[:count], refs[count + kept :]
        targets, refs = refs[: len(outs)], refs[len(outs) :]
        stack_refs, refs = refs[: len(stacks)], refs[len(stacks) :]
        buffers, refs = refs[: len(inputs)], refs[len(inputs) :]
        results, refs = refs[: len(outs)], refs[len(outs) :]
        signals, own = refs[0], refs[1:]
        arriving, used = [], 0
        for item, group, buffer in zip(inputs, arrays, buffers):
            sources = list(given[used : used + len(group)])
            places = [buffer.at[at] for at in range(len(group))] if isinstance(item, Stack) else [buffer]
            if isinstance(item, Rows):
                sources = [item.of(sources[0], scalars_ref)]
            slots = [signals.at[used + at] for at in range(len(group))]
            arriving.append(Arriving(sources, places, slots, buffer))
            used += len(group)
        leaving = [
            Leaving(result, target, signals.at[count + at])
            for at, (result, target) in enumerate(zip(results, targets))
        ]
        body(scalars_ref, *arriving, *leaving, *stack_refs, *own)
        for item in arriving:
            item.ready()
        for item in leaving:
            item.leave()
        for item in leaving:
            item.copy.wait()

    near = pl.BlockSpec(memory_space=pl.ANY)
    far = pl.BlockSpec(memory_space=pltpu.HBM)
    return pl.pallas_call(
        run,
        in_specs=[pl.BlockSpec(memory_space=pltpu.SMEM)] + [near] * count + [far] * kept,
        out_specs=[far] * (len(outs) + len(stacks)),
        out_shape=[*outs, *stacks],
        scratch_shapes=[pltpu.VMEM(item.shape, item.dtype) for item in (*inputs, *outs)]
        + [pltpu.SemaphoreType.DMA((count + len(outs),))]
        + list(scratch),
        input_output_aliases={1 + count + at: len(outs) + at for at in range(kept)},
        cost_estimate=cost_of(inputs, (*outs, *stacks), flops),
        compiler_params=pltpu.CompilerParams(vmem_limit_bytes=VMEM_LIMIT),
        name=name,
    )(scalars, *[array for group in arrays for array in group], *held)


def shape_of(shape, dtype):
    return jax.ShapeDtypeStruct(shape, dtype)


def stacked(values):
    return jnp.concatenate(
        [values[:, at : at + LANES] for at in range(0, values.shape[1], LANES)], axis=0
    )


def key_value_rows(scalars, shard_refs, wk_ref, wv_ref, gain_ref, k_gain_ref, freq, base_ref, acts, kv, head_dim):
    count, rows = len(shard_refs), shard_refs[0].shape[0]
    for at, ref in enumerate(shard_refs):
        values = ref[...].astype(jnp.float32)
        acts[at] = (values * inverse_root(values) * gain_ref[...]).astype(jnp.bfloat16)
    cosine, sine = turns(freq, base_ref, [scalars[at] * rows for at in range(count)])
    flat = acts[...].reshape(count * rows, -1)
    left = lane_of((count * rows, LANES)) < head_dim
    keys = bf16_dot(flat, wk_ref[...], NN)
    values = bf16_dot(flat, wv_ref[...], NN)
    for chunk in range(wk_ref.shape[1] // LANES):
        at = slice(chunk * LANES, (chunk + 1) * LANES)
        turned = head_turn(keys[:, at], k_gain_ref[...], cosine, sine, head_dim)
        value = values[:, at]
        for odd in range(2):
            pair = jnp.where(
                left,
                pltpu.roll(turned, head_dim, axis=1) if odd else turned,
                value if odd else pltpu.roll(value, head_dim, axis=1),
            )
            start = (2 * chunk + odd) * LANES
            kv[:, :, start : start + LANES] = pair.astype(jnp.bfloat16).reshape(count, rows, LANES)


def key_value_body(count, head_dim, scalars, *refs):
    acts_out, kv_out, acts, kv, signals = refs[count + 6 :]
    key_value_rows(
        scalars, refs[:count], *refs[count : count + 4], refs[count + 4][...], refs[count + 5], acts, kv, head_dim
    )
    leaving = [
        pltpu.make_async_copy(buffer.at[at], out.at[scalars[at]], signals.at[2 * at + turn])
        for at in range(count)
        for turn, (buffer, out) in enumerate(((acts, acts_out), (kv, kv_out)))
    ]
    for copy in leaving:
        copy.start()
    for copy in leaving:
        copy.wait()


def key_value_part(scalars, shards, weights, parts, head_dim, held):
    rows, width = shards[0].shape
    kv_width = 2 * weights[0].shape[1]
    count = len(shards)
    return kernel_call(
        lambda *refs: key_value_body(count, head_dim, *refs),
        scalars,
        [*shards, *weights],
        [],
        [
            pltpu.VMEM((count, rows, width), jnp.bfloat16),
            pltpu.VMEM((count, rows, kv_width), jnp.bfloat16),
            pltpu.SemaphoreType.DMA((2 * count,)),
        ],
        2 * count * rows * width * kv_width,
        "key_value_part",
        held,
        [
            shape_of((parts, rows, width), jnp.bfloat16),
            shape_of((parts, rows, kv_width), jnp.bfloat16),
        ],
    )


def attend_body(known, fresh, head_dim, scalars, *refs):
    shard_refs, refs = refs[:fresh], refs[fresh:]
    wk_ref, wv_ref, gain_ref, k_gain_ref, freq_ref, base_ref, x_ref, wq_ref, q_gain_ref = refs[:9]
    kv_refs, refs = refs[9 : 9 + known], refs[9 + known :]
    out_ref, acts_out, acts, kv, bias, turned, signals = refs
    place, length = scalars[known + fresh], scalars[known + fresh + 1]
    rows = x_ref.shape[0]
    count = (known + fresh) * rows
    chunks = wq_ref.shape[1] // LANES
    freq = freq_ref[...]
    key_value_rows(
        [scalars[known + at] for at in range(fresh)],
        shard_refs,
        wk_ref,
        wv_ref,
        gain_ref,
        k_gain_ref,
        freq,
        base_ref,
        acts,
        kv.at[pl.ds(known, fresh)],
        head_dim,
    )
    leaving = [
        pltpu.make_async_copy(acts.at[at], acts_out.at[scalars[known + at]], signals.at[at])
        for at in range(fresh)
    ]
    for copy in leaving:
        copy.start()
    values = x_ref[...].astype(jnp.float32)
    own = (values * inverse_root(values) * gain_ref[...]).astype(jnp.bfloat16)
    tables = turns(freq, base_ref, [place * rows])
    cosine, sine = (jnp.concatenate([table] * chunks, axis=0) for table in tables)
    flat = stacked(bf16_dot(own, wq_ref[...], NN))
    turned[...] = (0.125 * head_turn(flat, q_gain_ref[...], cosine, sine, head_dim)).reshape(
        chunks, rows, LANES
    )
    query_pos = place * rows + lane_of((rows, 2 * rows)) % rows
    for slot in range(known + fresh):
        key_pos = scalars[slot] * rows + lax.broadcasted_iota(jnp.int32, (rows, 2 * rows), 0)
        bias[slot * rows : (slot + 1) * rows, :] = jnp.where(
            (key_pos <= query_pos) & (key_pos < length), 0.0, MASKED
        )
        if slot < known:
            kv[slot] = kv_refs[slot][...]
    left = lane_of((rows, LANES)) < head_dim

    def one_head(index, carry):
        at = pl.ds(pl.multiple_of(index * LANES, LANES), LANES)
        mine = turned[index]
        both = jnp.concatenate(
            [jnp.where(left, mine, 0.0), jnp.where(left, pltpu.roll(mine, head_dim, axis=1), 0.0)],
            axis=0,
        ).astype(jnp.bfloat16)
        head_kv = kv[:, :, at].reshape(count, LANES)
        scores = bf16_dot(head_kv, both, NT) + bias[...]
        top = jnp.max(scores, axis=0, keepdims=True)
        weights = jnp.exp(scores - top)
        total = jnp.sum(weights, axis=0, keepdims=True)
        summed = bf16_dot(head_kv, weights.astype(jnp.bfloat16), TN)[head_dim:] / total
        heads = jnp.concatenate([summed[:, :rows], summed[:, rows:]], axis=0)
        out_ref[:, at] = heads.T.astype(jnp.bfloat16)
        return carry

    lax.fori_loop(0, chunks, one_head, 0, unroll=2)
    for copy in leaving:
        copy.wait()


def attend(scalars, shards, x_own, early, weights, w_query, q_gain, head_dim):
    parts, rows, width = early[0].shape
    q_width, kv_width = w_query.shape[1], 2 * weights[0].shape[1]
    fresh = len(shards)
    known = parts - fresh
    blocks = [Rows(early[1], at) for at in range(known)]
    return kernel_call(
        lambda *refs: attend_body(known, fresh, head_dim, *refs),
        scalars,
        [*shards, *weights, x_own, w_query, q_gain, *blocks],
        [shape_of((rows, q_width), jnp.bfloat16)],
        [
            pltpu.VMEM((fresh, rows, width), jnp.bfloat16),
            pltpu.VMEM((parts, rows, kv_width), jnp.bfloat16),
            pltpu.VMEM((parts * rows, 2 * rows), jnp.float32),
            pltpu.VMEM((q_width // LANES, rows, LANES), jnp.float32),
            pltpu.SemaphoreType.DMA((fresh,)),
        ],
        2 * rows * width * (q_width + fresh * kv_width) + 4 * rows * parts * rows * q_width,
        "attend",
        [early[0]],
        [shape_of((parts, rows, width), jnp.bfloat16)],
    )


def ffn_terms(gate, up, grad_hidden):
    sig = 1.0 / (1.0 + jnp.exp(-gate))
    swish = gate * sig
    hidden = (swish * up).astype(jnp.bfloat16)
    grad_gate = (grad_hidden * up * (sig * (1.0 + gate * (1.0 - sig)))).astype(jnp.bfloat16)
    grad_up = (grad_hidden * swish).astype(jnp.bfloat16)
    return hidden, grad_gate, grad_up


def valid_rows(values, start, length):
    pos = start + lax.broadcasted_iota(jnp.int32, (values.shape[0], 1), 0)
    return jnp.where(pos < length, values.astype(jnp.float32), 0.0).astype(jnp.bfloat16)


def ffn_body(
    sums,
    first,
    last,
    scalars,
    x_ref,
    att_ref,
    cot_ref,
    w_out_ref,
    gain_ref,
    gate_ref,
    up_ref,
    down_ref,
    *refs,
):
    if not first:
        before, refs = refs[:2], refs[2:]
    outs, (mid, inner, grad_low, out_acc, inner_acc) = refs[:-5], refs[-5:]
    step = pl.program_id(0)
    gain = gain_ref[...]
    rows = x_ref.shape[0]

    @pl.when(step == 0)
    def _():
        middle = x_ref[...].astype(jnp.float32) + bf16_dot(att_ref[...], w_out_ref[...], NN)
        mid[...] = middle
        inner[...] = (middle * inverse_root(middle) * gain).astype(jnp.bfloat16)
        grad_low[...] = valid_rows(cot_ref[...], scalars[0] * rows, scalars[1])
        out_acc[...] = middle if first else before[0][...]
        inner_acc[...] = jnp.zeros_like(inner_acc) if first else before[1][...]

    gate_w, up_w, down_w = gate_ref[...], up_ref[...], down_ref[...]
    hidden, grad_gate, grad_up = ffn_terms(
        bf16_dot(inner[...], gate_w, NN),
        bf16_dot(inner[...], up_w, NN),
        bf16_dot(grad_low[...], down_w, NT),
    )
    out_acc[...] += bf16_dot(hidden, down_w, NN)
    inner_acc[...] += bf16_dot(grad_gate, gate_w, NT) + bf16_dot(grad_up, up_w, NT)

    @pl.when(step == pl.num_programs(0) - 1)
    def _():
        if not last:
            outs[0][...] = out_acc[...]
            outs[1][...] = inner_acc[...]
            return
        result_ref, grad_mid_ref, sent_ref, gain_grad_ref = outs
        result_ref[...] = out_acc[...].astype(jnp.bfloat16)
        middle = mid[...]
        grad_inner = inner_acc[...]
        root = inverse_root(middle)
        scaled = grad_inner * gain
        mean = jnp.mean(scaled * middle, axis=-1, keepdims=True)
        grad_mid = (
            grad_low[...].astype(jnp.float32) + root * scaled - middle * (root * root * root * mean)
        )
        grad_mid_ref[...] = grad_mid
        gain_grad_ref[...] = jnp.sum(grad_inner * middle * root, axis=0, keepdims=True)
        branch = grad_mid.astype(jnp.bfloat16)
        grad_att = bf16_dot(branch, w_out_ref[...], NT)
        parts = sent_ref.shape[0]
        each = grad_mid.shape[1] // (parts * sums)
        lane = lane_of((rows, LANES))
        for part in range(parts):
            head_at = slice(part * LANES, (part + 1) * LANES)
            sent_ref[part, :, :LANES] = grad_att[:, head_at].astype(jnp.bfloat16)
            picked = jnp.zeros((rows, LANES), jnp.float32)
            for block in range(sums):
                start = (block * parts + part) * each
                chunk = grad_mid[:, start // LANES * LANES : start // LANES * LANES + LANES]
                turn = (block * each - start % LANES) % LANES
                moved = pltpu.roll(chunk, turn, axis=1) if turn else chunk
                picked = jnp.where(lane // each == block, moved, picked)
            sent_ref[part, :, LANES:] = picked.astype(jnp.bfloat16)


def ffn_part(scalars, own, weights, blocks, chunk, before, last, parts, sums):
    rows, width = own[0].shape
    low, high = blocks
    w_gate, w_up, w_down = weights
    inputs = [*own, *weights, *before]
    specs = [whole_spec(item.shape) for item in own] + [
        pl.BlockSpec((width, chunk), lambda i, s: (0, i + low)),
        pl.BlockSpec((width, chunk), lambda i, s: (0, i + low)),
        pl.BlockSpec((chunk, width), lambda i, s: (i + low, 0)),
    ]
    specs += [whole_spec(item.shape) for item in before]
    outs = [shape_of((rows, width), jnp.float32)] * 2
    if last:
        outs = [
            shape_of((rows, width), jnp.bfloat16),
            shape_of((rows, width), jnp.float32),
            shape_of((parts, rows, 2 * LANES), jnp.bfloat16),
            shape_of((1, width), jnp.float32),
        ]
    return pl.pallas_call(
        lambda *refs: ffn_body(sums, not before, last, *refs),
        grid_spec=pltpu.PrefetchScalarGridSpec(
            num_scalar_prefetch=1,
            grid=(high - low,),
            in_specs=specs,
            out_specs=[whole_spec(item.shape) for item in outs],
            scratch_shapes=[
                pltpu.VMEM((rows, width), jnp.float32),
                pltpu.VMEM((rows, width), jnp.bfloat16),
                pltpu.VMEM((rows, width), jnp.bfloat16),
                pltpu.VMEM((rows, width), jnp.float32),
                pltpu.VMEM((rows, width), jnp.float32),
            ],
        ),
        out_shape=outs,
        cost_estimate=pl.CostEstimate(
            flops=12 * rows * width * chunk * (high - low),
            bytes_accessed=6 * width * chunk * (high - low),
            transcendentals=0,
        ),
        compiler_params=pltpu.CompilerParams(vmem_limit_bytes=VMEM_LIMIT),
        name="ffn_part",
    )(scalars, *inputs)


def factor_loop(count, scalars, refs, inner_ref, grad_ref, gate_ref, up_ref, hidden_ref):
    x_ref, att_ref, cot_ref, w_out_ref, gain_ref, gate_up_ref, down_ref = refs
    x_all, att_all, cot_all = x_ref.ready(), att_ref.ready(), cot_ref.ready()
    w_out, gain, gate_up, down = w_out_ref[...], gain_ref[...], gate_up_ref[...], down_ref[...]
    rows, padded = x_ref.shape[1], down_ref.shape[0]

    def one_pair(pair, carry):
        at = pl.ds(pl.multiple_of(2 * pair * rows, 2 * rows), 2 * rows)
        both = pl.ds(2 * pair, 2)
        middle = x_all[both].reshape(2 * rows, -1).astype(jnp.float32)
        middle = middle + bf16_dot(att_all[both].reshape(2 * rows, -1), w_out, NN)
        inner = (middle * inverse_root(middle) * gain).astype(jnp.bfloat16)
        grad_low = jnp.concatenate(
            [
                valid_rows(cot_all[2 * pair + odd], scalars[2 * pair + odd] * rows, scalars[count])
                for odd in range(2)
            ],
            axis=0,
        )
        wide = bf16_dot(inner, gate_up, NN)
        grad_hidden = bf16_dot(grad_low, down, NT)
        hidden, grad_gate, grad_up = ffn_terms(wide[:, :padded], wide[:, padded:], grad_hidden)
        inner_ref[at, :], grad_ref[at, :], hidden_ref[at, :] = inner, grad_low, hidden
        gate_ref[at, :], up_ref[at, :] = grad_gate, grad_up
        return carry

    lax.fori_loop(0, count // 2, one_pair, 0)


def factor_body(count, scalars, *refs):
    factor_loop(count, scalars, refs[:7], *[ref.ref for ref in refs[7:]])


def factor_part(scalars, x_shards, att_shards, cot_shards, weights):
    rows, width = x_shards[0].shape
    columns = weights[-1].shape[0]
    count = len(x_shards)
    outs = [shape_of((count * rows, width), jnp.bfloat16)] * 2
    outs += [shape_of((count * rows, columns), jnp.bfloat16)] * 3
    return kernel_call(
        lambda *refs: factor_body(count, *refs),
        scalars,
        [Stack(x_shards), Stack(att_shards), Stack(cot_shards), *weights],
        outs,
        [],
        2 * count * rows * width * (width + 3 * columns),
        "factor_part",
    )


def cut_rows(kept_ref, given_ref, values, start, core):
    size = values.shape[0] // 4
    columns = slice(start, start + values.shape[1])
    for block in range(4):
        piece = values[block * size : (block + 1) * size]
        rows = slice(block // 2 * size, (block // 2 + 1) * size)

        @pl.when(core == block % 2)
        def _(piece=piece, rows=rows):
            kept_ref[rows, columns] = piece

        @pl.when(core != block % 2)
        def _(piece=piece, rows=rows):
            given_ref[rows, columns] = piece


def turned_product(rights, lefts, columns):
    total = None
    for right, left in zip(rights, lefts):
        term = bf16_dot(right, left, TN)
        total = term if total is None else total + term
    return total.T[:, :columns].astype(jnp.bfloat16)


def last_body(count, known, columns, scalars, *refs):
    left_ref, right_ref, kept_ref, given_ref, lefts, rights, found = refs[7:]
    core = scalars[count + 1]
    factor_loop(
        count, scalars, refs[:7], lefts.at[0], lefts.at[1], rights.at[0], rights.at[1], rights.at[2]
    )
    lefts_known, rights_known = left_ref.ready(), right_ref.ready()

    def product(index, carry):
        side = index // 2
        total = bf16_dot(rights[index], lefts[side], TN)
        for at in range(known):
            total = total + bf16_dot(rights_known[index * known + at], lefts_known[side * known + at], TN)
        found[index] = total.T.astype(jnp.bfloat16)
        return carry

    lax.fori_loop(0, 3, product, 0)
    for index in range(3):
        cut_rows(kept_ref, given_ref, found[index, :, :columns], index * columns, core)


def last_products(scalars, x_shards, att_shards, cot_shards, weights, before, columns):
    rows, width = x_shards[0].shape
    padded = weights[-1].shape[0]
    count = len(x_shards)
    total = 3 * columns + -3 * columns % LANES
    return kernel_call(
        lambda *refs: last_body(count, len(before), columns, *refs),
        scalars,
        [
            Stack(x_shards),
            Stack(att_shards),
            Stack(cot_shards),
            *weights,
            Stack([item[side] for side in (0, 1) for item in before]),
            Stack([item[side] for side in (2, 3, 4) for item in before]),
        ],
        [shape_of((width // 2, total), jnp.bfloat16)] * 2,
        [
            pltpu.VMEM((2, count * rows, width), jnp.bfloat16),
            pltpu.VMEM((3, count * rows, padded), jnp.bfloat16),
            pltpu.VMEM((3, width, padded), jnp.bfloat16),
        ],
        2 * count * rows * width * (width + 3 * padded) + 12 * count * rows * width * columns,
        "last_products",
    )


def head_body(head_dim, scalars, *refs):
    w_ref, q_gain_ref, k_gain_ref, freq_ref, base_ref, acts_ref, came_ref, low_ref, gains_ref = refs[:9]
    flat_q, flat_kv, cosines, sines, queries, keys, values, query_grad, key_grad, value_grad = refs[9:]
    parts, rows, width = acts_ref.shape
    count = parts * rows
    length = scalars[1]
    span = 2 * rows
    blocks = count // span
    q_gain, k_gain, freq, w = q_gain_ref[...], k_gain_ref[...], freq_ref[...], w_ref[...]
    acts, base = acts_ref.ready(), base_ref.ready()
    left = lane_of((span, LANES)) < head_dim

    def rows_of(block):
        return pl.ds(pl.multiple_of(block * span, span), span)

    def project(block, carry):
        at = rows_of(block)
        cosine, sine = turns(freq, base, [block * span, block * span + rows])
        flat = bf16_dot(acts[pl.ds(2 * block, 2)].reshape(span, width), w, NN)
        query, kv = flat[:, :LANES], flat[:, LANES:]
        flat_q[at, :], flat_kv[at, :], cosines[at, :], sines[at, :] = query, kv, cosine, sine
        queries[at, :] = (0.125 * head_turn(query, q_gain, cosine, sine, head_dim)).astype(jnp.bfloat16)
        turned = head_turn(kv, k_gain, cosine, sine, head_dim)
        keys[at, :] = jnp.where(left, turned, pltpu.roll(turned, head_dim, axis=1)).astype(jnp.bfloat16)
        values[at, :] = jnp.where(left, pltpu.roll(kv, head_dim, axis=1), kv).astype(jnp.bfloat16)
        key_grad[at, :] = jnp.zeros((span, LANES), jnp.float32)
        value_grad[at, :] = jnp.zeros((span, LANES), jnp.float32)
        return carry

    lax.fori_loop(0, blocks, project, 0)
    came = came_ref.ready()
    nothing = jnp.zeros((span, LANES), jnp.bfloat16)
    for block in range(blocks):
        extent = (block + 1) * span
        at = slice(block * span, extent)
        query_grad[...] = jnp.zeros_like(query_grad)

        def one_head(head, carry, extent=extent, at=at, block=block):
            key_pos = lax.broadcasted_iota(jnp.int32, (extent, span), 0)
            query_pos = block * span + lane_of((extent, span))
            counted = (key_pos <= query_pos) & (key_pos < length)
            mine = (lane_of((span, LANES)) // head_dim) == head
            query = jnp.where(mine, queries[at, :], nothing)
            grad = jnp.where(mine, came[2 * block : 2 * block + 2, :, :LANES].reshape(span, LANES), nothing)
            scores = jnp.where(counted, bf16_dot(keys[:extent, :], query, NT), MASKED)
            top = jnp.max(scores, axis=0, keepdims=True)
            weights = jnp.exp(scores - top)
            probs = weights * (1.0 / jnp.sum(weights, axis=0, keepdims=True))
            grad_probs = bf16_dot(values[:extent, :], grad, NT)
            delta = jnp.sum(probs * grad_probs, axis=0, keepdims=True)
            grad_scores = (probs * (grad_probs - delta)).astype(jnp.bfloat16)
            value_grad[:extent, :] += bf16_dot(probs.astype(jnp.bfloat16), grad, NN)
            key_grad[:extent, :] += bf16_dot(grad_scores, query, NN)
            own = (lane_of((extent, LANES)) // head_dim) == head
            key = jnp.where(own, keys[:extent, :], jnp.zeros((extent, LANES), jnp.bfloat16))
            query_grad[...] += bf16_dot(key, grad_scores, TN)
            return carry

        lax.fori_loop(0, 2, one_head, 0, unroll=2)
        sines_at, cosines_at = sines[at, :], cosines[at, :]
        low, q_part = head_turn_back(
            0.125 * query_grad[...].T, flat_q[at, :], q_gain, cosines_at, sines_at, head_dim
        )
        low_ref[2 * block : 2 * block + 2, :, :LANES] = low.astype(jnp.bfloat16).reshape(2, rows, LANES)
        gains_ref[0:1, :] = q_part if block == 0 else gains_ref[0:1, :] + q_part

    def finish(block, total):
        at = rows_of(block)
        key, value = key_grad[at, :], value_grad[at, :]
        key = key + pltpu.roll(key, head_dim, axis=1)
        value = value + pltpu.roll(value, head_dim, axis=1)
        low, part = head_turn_back(key, flat_kv[at, :], k_gain, cosines[at, :], sines[at, :], head_dim)
        both = jnp.where(left, low, value).astype(jnp.bfloat16).reshape(2, rows, LANES)
        low_ref.ref[pl.ds(2 * block, 2), :, LANES:] = both
        return total + part

    gains_ref[1:2, :] = lax.fori_loop(0, blocks, finish, jnp.zeros((1, LANES), jnp.float32))


def head_gradients(scalars, acts, w_head, q_gain, k_gain, freq, base, came, head_dim):
    parts, rows, width = acts.shape
    count = parts * rows
    return kernel_call(
        lambda *refs: head_body(head_dim, *refs),
        scalars,
        [w_head, q_gain, k_gain, freq, base, acts, came],
        [
            shape_of((parts, rows, 2 * LANES), jnp.bfloat16),
            shape_of((8, LANES), jnp.float32),
        ],
        [pltpu.VMEM((count, LANES), jnp.float32)] * 4
        + [pltpu.VMEM((count, LANES), jnp.bfloat16)] * 3
        + [pltpu.VMEM((LANES, 2 * rows), jnp.float32)]
        + [pltpu.VMEM((count, LANES), jnp.float32)] * 2,
        4 * count * width * LANES + 14 * count * count * head_dim,
        "head_gradients",
    )


def token_grad_body(head_dim, *refs):
    back_ref, wq_ref, wk_ref, wv_ref, x_ref, grad_mid_ref, gain_ref, out_ref = refs
    parts = back_ref.shape[0]
    back = back_ref.ready()
    left = lane_of((back.shape[1], LANES)) < head_dim
    keys, values = [], []
    for part in range(0, parts, 2):
        even = back[part, :, LANES:].astype(jnp.float32)
        odd = back[part + 1, :, LANES:].astype(jnp.float32)
        keys.append(jnp.where(left, even, pltpu.roll(odd, head_dim, axis=1)).astype(jnp.bfloat16))
        values.append(jnp.where(left, pltpu.roll(even, head_dim, axis=1), odd).astype(jnp.bfloat16))
    queries = [back[part, :, :LANES] for part in range(parts)]
    grad = (
        bf16_dot(jnp.concatenate(queries, axis=1), wq_ref[...], NT)
        + bf16_dot(jnp.concatenate(keys, axis=1), wk_ref[...], NT)
        + bf16_dot(jnp.concatenate(values, axis=1), wv_ref[...], NT)
    )
    values = x_ref[...].astype(jnp.float32)
    root = inverse_root(values)
    scaled = grad * gain_ref[...]
    mean = jnp.mean(scaled * values, axis=-1, keepdims=True)
    out_ref[...] = grad_mid_ref[...] + root * scaled - values * (root * root * root * mean)


def head_products_body(sources, head_dim, scalars, *refs):
    low_ref, acts_ref, w_ref, came_ref = refs[:4]
    att_refs, refs = refs[4 : 4 + sources], refs[4 + sources :]
    token_refs, refs = refs[:7], refs[7:]
    kept_ref, given_ref, out_kept_ref, out_given_ref, gain_ref, grad_tokens_ref = refs
    parts, rows, width = acts_ref.shape
    count = parts * rows
    core = scalars[sources]
    low = low_ref[...].reshape(count, 2 * LANES)
    turned = bf16_dot(low, acts_ref[...].reshape(count, width), TN).T
    cut_rows(kept_ref, given_ref, turned.astype(jnp.bfloat16), 0, core)
    gain_ref[...] = jnp.sum(turned * w_ref[...].astype(jnp.float32), axis=-1, keepdims=True)
    total = None
    came = came_ref.ready()
    for slot in range(sources):
        branch = came[scalars[slot], :, LANES:]
        term = bf16_dot(branch, att_refs[slot][...], TN)
        total = term if total is None else total + term
    cut_rows(out_kept_ref, out_given_ref, total.astype(jnp.bfloat16), 0, core)
    for ref in (kept_ref, given_ref, out_kept_ref, out_given_ref, gain_ref):
        ref.leave()
    token_grad_body(head_dim, *token_refs, grad_tokens_ref)


def head_products(scalars, low, acts, came, w_head, att_shards, token_inputs, head_dim):
    parts, rows, width = acts.shape
    out_width = att_shards[0].shape[1]
    return kernel_call(
        lambda *refs: head_products_body(len(att_shards), head_dim, *refs),
        scalars,
        [low, acts, w_head, came, *att_shards, *token_inputs],
        [
            shape_of((width // 2, 2 * LANES), jnp.bfloat16),
            shape_of((width // 2, 2 * LANES), jnp.bfloat16),
            shape_of((LANES // 2, out_width), jnp.bfloat16),
            shape_of((LANES // 2, out_width), jnp.bfloat16),
            shape_of((width, 1), jnp.float32),
            shape_of((rows, width), jnp.float32),
        ],
        [],
        6 * parts * rows * width * LANES + 4 * rows * width * width,
        "head_products",
    )


def spread_body(columns, count, scalars, came_ref, *outs):
    for part in range(came_ref.shape[0]):
        for index in range(count):
            piece = came_ref[part, :, index * columns : (index + 1) * columns].astype(jnp.float32)
            outs[index][:, part * columns : (part + 1) * columns] = piece


def spread_out(scalars, came, columns, count):
    parts, rows, width = came.shape
    outs = [shape_of((rows, parts * columns), jnp.float32)] * count
    return kernel_call(
        lambda *refs: spread_body(columns, count, *refs),
        scalars,
        [came],
        outs,
        [],
        0,
        "spread_out",
    )


def joined_body(parts, head_dim, scalars, *refs):
    came_refs, outs = refs[:parts], refs[parts:-2]
    joined, signals = refs[-2:]
    copies = [
        pltpu.make_async_copy(ref.ready(), joined.at[(scalars[0] + parts - at) % parts], signals.at[at])
        for at, ref in enumerate(came_refs)
    ]
    for copy in copies:
        copy.start()
    for copy in copies:
        copy.wait()
    query_ref, key_ref, value_ref, gain_ref = outs
    total = None
    for part in range(parts):
        piece = joined[part, :, : 2 * LANES].astype(jnp.float32)
        query_ref[:, part * LANES : (part + 1) * LANES] = piece[:, :LANES]
        at = slice(part * head_dim, (part + 1) * head_dim)
        key_ref[:, at] = piece[:, LANES : LANES + head_dim]
        value_ref[:, at] = piece[:, LANES + head_dim :]
        gain = joined[part, :, 2 * LANES :].astype(jnp.float32)
        total = gain if total is None else total + gain
    gain_ref[...] = total


def joined_out(scalars, came, head_dim):
    parts, (rows, width) = len(came), came[0].shape
    outs = [shape_of((rows, parts * size), jnp.float32) for size in (LANES, head_dim, head_dim)]
    outs.append(shape_of((rows, width - 2 * LANES), jnp.float32))
    return kernel_call(
        lambda *refs: joined_body(parts, head_dim, *refs),
        scalars,
        came,
        outs,
        [pltpu.VMEM((parts, rows, width), jnp.bfloat16), pltpu.SemaphoreType.DMA((parts,))],
        0,
        "joined_out",
    )


def cut_body(parts, scalars, mine_ref, got_ref, gain_ref, *refs):
    outs, (joined, signals) = refs[:parts], refs[parts:]
    each = joined.shape[1]
    width = mine_ref.shape[1]
    total = mine_ref[...].astype(jnp.float32) + got_ref[...].astype(jnp.float32)
    joined[:, :, :width] = total.astype(jnp.bfloat16).reshape(parts, each, width)
    for part in range(parts):
        joined[part, :, width:] = gain_ref[...]
    copies = [
        pltpu.make_async_copy(joined.at[(scalars[0] + at) % parts], out, signals.at[at])
        for at, out in enumerate(outs)
    ]
    for copy in copies:
        copy.start()
    for copy in copies:
        copy.wait()


def cut_blocks(scalars, mine, got, gains, parts):
    rows, width = mine.shape
    each = rows // parts
    total = width + gains.shape[1]
    outs = [shape_of((each, total), jnp.bfloat16)] * parts
    return kernel_call(
        lambda *refs: cut_body(parts, *refs),
        scalars,
        [mine, got, gains],
        [],
        [pltpu.VMEM((parts, each, total), jnp.bfloat16), pltpu.SemaphoreType.DMA((parts,))],
        0,
        "cut_blocks",
        (),
        outs,
    )


def swapped(value, axis, by):
    count = lax.axis_size(axis)
    return lax.ppermute(value, axis, [(i, i ^ by) for i in range(count)])


def after(value, *others):
    return lax.optimization_barrier((value, *others))[0]


def split_form(
    tokens,
    lengths,
    attn_gain,
    q_gain,
    k_gain,
    w_query,
    w_key,
    w_value,
    w_out,
    ffn_gain,
    w_gate,
    w_up,
    w_down,
    cotangent,
):
    _, rows, width = tokens.shape
    head_dim = q_gain.shape[0]
    hidden_width = w_gate.shape[1]
    parts = lax.axis_size("ctx")
    sums = lax.axis_size("dp")
    place = lax.axis_index("ctx").astype(jnp.int32)
    row = lax.axis_index("dp").astype(jnp.int32)
    core, line = row % 2, row // 2
    length = lengths[0]
    columns = hidden_width // parts
    each = width // (sums * parts)
    steps = parts // 2
    sources = [((place - 2 * (slot // 2)) % parts) ^ (slot % 2) for slot in range(parts)]
    freq = THETA ** (-(jnp.arange(head_dim // 2, dtype=jnp.float32) * 2.0 / head_dim))
    sign = jnp.ones_like(freq)
    freq = jnp.stack([jnp.concatenate([freq] * 4), jnp.concatenate([-sign, sign, -sign, sign])])
    base = jnp.arange(rows, dtype=jnp.float32)[:, None] * freq[0:1]
    base = jnp.stack([jnp.cos(base), jnp.sin(base)])
    attn_row, ffn_row = attn_gain[None], ffn_gain[None]
    q_row = jnp.concatenate([q_gain, q_gain])[None]
    k_row = jnp.concatenate([k_gain, k_gain])[None]
    x_own, cot_own = tokens[0], cotangent[0]

    def own_columns(weights, size, axis):
        return lax.dynamic_slice_in_dim(weights, place * size, size, axis)

    w_head = jnp.concatenate(
        [
            own_columns(w_query, LANES, 1),
            own_columns(w_key, head_dim, 1),
            own_columns(w_value, head_dim, 1),
        ],
        axis=-1,
    )
    spare = -columns % LANES
    wide = columns + spare
    gate_up = jnp.concatenate(
        [
            jnp.pad(own_columns(w_gate, columns, 1), ((0, 0), (0, spare))),
            jnp.pad(own_columns(w_up, columns, 1), ((0, 0), (0, spare))),
        ],
        axis=-1,
    )
    down = jnp.pad(own_columns(w_down, columns, 0), ((0, spare), (0, 0)))

    half = parts // 2
    kv_weights = [w_key, w_value, attn_row, k_row, freq, base]

    def key_values(low, high, held):
        return key_value_part(
            jnp.stack(sources[low:high]), x_shards[low:high], kv_weights, parts, head_dim, held
        )

    held, x_shards, early = x_own, [], None
    for step in range(steps):
        if step:
            held = from_behind(held, "ctx", 2)
        other = held
        if step == steps - 1:
            early = key_values(0, half, ())
            other = after(held, early[0], gate_up, down, w_head, x_shards[-1])
        x_shards += [held, swapped(other, "ctx", 1)]
    fresh = 2 if parts - 2 > half else parts - half
    if parts - fresh > half:
        early = key_values(half, parts - fresh, early)
    attn_low, acts = attend(
        jnp.stack(sources + [place, length]),
        x_shards[parts - fresh :],
        x_own,
        early,
        kv_weights,
        w_query,
        q_row,
        head_dim,
    )
    where = jnp.stack([place, length])

    def along(shard):
        return [shard] + [from_behind(shard, "ctx", 2 * step) for step in range(1, steps)]

    def across(shards):
        return [swapped(shard, "ctx", 1) for shard in shards]

    cot_ready = after(cot_own, *x_shards[-2:])
    cot_along = along(cot_ready)
    cot_across = across(cot_along[:1])
    attn_low = after(attn_low, *cot_along, *cot_across)
    att_along = along(attn_low)
    att_across = across(att_along[:1])
    cot_across += across([after(shard, attn_low) for shard in cot_along[1:]])
    chunk = next(c for c in (512, 384, 256, 128) if hidden_width % c == 0)
    turned_to = sources[0::2] + sources[1::2]
    slots = jnp.stack(turned_to + [core, length])
    weights = [w_out, ffn_row, gate_up, down]
    x_along, x_across = x_shards[0::2], x_shards[1::2]
    result, grad_mid, sent, ffn_gain_part = ffn_part(
        where,
        [x_own, attn_low, cot_own, w_out, ffn_row],
        [w_gate, w_up, w_down],
        (0, hidden_width // chunk),
        chunk,
        [],
        True,
        parts,
        sums,
    )
    sent = after(sent, *att_along[1:], *att_across, *cot_across[1:])
    came = lax.all_to_all(sent, "ctx", 0, 0, tiled=True)
    att_across += across([after(shard, sent) for shard in att_along[1:]])
    factors = [
        factor_part(
            jnp.stack(turned_to[:steps] + [length]),
            [after(x_along[0], sent)] + x_along[1:],
            att_along,
            cot_along,
            weights,
        )
    ]
    came = after(came, factors[0][0], *att_across[1:])
    low, head_gains = head_gradients(
        where, acts, w_head, q_row, k_row, freq, base, came, head_dim
    )
    back = lax.all_to_all(low, "ctx", 0, 0, tiled=True)
    def core_sum(kept, given):
        total = kept.astype(jnp.float32) + swapped(given, "dp", 1).astype(jnp.float32)
        return total.astype(jnp.bfloat16)

    def line_halves(half):
        size = half.shape[0] // 2
        mine = lax.dynamic_slice_in_dim(half, line * size, size, 0)
        return mine, lax.dynamic_slice_in_dim(half, (1 - line) * size, size, 0)

    def line_sum(half):
        mine, other = line_halves(half)
        return mine.astype(jnp.float32) + swapped(other, "dp", 2).astype(jnp.float32)

    kept, given = last_products(
        jnp.stack(turned_to[steps:] + [length, core]),
        [after(x_across[0], low)] + x_across[1:],
        att_across,
        cot_across,
        weights,
        factors,
        columns,
    )
    wide_half = core_sum(kept, after(given, back))
    wide_mine, wide_other = line_halves(wide_half)
    wide_got = swapped(wide_other, "dp", 2)
    head_kept, head_given, out_kept, out_given, attn_part, grad_tokens = head_products(
        slots,
        after(low, wide_other),
        acts,
        came,
        w_head,
        att_along + att_across,
        [back, w_query, w_key, w_value, x_own, grad_mid, attn_row],
        head_dim,
    )
    wide_sum = after(wide_mine, head_kept).astype(jnp.float32) + wide_got.astype(jnp.float32)
    wide_sum = wide_sum.astype(jnp.bfloat16).reshape(parts, each, -1)
    wide_came = lax.all_to_all(wide_sum, "ctx", 0, 0, tiled=True)
    head_half = core_sum(head_kept, after(head_given, wide_sum))
    out_half = core_sum(out_kept, after(out_given, wide_sum))
    gains = jnp.concatenate(
        [
            attn_part[:, 0] / attn_gain,
            ffn_gain_part[0],
            head_gains[0, :head_dim] + head_gains[0, head_dim:],
            head_gains[1, :head_dim],
        ]
    )
    gain_count = gains.shape[0]
    gains = after(gains, wide_sum)
    gains = gains + swapped(gains, "dp", 1)
    head_mine, head_other = line_halves(head_half)

    def high_low(values, columns_at):
        high = lax.reduce_precision(values, 8, 7)
        both = jnp.concatenate([high, values - high]).astype(jnp.bfloat16)
        room = -(-both.shape[0] // (16 * columns_at)) * 16
        return jnp.pad(both, (0, room * columns_at - both.shape[0])).reshape(room, columns_at)

    packed = jnp.concatenate([head_other, high_low(gains, head_other.shape[1])])
    got = swapped(packed, "dp", 2)
    head_got, gains_got = got[: head_other.shape[0]], got[head_other.shape[0] :].reshape(-1)
    gains = gains + gains_got[:gain_count].astype(jnp.float32)
    gains = gains + gains_got[gain_count : 2 * gain_count].astype(jnp.float32)
    out_sum = line_sum(out_half)
    pieces = high_low(gains, each * LANES // 32).reshape(-1)
    room = -(-pieces.shape[0] // (each * LANES)) * LANES
    pieces = jnp.pad(pieces, (0, each * room - pieces.shape[0])).reshape(each, room)
    leaving = cut_blocks(place[None], head_mine, head_got, pieces, parts)
    last = [leaving[0]] + [from_behind(leaving[at], "ctx", at) for at in range(1, parts)]
    query_out, key_out, value_out, totals = joined_out(place[None], last, head_dim)
    gate_sum, up_sum, down_out = spread_out(place[None], wide_came, columns, 3)
    totals = totals.reshape(-1)
    totals = totals[:gain_count] + totals[gain_count : 2 * gain_count]
    return (
        result[None],
        grad_tokens[None],
        totals[:width],
        totals[2 * width : 2 * width + head_dim],
        totals[2 * width + head_dim :],
        query_out,
        key_out,
        value_out,
        out_sum.T,
        totals[width : 2 * width],
        gate_sum,
        up_sum,
        down_out.T,
    )


def per_device(*arguments):
    tokens, q_gain, w_query, w_key = (arguments[i] for i in (0, 3, 5, 6))
    parts = lax.axis_size("ctx")
    sums = lax.axis_size("dp")
    head_dim = q_gain.shape[0]
    fits = (
        tokens.shape[0] == 1
        and sums == 4
        and parts % 2 == 0
        and 2 * head_dim == LANES
        and w_query.shape[1] == parts * LANES
        and w_key.shape[1] == parts * head_dim
        and tokens.shape[2] == sums * parts * 32
        and tokens.shape[1] == LANES
        and parts <= 8
    )
    return (split_form if fits else ring_form)(*arguments)


def solution(mesh):
    placed = (
        P("dp", "ctx", None),
        P("dp"),
        P(),
        P(),
        P(),
        P(),
        P(),
        P(),
        P(),
        P(),
        P(),
        P(),
        P(),
        P("dp", "ctx", None),
    )
    return jax.shard_map(
        per_device,
        mesh=mesh,
        in_specs=placed,
        out_specs=(
            P("dp", "ctx", None),
            P("dp", "ctx", None),
            P(),
            P(),
            P(),
            P(("dp", "ctx"), None),
            P(("dp", "ctx"), None),
            P(("dp", "ctx"), None),
            P(None, ("dp", "ctx")),
            P(),
            P(("dp", "ctx"), None),
            P(("dp", "ctx"), None),
            P(None, ("dp", "ctx")),
        ),
        check_vma=False,
    )
```

```python
import math

import jax
import jax.numpy as jnp
from jax import lax
from jax.experimental import pallas as pl
from jax.experimental.pallas import tpu as pltpu
from jax.sharding import PartitionSpec as P

EPS = 1e-05
THETA = 1000000.0
MASKED = -1e30


def passed_along(shard, axis, by):
    count = lax.axis_size(axis)
    pairs = [(i, i + by) for i in range(count) if 0 <= i + by < count]
    return lax.ppermute(shard, axis, pairs)


def from_behind(value, axis, steps):
    count = lax.axis_size(axis)
    pairs = [(source, (source + steps) % count) for source in range(count)]
    return lax.ppermute(value, axis, pairs)


def root_norm(values, gain):
    return values * lax.rsqrt(jnp.mean(values * values, axis=-1, keepdims=True) + EPS) * gain


def rotate(values, cosine, sine):
    half = values.shape[-1] // 2
    first_half = values[..., :half]
    second_half = values[..., half:]
    return jnp.concatenate(
        [first_half * cosine - second_half * sine, second_half * cosine + first_half * sine],
        axis=-1,
    )


def angles(positions, width):
    freqs = THETA ** (-(jnp.arange(width // 2, dtype=jnp.float32) * 2.0 / width))
    turned = positions.astype(jnp.float32)[:, None] * freqs[None, :]
    return (jnp.cos(turned), jnp.sin(turned))


def query_form(flat, gain, cosine, sine, groups):
    seq_count, row_count, width = flat.shape
    head_dim = gain.shape[0]
    normed = root_norm(flat.reshape(seq_count, row_count, width // head_dim, head_dim), gain)
    turned = rotate(normed, cosine, sine)
    return turned.reshape(seq_count, row_count, -1, groups, head_dim).transpose(0, 2, 3, 1, 4)


def key_form(flat, gain, cosine, sine):
    seq_count, row_count, width = flat.shape
    head_dim = gain.shape[0]
    normed = root_norm(flat.reshape(seq_count, row_count, width // head_dim, head_dim), gain)
    return rotate(normed, cosine, sine)


def ring_form(
    tokens,
    lengths,
    attn_gain,
    q_gain,
    k_gain,
    w_query,
    w_key,
    w_value,
    w_out,
    ffn_gain,
    w_gate,
    w_up,
    w_down,
    cotangent,
):
    seq_count, row_count, width = tokens.shape
    head_dim = q_gain.shape[0]
    heads = w_query.shape[1] // head_dim
    kv_heads = w_key.shape[1] // head_dim
    groups = heads // kv_heads
    loop_size = lax.axis_size("ctx")
    my_place = lax.axis_index("ctx")
    query_start = my_place * row_count
    query_pos = query_start + jnp.arange(row_count, dtype=jnp.int32)
    longest = jnp.max(lengths)
    cosine, sine = angles(query_pos, head_dim)
    cosine = cosine[None, :, None, :]
    sine = sine[None, :, None, :]
    inputs = tokens.astype(jnp.float32)
    acts = root_norm(inputs, attn_gain).astype(jnp.bfloat16).reshape(-1, width)
    qproj = jnp.dot(acts, w_query, preferred_element_type=jnp.float32).reshape(
        seq_count, row_count, -1
    )
    kproj = jnp.dot(acts, w_key, preferred_element_type=jnp.float32).reshape(
        seq_count, row_count, -1
    )
    vproj = jnp.dot(acts, w_value, preferred_element_type=jnp.float32)
    queries = query_form(qproj, q_gain, cosine, sine, groups).astype(jnp.bfloat16)
    keys = key_form(kproj, k_gain, cosine, sine).astype(jnp.bfloat16)
    values = vproj.astype(jnp.bfloat16).reshape(seq_count, row_count, kv_heads, head_dim)
    key_values = jnp.stack([keys, values])

    def block_mask(key_start, count):
        key_pos = key_start + jnp.arange(count, dtype=jnp.int32)
        causal = key_pos[None, None, :] <= query_pos[None, :, None]
        inside = key_pos[None, None, :] < lengths[:, None, None]
        return (causal & inside)[:, None, None, :, :]

    def needed(key_start):
        return (key_start < query_start + row_count) & (key_start < longest)

    def scores_of(key_piece):
        return 0.125 * jnp.einsum(
            "scgtd,sucd->scgtu", queries, key_piece, preferred_element_type=jnp.float32
        )

    def absorb(state, pair, key_start):

        def absorb_work(current):
            top_row, row_total, summed = current
            counted = block_mask(key_start, pair.shape[2])
            masked = jnp.where(counted, scores_of(pair[0]), MASKED)
            top_new = jnp.maximum(top_row, jnp.max(masked, axis=-1))
            weights = jnp.where(counted, jnp.exp(masked - top_new[..., None]), 0.0)
            factor = jnp.exp(top_row - top_new)
            row_total = row_total * factor + jnp.sum(weights, axis=-1)
            summed = summed * factor[..., None] + jnp.einsum(
                "scgtu,sucd->scgtd",
                weights.astype(jnp.bfloat16),
                pair[1],
                preferred_element_type=jnp.float32,
            )
            return (top_new, row_total, summed)

        return lax.cond(needed(key_start), absorb_work, lambda current: current, state)

    stat_shape = (seq_count, kv_heads, groups, row_count)
    start_state = (
        jnp.full(stat_shape, MASKED, jnp.float32),
        jnp.zeros(stat_shape, jnp.float32),
        jnp.zeros(stat_shape + (head_dim,), jnp.float32),
    )
    first_state = absorb(start_state, key_values, query_start)

    def forward_turn(step, carry):
        held, state = carry
        held = passed_along(held, "ctx", 1)
        source = (my_place - step) % loop_size
        return (held, absorb(state, held, source * row_count))

    _, (top_row, row_total, summed) = lax.fori_loop(
        1, loop_size, forward_turn, (key_values, first_state)
    )
    attended = summed / row_total[..., None]
    attn_low = attended.astype(jnp.bfloat16)
    out_heads = w_out.reshape(kv_heads, groups, head_dim, width)
    attn_branch = jnp.einsum(
        "scgtd,cgde->ste", attn_low, out_heads, preferred_element_type=jnp.float32
    )
    middle = inputs + attn_branch
    inner = root_norm(middle, ffn_gain).astype(jnp.bfloat16).reshape(-1, width)
    gate_proj = jnp.dot(inner, w_gate, preferred_element_type=jnp.float32)
    up_proj = jnp.dot(inner, w_up, preferred_element_type=jnp.float32)
    hidden = (jax.nn.silu(gate_proj) * up_proj).astype(jnp.bfloat16)
    output = middle + jnp.dot(hidden, w_down, preferred_element_type=jnp.float32).reshape(
        seq_count, row_count, width
    )
    result = output.astype(jnp.bfloat16)
    valid = (query_pos[None, :] < lengths[:, None]).astype(jnp.float32)
    grad_out = cotangent.astype(jnp.float32) * valid[..., None]
    grad_low = grad_out.astype(jnp.bfloat16).reshape(-1, width)
    down_turned = jnp.einsum("nd,nf->df", grad_low, hidden, preferred_element_type=jnp.float32)
    grad_hidden = jnp.einsum("nd,fd->nf", grad_low, w_down, preferred_element_type=jnp.float32)
    _, pull_gate = jax.vjp(lambda gate_in, up_in: jax.nn.silu(gate_in) * up_in, gate_proj, up_proj)
    grad_gate, grad_up = pull_gate(grad_hidden)
    gate_low = grad_gate.astype(jnp.bfloat16)
    up_low = grad_up.astype(jnp.bfloat16)
    gate_local = jnp.einsum("nd,nf->df", inner, gate_low, preferred_element_type=jnp.float32)
    up_local = jnp.einsum("nd,nf->df", inner, up_low, preferred_element_type=jnp.float32)
    grad_inner = jnp.einsum("nf,df->nd", gate_low, w_gate, preferred_element_type=jnp.float32)
    grad_inner = grad_inner + jnp.einsum(
        "nf,df->nd", up_low, w_up, preferred_element_type=jnp.float32
    )
    _, pull_second = jax.vjp(root_norm, middle, ffn_gain)
    grad_middle, ffn_local = pull_second(grad_inner.reshape(seq_count, row_count, width))
    grad_middle = grad_middle + grad_out
    branch_low = grad_middle.astype(jnp.bfloat16)
    out_turned = jnp.einsum(
        "std,scgte->dcge", branch_low, attn_low, preferred_element_type=jnp.float32
    ).reshape(width, -1)
    grad_attended = jnp.einsum(
        "ste,cgde->scgtd", branch_low, out_heads, preferred_element_type=jnp.float32
    ).astype(jnp.bfloat16)
    grad_wide = grad_attended.astype(jnp.float32)
    delta = jnp.sum(grad_wide * attended, axis=-1)
    grad_scaled = grad_wide / row_total[..., None]

    def block_back(pair, key_start):
        counted = block_mask(key_start, pair.shape[2])
        weights = jnp.where(counted, jnp.exp(scores_of(pair[0]) - top_row[..., None]), 0.0)
        probs = weights / row_total[..., None]
        grad_values = jnp.einsum(
            "scgtu,scgtd->sucd",
            weights.astype(jnp.bfloat16),
            grad_scaled,
            preferred_element_type=jnp.float32,
        )
        grad_probs = jnp.einsum(
            "scgtd,sucd->scgtu", grad_attended, pair[1], preferred_element_type=jnp.float32
        )
        grad_scores = (probs * (grad_probs - delta[..., None])).astype(jnp.bfloat16)
        more_queries = 0.125 * jnp.einsum(
            "scgtu,sucd->scgtd", grad_scores, pair[0], preferred_element_type=jnp.float32
        )
        grad_keys = 0.125 * jnp.einsum(
            "scgtu,scgtd->sucd", grad_scores, queries, preferred_element_type=jnp.float32
        )
        return (more_queries, jnp.stack([grad_keys, grad_values]))

    start_queries = jnp.zeros(stat_shape + (head_dim,), jnp.float32)

    def backward_turn(step, carry):
        held, held_grads, grad_queries = carry
        key_start = (my_place - step) % loop_size * row_count

        def backward_work(current):
            query_acc, pair_acc = current
            more_queries, more_pair = block_back(held, key_start)
            return (query_acc + more_queries, pair_acc + more_pair)

        grad_queries, held_grads = lax.cond(
            needed(key_start), backward_work, lambda current: current, (grad_queries, held_grads)
        )
        held = passed_along(held, "ctx", 1)
        held_grads = from_behind(held_grads.astype(jnp.bfloat16), "ctx", 1).astype(held_grads.dtype)
        return (held, held_grads, grad_queries)

    start_grads = jnp.zeros((2, seq_count, row_count, kv_heads, head_dim), jnp.float32)
    _, pair_grads, grad_queries = lax.fori_loop(
        0, loop_size, backward_turn, (key_values, start_grads, start_queries)
    )
    _, pull_query = jax.vjp(
        lambda proj_in, gain_in: query_form(proj_in, gain_in, cosine, sine, groups), qproj, q_gain
    )
    grad_qproj, q_local = pull_query(grad_queries)
    _, pull_key = jax.vjp(
        lambda proj_in, gain_in: key_form(proj_in, gain_in, cosine, sine), kproj, k_gain
    )
    grad_kproj, k_local = pull_key(pair_grads[0])
    query_low = grad_qproj.reshape(-1, heads * head_dim).astype(jnp.bfloat16)
    key_low = grad_kproj.reshape(-1, kv_heads * head_dim).astype(jnp.bfloat16)
    value_low = pair_grads[1].reshape(-1, kv_heads * head_dim).astype(jnp.bfloat16)
    query_local = jnp.einsum("nd,ne->de", acts, query_low, preferred_element_type=jnp.float32)
    key_local = jnp.einsum("nd,ne->de", acts, key_low, preferred_element_type=jnp.float32)
    value_local = jnp.einsum("nd,ne->de", acts, value_low, preferred_element_type=jnp.float32)
    grad_acts = jnp.einsum("ne,de->nd", query_low, w_query, preferred_element_type=jnp.float32)
    grad_acts = grad_acts + jnp.einsum(
        "ne,de->nd", key_low, w_key, preferred_element_type=jnp.float32
    )
    grad_acts = grad_acts + jnp.einsum(
        "ne,de->nd", value_low, w_value, preferred_element_type=jnp.float32
    )
    _, pull_first = jax.vjp(root_norm, inputs, attn_gain)
    grad_inputs, attn_local = pull_first(grad_acts.reshape(seq_count, row_count, width))
    grad_inputs = grad_inputs + grad_middle
    query_sum, key_sum, value_sum, out_sum, gate_sum, up_sum, down_sum = (
        lax.psum_scatter(query_local, ("dp", "ctx"), scatter_dimension=0, tiled=True),
        lax.psum_scatter(key_local, ("dp", "ctx"), scatter_dimension=0, tiled=True),
        lax.psum_scatter(value_local, ("dp", "ctx"), scatter_dimension=0, tiled=True),
        lax.psum_scatter(out_turned, ("dp", "ctx"), scatter_dimension=0, tiled=True),
        lax.psum_scatter(gate_local, ("dp", "ctx"), scatter_dimension=0, tiled=True),
        lax.psum_scatter(up_local, ("dp", "ctx"), scatter_dimension=0, tiled=True),
        lax.psum_scatter(down_turned, ("dp", "ctx"), scatter_dimension=0, tiled=True),
    )
    attn_sum, q_sum, k_sum, ffn_sum = lax.psum(
        (attn_local, q_local, k_local, ffn_local), ("dp", "ctx")
    )
    return (
        result,
        grad_inputs,
        attn_sum,
        q_sum,
        k_sum,
        query_sum,
        key_sum,
        value_sum,
        out_sum.T,
        ffn_sum,
        gate_sum,
        up_sum,
        down_sum.T,
    )


LANES = 128
VMEM_LIMIT = 60 << 20
NN = ((1,), (0,))
NT = ((1,), (1,))
TN = ((0,), (0,))


def bf16_dot(left, right, dims):
    return lax.dot_general(left, right, (dims, ((), ())), preferred_element_type=jnp.float32)


def inverse_root(values):
    return lax.rsqrt(jnp.mean(values * values, axis=-1, keepdims=True) + EPS)


def lane_of(shape):
    return lax.broadcasted_iota(jnp.int32, shape, len(shape) - 1)


def head_mean(values, head_dim):
    rows = lax.broadcasted_iota(jnp.int32, (LANES, LANES), 0) // head_dim
    columns = lane_of((LANES, LANES)) // head_dim
    spread = jnp.where(rows == columns, 1.0 / head_dim, 0.0).astype(jnp.bfloat16)
    return bf16_dot(values.astype(jnp.bfloat16), spread, NN)


def partner(values, head_dim):
    half = head_dim // 2
    first = lane_of(values.shape) % head_dim < half
    return jnp.where(
        first, pltpu.roll(values, LANES - half, axis=1), pltpu.roll(values, half, axis=1)
    )


def head_turn(flat, gain, cosine, sine, head_dim):
    normed = flat * lax.rsqrt(head_mean(flat * flat, head_dim) + EPS) * gain
    return normed * cosine + partner(normed, head_dim) * sine


def head_turn_back(grad, flat, gain, cosine, sine, head_dim):
    back = grad * cosine + partner(grad * sine, head_dim)
    root = lax.rsqrt(head_mean(flat * flat, head_dim) + EPS)
    scaled = gain * back
    mean = head_mean(scaled * flat, head_dim)
    return (
        root * scaled - flat * (root * root * root * mean),
        jnp.sum(back * flat * root, axis=0, keepdims=True),
    )


def turns(freq, base_ref, starts):
    base_cos, base_sin = base_ref[0], base_ref[1]
    cosines, sines = [], []
    for start in starts:
        angle = jnp.asarray(start, jnp.float32) * freq[0:1, :]
        cos, sin = jnp.cos(angle), jnp.sin(angle)
        cosines.append(base_cos * cos - base_sin * sin)
        sines.append((base_sin * cos + base_cos * sin) * freq[1:2, :])
    return jnp.concatenate(cosines, axis=0), jnp.concatenate(sines, axis=0)


def whole_spec(shape):
    return pl.BlockSpec(shape, lambda *_: (0,) * len(shape))


def cost_of(inputs, outs, flops):
    moved = sum(item.size * item.dtype.itemsize for item in (*inputs, *outs))
    return pl.CostEstimate(flops=flops, bytes_accessed=moved, transcendentals=0)


class Arriving:
    def __init__(self, sources, targets, signals, ref):
        self.copies = [pltpu.make_async_copy(*item) for item in zip(sources, targets, signals)]
        self.ref, self.shape = ref, ref.shape
        for copy in self.copies:
            copy.start()

    def ready(self):
        for copy in self.copies:
            copy.wait()
        self.copies = []
        return self.ref

    def __getitem__(self, at):
        return self.ready()[at]


class Leaving:
    def __init__(self, ref, target, signal):
        self.ref, self.target, self.signal, self.shape = ref, target, signal, ref.shape
        self.copy = None

    def __setitem__(self, at, value):
        self.ref[at] = value

    def __getitem__(self, at):
        return self.ref[at]

    def leave(self):
        if self.copy is None:
            self.copy = pltpu.make_async_copy(self.ref, self.target, self.signal)
            self.copy.start()


class Part:
    def __init__(self, array, index):
        self.array, self.index = array, index
        self.shape = array.shape if index is None else array.shape[1:]


class Stack:
    def __init__(self, arrays):
        self.parts = [item if isinstance(item, Part) else Part(item, None) for item in arrays]
        self.arrays, self.dtype = [item.array for item in self.parts], self.parts[0].array.dtype
        self.shape = (len(arrays),) + self.parts[0].shape
        self.size = len(arrays) * math.prod(self.parts[0].shape)

    def of(self, refs):
        return [ref if item.index is None else ref.at[item.index] for ref, item in zip(refs, self.parts)]


class Rows:
    def __init__(self, array, scalar, rows=0):
        self.array, self.scalar, self.rows = array, scalar, rows
        self.shape = (rows,) + array.shape[1:] if rows else array.shape[1:]
        self.dtype, self.size = array.dtype, array.size

    def of(self, ref, scalars):
        at = scalars[self.scalar]
        if not self.rows:
            return ref.at[at]
        return ref.at[pl.ds(pl.multiple_of(at * self.rows, self.rows), self.rows)]


def kernel_call(body, scalars, inputs, outs, scratch, flops, name, held=(), stacks=()):
    arrays = [item.arrays if isinstance(item, Stack) else [getattr(item, "array", item)] for item in inputs]
    count, kept = sum(map(len, arrays)), len(held)

    def run(scalars_ref, *refs):
        given, refs = refs[:count], refs[count + kept :]
        targets, refs = refs[: len(outs)], refs[len(outs) :]
        stack_refs, refs = refs[: len(stacks)], refs[len(stacks) :]
        buffers, refs = refs[: len(inputs)], refs[len(inputs) :]
        results, refs = refs[: len(outs)], refs[len(outs) :]
        signals, own = refs[0], refs[1:]
        arriving, used = [], 0
        for item, group, buffer in zip(inputs, arrays, buffers):
            sources = list(given[used : used + len(group)])
            places = [buffer.at[at] for at in range(len(group))] if isinstance(item, Stack) else [buffer]
            if isinstance(item, Rows):
                sources = [item.of(sources[0], scalars_ref)]
            if isinstance(item, Stack):
                sources = item.of(sources)
            slots = [signals.at[used + at] for at in range(len(group))]
            arriving.append(Arriving(sources, places, slots, buffer))
            used += len(group)
        leaving = [
            Leaving(result, target, signals.at[count + at])
            for at, (result, target) in enumerate(zip(results, targets))
        ]
        body(scalars_ref, *arriving, *leaving, *stack_refs, *own)
        for item in arriving:
            item.ready()
        for item in leaving:
            item.leave()
        for item in leaving:
            item.copy.wait()

    near = pl.BlockSpec(memory_space=pl.ANY)
    far = pl.BlockSpec(memory_space=pltpu.HBM)
    return pl.pallas_call(
        run,
        in_specs=[pl.BlockSpec(memory_space=pltpu.SMEM)] + [near] * count + [far] * kept,
        out_specs=[far] * (len(outs) + len(stacks)),
        out_shape=[*outs, *stacks],
        scratch_shapes=[pltpu.VMEM(item.shape, item.dtype) for item in (*inputs, *outs)]
        + [pltpu.SemaphoreType.DMA((count + len(outs),))]
        + list(scratch),
        input_output_aliases={1 + count + at: len(outs) + at for at in range(kept)},
        cost_estimate=cost_of(inputs, (*outs, *stacks), flops),
        compiler_params=pltpu.CompilerParams(vmem_limit_bytes=VMEM_LIMIT),
        name=name,
    )(scalars, *[array for group in arrays for array in group], *held)


def shape_of(shape, dtype):
    return jax.ShapeDtypeStruct(shape, dtype)


def stacked(values):
    return jnp.concatenate(
        [values[:, at : at + LANES] for at in range(0, values.shape[1], LANES)], axis=0
    )


def key_value_rows(scalars, shard_refs, wk_ref, wv_ref, gain_ref, k_gain_ref, freq, base_ref, acts, kv, head_dim):
    count, rows = len(shard_refs), shard_refs[0].shape[0]
    for at, ref in enumerate(shard_refs):
        values = ref[...].astype(jnp.float32)
        acts[at] = (values * inverse_root(values) * gain_ref[...]).astype(jnp.bfloat16)
    cosine, sine = turns(freq, base_ref, [scalars[at] * rows for at in range(count)])
    flat = acts[...].reshape(count * rows, -1)
    left = lane_of((count * rows, LANES)) < head_dim
    keys = bf16_dot(flat, wk_ref[...], NN)
    values = bf16_dot(flat, wv_ref[...], NN)
    for chunk in range(wk_ref.shape[1] // LANES):
        at = slice(chunk * LANES, (chunk + 1) * LANES)
        turned = head_turn(keys[:, at], k_gain_ref[...], cosine, sine, head_dim)
        value = values[:, at]
        for odd in range(2):
            pair = jnp.where(
                left,
                pltpu.roll(turned, head_dim, axis=1) if odd else turned,
                value if odd else pltpu.roll(value, head_dim, axis=1),
            )
            start = (2 * chunk + odd) * LANES
            kv[:, :, start : start + LANES] = pair.astype(jnp.bfloat16).reshape(count, rows, LANES)


def key_value_body(count, head_dim, scalars, *refs):
    shard_ref, wk_ref, wv_ref, gain_ref, k_gain_ref, freq_ref, base_ref = refs[:7]
    acts_out, kv_out, acts, kv, signals = refs[7:]
    shards, freq = shard_ref.ready(), freq_ref[...]
    for ref in (wk_ref, wv_ref, gain_ref, k_gain_ref, base_ref):
        ref.ready()

    def one_pair(pair, carry):
        both = pl.ds(2 * pair, 2)
        key_value_rows(
            [scalars[2 * pair], scalars[2 * pair + 1]],
            [shards.at[2 * pair], shards.at[2 * pair + 1]],
            wk_ref,
            wv_ref,
            gain_ref,
            k_gain_ref,
            freq,
            base_ref,
            acts.at[both],
            kv.at[both],
            head_dim,
        )
        return carry

    lax.fori_loop(0, count // 2, one_pair, 0)
    leaving = [
        pltpu.make_async_copy(buffer.at[at], out.at[scalars[at]], signals.at[2 * at + turn])
        for at in range(count)
        for turn, (buffer, out) in enumerate(((acts, acts_out), (kv, kv_out)))
    ]
    for copy in leaving:
        copy.start()
    for copy in leaving:
        copy.wait()


def key_value_part(scalars, shards, weights, parts, head_dim, held):
    rows, width = shards[0].shape
    kv_width = 2 * weights[0].shape[1]
    count = len(shards)
    return kernel_call(
        lambda *refs: key_value_body(count, head_dim, *refs),
        scalars,
        [Stack(shards), *weights],
        [],
        [
            pltpu.VMEM((count, rows, width), jnp.bfloat16),
            pltpu.VMEM((count, rows, kv_width), jnp.bfloat16),
            pltpu.SemaphoreType.DMA((2 * count,)),
        ],
        2 * count * rows * width * kv_width,
        "key_value_part",
        held,
        [
            shape_of((parts, rows, width), jnp.bfloat16),
            shape_of((parts, rows, kv_width), jnp.bfloat16),
        ],
    )


def attend_body(known, fresh, head_dim, scalars, *refs):
    shard_refs, refs = refs[:fresh], refs[fresh:]
    wk_ref, wv_ref, gain_ref, k_gain_ref, freq_ref, base_ref, x_ref, wq_ref, q_gain_ref = refs[:9]
    kv_refs, refs = refs[9 : 9 + known], refs[9 + known :]
    out_ref, acts_out, acts, kv, bias, turned, signals = refs
    place, length = scalars[known + fresh], scalars[known + fresh + 1]
    rows = x_ref.shape[0]
    count = (known + fresh) * rows
    chunks = wq_ref.shape[1] // LANES
    freq = freq_ref[...]
    key_value_rows(
        [scalars[known + at] for at in range(fresh)],
        shard_refs,
        wk_ref,
        wv_ref,
        gain_ref,
        k_gain_ref,
        freq,
        base_ref,
        acts,
        kv.at[pl.ds(known, fresh)],
        head_dim,
    )
    leaving = [
        pltpu.make_async_copy(acts.at[at], acts_out.at[scalars[known + at]], signals.at[at])
        for at in range(fresh)
    ]
    for copy in leaving:
        copy.start()
    values = x_ref[...].astype(jnp.float32)
    own = (values * inverse_root(values) * gain_ref[...]).astype(jnp.bfloat16)
    tables = turns(freq, base_ref, [place * rows])
    cosine, sine = (jnp.concatenate([table] * chunks, axis=0) for table in tables)
    flat = stacked(bf16_dot(own, wq_ref[...], NN))
    turned[...] = (0.125 * head_turn(flat, q_gain_ref[...], cosine, sine, head_dim)).reshape(
        chunks, rows, LANES
    )
    query_pos = place * rows + lane_of((rows, 2 * rows)) % rows
    for slot in range(known + fresh):
        key_pos = scalars[slot] * rows + lax.broadcasted_iota(jnp.int32, (rows, 2 * rows), 0)
        bias[slot * rows : (slot + 1) * rows, :] = jnp.where(
            (key_pos <= query_pos) & (key_pos < length), 0.0, MASKED
        )
        if slot < known:
            kv[slot] = kv_refs[slot][...]
    left = lane_of((rows, LANES)) < head_dim

    def one_head(index, carry):
        at = pl.ds(pl.multiple_of(index * LANES, LANES), LANES)
        mine = turned[index]
        both = jnp.concatenate(
            [jnp.where(left, mine, 0.0), jnp.where(left, pltpu.roll(mine, head_dim, axis=1), 0.0)],
            axis=0,
        ).astype(jnp.bfloat16)
        head_kv = kv[:, :, at].reshape(count, LANES)
        scores = bf16_dot(head_kv, both, NT) + bias[...]
        top = jnp.max(scores, axis=0, keepdims=True)
        weights = jnp.exp(scores - top)
        total = jnp.sum(weights, axis=0, keepdims=True)
        summed = bf16_dot(head_kv, weights.astype(jnp.bfloat16), TN)[head_dim:] / total
        heads = jnp.concatenate([summed[:, :rows], summed[:, rows:]], axis=0)
        out_ref[:, at] = heads.T.astype(jnp.bfloat16)
        return carry

    lax.fori_loop(0, chunks, one_head, 0)
    for copy in leaving:
        copy.wait()


def attend(scalars, shards, x_own, early, weights, w_query, q_gain, head_dim):
    parts, rows, width = early[0].shape
    q_width, kv_width = w_query.shape[1], 2 * weights[0].shape[1]
    fresh = len(shards)
    known = parts - fresh
    blocks = [Rows(early[1], at) for at in range(known)]
    return kernel_call(
        lambda *refs: attend_body(known, fresh, head_dim, *refs),
        scalars,
        [*shards, *weights, x_own, w_query, q_gain, *blocks],
        [shape_of((rows, q_width), jnp.bfloat16)],
        [
            pltpu.VMEM((fresh, rows, width), jnp.bfloat16),
            pltpu.VMEM((parts, rows, kv_width), jnp.bfloat16),
            pltpu.VMEM((parts * rows, 2 * rows), jnp.float32),
            pltpu.VMEM((q_width // LANES, rows, LANES), jnp.float32),
            pltpu.SemaphoreType.DMA((fresh,)),
        ],
        2 * rows * width * (q_width + fresh * kv_width) + 4 * rows * parts * rows * q_width,
        "attend",
        [early[0]],
        [shape_of((parts, rows, width), jnp.bfloat16)],
    )


def ffn_terms(gate, up, grad_hidden):
    sig = 1.0 / (1.0 + jnp.exp(-gate))
    swish = gate * sig
    hidden = (swish * up).astype(jnp.bfloat16)
    grad_gate = (grad_hidden * up * (sig * (1.0 + gate * (1.0 - sig)))).astype(jnp.bfloat16)
    grad_up = (grad_hidden * swish).astype(jnp.bfloat16)
    return hidden, grad_gate, grad_up


def valid_rows(values, start, length):
    pos = start + lax.broadcasted_iota(jnp.int32, (values.shape[0], 1), 0)
    return jnp.where(pos < length, values.astype(jnp.float32), 0.0).astype(jnp.bfloat16)


def ffn_body(
    sums,
    first,
    last,
    scalars,
    x_ref,
    att_ref,
    cot_ref,
    w_out_ref,
    gain_ref,
    gate_ref,
    up_ref,
    down_ref,
    *refs,
):
    if not first:
        before, refs = refs[:2], refs[2:]
    outs, (mid, inner, grad_low, out_acc, inner_acc) = refs[:-5], refs[-5:]
    step = pl.program_id(0)
    gain = gain_ref[...]
    rows = x_ref.shape[0]

    @pl.when(step == 0)
    def _():
        middle = x_ref[...].astype(jnp.float32) + bf16_dot(att_ref[...], w_out_ref[...], NN)
        mid[...] = middle
        inner[...] = (middle * inverse_root(middle) * gain).astype(jnp.bfloat16)
        grad_low[...] = valid_rows(cot_ref[...], scalars[0] * rows, scalars[1])
        out_acc[...] = middle if first else before[0][...]
        inner_acc[...] = jnp.zeros_like(inner_acc) if first else before[1][...]

    gate_w, up_w, down_w = gate_ref[...], up_ref[...], down_ref[...]
    hidden, grad_gate, grad_up = ffn_terms(
        bf16_dot(inner[...], gate_w, NN),
        bf16_dot(inner[...], up_w, NN),
        bf16_dot(grad_low[...], down_w, NT),
    )
    out_acc[...] += bf16_dot(hidden, down_w, NN)
    inner_acc[...] += bf16_dot(grad_gate, gate_w, NT) + bf16_dot(grad_up, up_w, NT)

    @pl.when(step == pl.num_programs(0) - 1)
    def _():
        if not last:
            outs[0][...] = out_acc[...]
            outs[1][...] = inner_acc[...]
            return
        result_ref, grad_mid_ref, sent_ref, gain_grad_ref = outs
        result_ref[...] = out_acc[...].astype(jnp.bfloat16)
        middle = mid[...]
        grad_inner = inner_acc[...]
        root = inverse_root(middle)
        scaled = grad_inner * gain
        mean = jnp.mean(scaled * middle, axis=-1, keepdims=True)
        grad_mid = (
            grad_low[...].astype(jnp.float32) + root * scaled - middle * (root * root * root * mean)
        )
        grad_mid_ref[...] = grad_mid
        gain_grad_ref[...] = jnp.sum(grad_inner * middle * root, axis=0, keepdims=True)
        branch = grad_mid.astype(jnp.bfloat16)
        grad_att = bf16_dot(branch, w_out_ref[...], NT)
        parts = sent_ref.shape[0]
        each = grad_mid.shape[1] // (parts * sums)
        lane = lane_of((rows, LANES))
        for part in range(parts):
            head_at = slice(part * LANES, (part + 1) * LANES)
            sent_ref[part, :, :LANES] = grad_att[:, head_at].astype(jnp.bfloat16)
            picked = jnp.zeros((rows, LANES), jnp.float32)
            for block in range(sums):
                start = (block * parts + part) * each
                chunk = grad_mid[:, start // LANES * LANES : start // LANES * LANES + LANES]
                turn = (block * each - start % LANES) % LANES
                moved = pltpu.roll(chunk, turn, axis=1) if turn else chunk
                picked = jnp.where(lane // each == block, moved, picked)
            sent_ref[part, :, LANES:] = picked.astype(jnp.bfloat16)


def ffn_part(scalars, own, weights, blocks, chunk, before, last, parts, sums):
    rows, width = own[0].shape
    low, high = blocks
    w_gate, w_up, w_down = weights
    inputs = [*own, *weights, *before]
    specs = [whole_spec(item.shape) for item in own] + [
        pl.BlockSpec((width, chunk), lambda i, s: (0, i + low)),
        pl.BlockSpec((width, chunk), lambda i, s: (0, i + low)),
        pl.BlockSpec((chunk, width), lambda i, s: (i + low, 0)),
    ]
    specs += [whole_spec(item.shape) for item in before]
    outs = [shape_of((rows, width), jnp.float32)] * 2
    if last:
        outs = [
            shape_of((rows, width), jnp.bfloat16),
            shape_of((rows, width), jnp.float32),
            shape_of((parts, rows, 2 * LANES), jnp.bfloat16),
            shape_of((1, width), jnp.float32),
        ]
    return pl.pallas_call(
        lambda *refs: ffn_body(sums, not before, last, *refs),
        grid_spec=pltpu.PrefetchScalarGridSpec(
            num_scalar_prefetch=1,
            grid=(high - low,),
            in_specs=specs,
            out_specs=[whole_spec(item.shape) for item in outs],
            scratch_shapes=[
                pltpu.VMEM((rows, width), jnp.float32),
                pltpu.VMEM((rows, width), jnp.bfloat16),
                pltpu.VMEM((rows, width), jnp.bfloat16),
                pltpu.VMEM((rows, width), jnp.float32),
                pltpu.VMEM((rows, width), jnp.float32),
            ],
        ),
        out_shape=outs,
        cost_estimate=pl.CostEstimate(
            flops=12 * rows * width * chunk * (high - low),
            bytes_accessed=6 * width * chunk * (high - low),
            transcendentals=0,
        ),
        compiler_params=pltpu.CompilerParams(vmem_limit_bytes=VMEM_LIMIT),
        name="ffn_part",
    )(scalars, *inputs)


def factor_loop(count, scalars, refs, inner_ref, grad_ref, gate_ref, up_ref, hidden_ref):
    x_ref, att_ref, cot_ref, w_out_ref, gain_ref, gate_up_ref, down_ref = refs
    x_all, att_all, cot_all = x_ref.ready(), att_ref.ready(), cot_ref.ready()
    w_out, gain, gate_up, down = w_out_ref[...], gain_ref[...], gate_up_ref[...], down_ref[...]
    rows, padded = x_ref.shape[1], down_ref.shape[0]

    def one_pair(pair, carry):
        at = pl.ds(pl.multiple_of(2 * pair * rows, 2 * rows), 2 * rows)
        both = pl.ds(2 * pair, 2)
        middle = x_all[both].reshape(2 * rows, -1).astype(jnp.float32)
        middle = middle + bf16_dot(att_all[both].reshape(2 * rows, -1), w_out, NN)
        inner = (middle * inverse_root(middle) * gain).astype(jnp.bfloat16)
        grad_low = jnp.concatenate(
            [
                valid_rows(cot_all[2 * pair + odd], scalars[2 * pair + odd] * rows, scalars[count])
                for odd in range(2)
            ],
            axis=0,
        )
        wide = bf16_dot(inner, gate_up, NN)
        grad_hidden = bf16_dot(grad_low, down, NT)
        hidden, grad_gate, grad_up = ffn_terms(wide[:, :padded], wide[:, padded:], grad_hidden)
        inner_ref[at, :], grad_ref[at, :], hidden_ref[at, :] = inner, grad_low, hidden
        gate_ref[at, :], up_ref[at, :] = grad_gate, grad_up
        return carry

    lax.fori_loop(0, count // 2, one_pair, 0)


def factor_body(count, scalars, *refs):
    factor_loop(count, scalars, refs[:7], *[ref.ref for ref in refs[7:]])


def factor_part(scalars, x_shards, att_shards, cot_shards, weights):
    rows, width = x_shards[0].shape
    columns = weights[-1].shape[0]
    count = len(x_shards)
    outs = [shape_of((count * rows, width), jnp.bfloat16)] * 2
    outs += [shape_of((count * rows, columns), jnp.bfloat16)] * 3
    return kernel_call(
        lambda *refs: factor_body(count, *refs),
        scalars,
        [Stack(x_shards), Stack(att_shards), Stack(cot_shards), *weights],
        outs,
        [],
        2 * count * rows * width * (width + 3 * columns),
        "factor_part",
    )


def cut_copies(whole, kept_out, given_out, core, signals):
    size = whole.shape[0] // 4
    copies = []
    for index, (out, bit) in enumerate(((kept_out, core), (given_out, 1 - core))):
        for half in range(2):
            start = pl.multiple_of((2 * half + bit) * size, size)
            copies.append(
                pltpu.make_async_copy(
                    whole.at[pl.ds(start, size)],
                    out.at[pl.ds(half * size, size)],
                    signals.at[2 * index + half],
                )
            )
    for copy in copies:
        copy.start()
    return copies


def last_body(count, known, columns, scalars, *refs):
    left_ref, right_ref, kept_out, given_out, lefts, rights, found, whole, signals = refs[7:]
    core = scalars[count + 1]
    factor_loop(
        count, scalars, refs[:7], lefts.at[0], lefts.at[1], rights.at[0], rights.at[1], rights.at[2]
    )
    lefts_known, rights_known = left_ref.ready(), right_ref.ready()

    def product(index, carry):
        side = index // 2
        total = bf16_dot(rights[index], lefts[side], TN)
        for at in range(known):
            total = total + bf16_dot(rights_known[index * known + at], lefts_known[side * known + at], TN)
        found[index] = total.T.astype(jnp.bfloat16)
        return carry

    lax.fori_loop(0, 3, product, 0)
    for index in range(3):
        whole[:, index * columns : (index + 1) * columns] = found[index, :, :columns]
    for copy in cut_copies(whole, kept_out, given_out, core, signals):
        copy.wait()


def last_products(scalars, x_shards, att_shards, cot_shards, weights, before, columns):
    rows, width = x_shards[0].shape
    padded = weights[-1].shape[0]
    count = len(x_shards)
    total = 3 * columns + -3 * columns % LANES
    return kernel_call(
        lambda *refs: last_body(count, len(before), columns, *refs),
        scalars,
        [
            Stack(x_shards),
            Stack(att_shards),
            Stack(cot_shards),
            *weights,
            Stack([item[side] for side in (0, 1) for item in before]),
            Stack([item[side] for side in (2, 3, 4) for item in before]),
        ],
        [],
        [
            pltpu.VMEM((2, count * rows, width), jnp.bfloat16),
            pltpu.VMEM((3, count * rows, padded), jnp.bfloat16),
            pltpu.VMEM((3, width, padded), jnp.bfloat16),
            pltpu.VMEM((width, total), jnp.bfloat16),
            pltpu.SemaphoreType.DMA((4,)),
        ],
        2 * count * rows * width * (width + 3 * padded) + 12 * count * rows * width * columns,
        "last_products",
        (),
        [shape_of((width // 2, total), jnp.bfloat16)] * 2,
    )


def head_body(head_dim, scalars, *refs):
    w_ref, q_gain_ref, k_gain_ref, freq_ref, base_ref, acts_ref, came_ref, low_ref, gains_ref = refs[:9]
    flat_q, flat_kv, cosines, sines, queries, keys, values, query_grad, key_grad, value_grad = refs[9:]
    parts, rows, width = acts_ref.shape
    count = parts * rows
    length = scalars[1]
    span = 2 * rows
    blocks = count // span
    q_gain, k_gain, freq, w = q_gain_ref[...], k_gain_ref[...], freq_ref[...], w_ref[...]
    acts, base = acts_ref.ready(), base_ref.ready()
    left = lane_of((span, LANES)) < head_dim

    def rows_of(block):
        return pl.ds(pl.multiple_of(block * span, span), span)

    def project(block, carry):
        at = rows_of(block)
        cosine, sine = turns(freq, base, [block * span, block * span + rows])
        flat = bf16_dot(acts[pl.ds(2 * block, 2)].reshape(span, width), w, NN)
        query, kv = flat[:, :LANES], flat[:, LANES:]
        flat_q[at, :], flat_kv[at, :], cosines[at, :], sines[at, :] = query, kv, cosine, sine
        queries[at, :] = (0.125 * head_turn(query, q_gain, cosine, sine, head_dim)).astype(jnp.bfloat16)
        turned = head_turn(kv, k_gain, cosine, sine, head_dim)
        keys[at, :] = jnp.where(left, turned, pltpu.roll(turned, head_dim, axis=1)).astype(jnp.bfloat16)
        values[at, :] = jnp.where(left, pltpu.roll(kv, head_dim, axis=1), kv).astype(jnp.bfloat16)
        key_grad[at, :] = jnp.zeros((span, LANES), jnp.float32)
        value_grad[at, :] = jnp.zeros((span, LANES), jnp.float32)
        return carry

    lax.fori_loop(0, blocks, project, 0)
    came = came_ref.ready()
    nothing = jnp.zeros((span, LANES), jnp.bfloat16)
    for block in range(blocks):
        extent = (block + 1) * span
        at = slice(block * span, extent)
        query_grad[...] = jnp.zeros_like(query_grad)

        def one_head(head, carry, extent=extent, at=at, block=block):
            key_pos = lax.broadcasted_iota(jnp.int32, (extent, span), 0)
            query_pos = block * span + lane_of((extent, span))
            counted = (key_pos <= query_pos) & (key_pos < length)
            mine = (lane_of((span, LANES)) // head_dim) == head
            query = jnp.where(mine, queries[at, :], nothing)
            grad = jnp.where(mine, came[2 * block : 2 * block + 2, :, :LANES].reshape(span, LANES), nothing)
            scores = jnp.where(counted, bf16_dot(keys[:extent, :], query, NT), MASKED)
            top = jnp.max(scores, axis=0, keepdims=True)
            weights = jnp.exp(scores - top)
            probs = weights * (1.0 / jnp.sum(weights, axis=0, keepdims=True))
            grad_probs = bf16_dot(values[:extent, :], grad, NT)
            delta = jnp.sum(probs * grad_probs, axis=0, keepdims=True)
            grad_scores = (probs * (grad_probs - delta)).astype(jnp.bfloat16)
            value_grad[:extent, :] += bf16_dot(probs.astype(jnp.bfloat16), grad, NN)
            key_grad[:extent, :] += bf16_dot(grad_scores, query, NN)
            own = (lane_of((extent, LANES)) // head_dim) == head
            key = jnp.where(own, keys[:extent, :], jnp.zeros((extent, LANES), jnp.bfloat16))
            query_grad[...] += bf16_dot(key, grad_scores, TN)
            return carry

        lax.fori_loop(0, 2, one_head, 0, unroll=2)
        sines_at, cosines_at = sines[at, :], cosines[at, :]
        low, q_part = head_turn_back(
            0.125 * query_grad[...].T, flat_q[at, :], q_gain, cosines_at, sines_at, head_dim
        )
        low_ref[2 * block : 2 * block + 2, :, :LANES] = low.astype(jnp.bfloat16).reshape(2, rows, LANES)
        gains_ref[0:1, :] = q_part if block == 0 else gains_ref[0:1, :] + q_part

    def finish(block, total):
        at = rows_of(block)
        key, value = key_grad[at, :], value_grad[at, :]
        key = key + pltpu.roll(key, head_dim, axis=1)
        value = value + pltpu.roll(value, head_dim, axis=1)
        low, part = head_turn_back(key, flat_kv[at, :], k_gain, cosines[at, :], sines[at, :], head_dim)
        both = jnp.where(left, low, value).astype(jnp.bfloat16).reshape(2, rows, LANES)
        low_ref.ref[pl.ds(2 * block, 2), :, LANES:] = both
        return total + part

    gains_ref[1:2, :] = lax.fori_loop(0, blocks, finish, jnp.zeros((1, LANES), jnp.float32))


def head_gradients(scalars, acts, w_head, q_gain, k_gain, freq, base, came, head_dim):
    parts, rows, width = acts.shape
    count = parts * rows
    return kernel_call(
        lambda *refs: head_body(head_dim, *refs),
        scalars,
        [w_head, q_gain, k_gain, freq, base, acts, came],
        [
            shape_of((parts, rows, 2 * LANES), jnp.bfloat16),
            shape_of((8, LANES), jnp.float32),
        ],
        [pltpu.VMEM((count, LANES), jnp.float32)] * 4
        + [pltpu.VMEM((count, LANES), jnp.bfloat16)] * 3
        + [pltpu.VMEM((LANES, 2 * rows), jnp.float32)]
        + [pltpu.VMEM((count, LANES), jnp.float32)] * 2,
        4 * count * width * LANES + 14 * count * count * head_dim,
        "head_gradients",
    )


def token_grad_body(head_dim, *refs):
    back_ref, wq_ref, wk_ref, wv_ref, x_ref, grad_mid_ref, gain_ref, out_ref = refs
    parts = back_ref.shape[0]
    back = back_ref.ready()
    left = lane_of((back.shape[1], LANES)) < head_dim
    keys, values = [], []
    for part in range(0, parts, 2):
        even = back[part, :, LANES:].astype(jnp.float32)
        odd = back[part + 1, :, LANES:].astype(jnp.float32)
        keys.append(jnp.where(left, even, pltpu.roll(odd, head_dim, axis=1)).astype(jnp.bfloat16))
        values.append(jnp.where(left, pltpu.roll(even, head_dim, axis=1), odd).astype(jnp.bfloat16))
    queries = [back[part, :, :LANES] for part in range(parts)]
    grad = (
        bf16_dot(jnp.concatenate(queries, axis=1), wq_ref[...], NT)
        + bf16_dot(jnp.concatenate(keys, axis=1), wk_ref[...], NT)
        + bf16_dot(jnp.concatenate(values, axis=1), wv_ref[...], NT)
    )
    values = x_ref[...].astype(jnp.float32)
    root = inverse_root(values)
    scaled = grad * gain_ref[...]
    mean = jnp.mean(scaled * values, axis=-1, keepdims=True)
    out_ref[...] = grad_mid_ref[...] + root * scaled - values * (root * root * root * mean)


def head_products_body(sources, head_dim, scalars, *refs):
    low_ref, acts_ref, w_ref, came_ref = refs[:4]
    att_ref, refs = refs[4], refs[5:]
    token_refs, refs = refs[:7], refs[7:]
    gain_ref, grad_tokens_ref, kept_out, given_out, out_kept, out_given, proj, outer, signals = refs
    parts, rows, width = acts_ref.shape
    count = parts * rows
    core = scalars[sources]
    low = low_ref[...].reshape(count, 2 * LANES)
    turned = bf16_dot(low, acts_ref[...].reshape(count, width), TN).T
    proj[...] = turned.astype(jnp.bfloat16)
    copies = cut_copies(proj, kept_out, given_out, core, signals.at[pl.ds(0, 4)])
    gain_ref[...] = jnp.sum(turned * w_ref[...].astype(jnp.float32), axis=-1, keepdims=True)
    total = None
    came = came_ref.ready()
    for slot in range(sources):
        branch = came[scalars[slot], :, LANES:]
        term = bf16_dot(branch, att_ref[slot], TN)
        total = term if total is None else total + term
    outer[...] = total.astype(jnp.bfloat16)
    copies += cut_copies(outer, out_kept, out_given, core, signals.at[pl.ds(4, 4)])
    token_grad_body(head_dim, *token_refs, grad_tokens_ref)
    for copy in copies:
        copy.wait()


def head_products(scalars, low, acts, came, w_head, att_shards, token_inputs, head_dim):
    parts, rows, width = acts.shape
    out_width = att_shards[0].shape[1]
    return kernel_call(
        lambda *refs: head_products_body(len(att_shards), head_dim, *refs),
        scalars,
        [low, acts, w_head, came, Stack(att_shards), *token_inputs],
        [
            shape_of((width, 1), jnp.float32),
            shape_of((rows, width), jnp.float32),
        ],
        [
            pltpu.VMEM((width, 2 * LANES), jnp.bfloat16),
            pltpu.VMEM((LANES, out_width), jnp.bfloat16),
            pltpu.SemaphoreType.DMA((8,)),
        ],
        6 * parts * rows * width * LANES + 4 * rows * width * width,
        "head_products",
        (),
        [shape_of((width // 2, 2 * LANES), jnp.bfloat16)] * 2
        + [shape_of((LANES // 2, out_width), jnp.bfloat16)] * 2,
    )


def spread_body(columns, count, scalars, came_ref, *outs):
    for part in range(came_ref.shape[0]):
        for index in range(count):
            piece = came_ref[part, :, index * columns : (index + 1) * columns].astype(jnp.float32)
            outs[index][:, part * columns : (part + 1) * columns] = piece


def spread_out(scalars, came, columns, count):
    parts, rows, width = came.shape
    outs = [shape_of((rows, parts * columns), jnp.float32)] * count
    return kernel_call(
        lambda *refs: spread_body(columns, count, *refs),
        scalars,
        [came],
        outs,
        [],
        0,
        "spread_out",
    )


def joined_body(parts, head_dim, scalars, *refs):
    came_refs, outs = refs[:parts], refs[parts:-2]
    joined, signals = refs[-2:]
    copies = [
        pltpu.make_async_copy(ref.ready(), joined.at[(scalars[0] + parts - at) % parts], signals.at[at])
        for at, ref in enumerate(came_refs)
    ]
    for copy in copies:
        copy.start()
    for copy in copies:
        copy.wait()
    query_ref, key_ref, value_ref, gain_ref = outs
    total = None
    for part in range(parts):
        piece = joined[part, :, : 2 * LANES].astype(jnp.float32)
        query_ref[:, part * LANES : (part + 1) * LANES] = piece[:, :LANES]
        at = slice(part * head_dim, (part + 1) * head_dim)
        key_ref[:, at] = piece[:, LANES : LANES + head_dim]
        value_ref[:, at] = piece[:, LANES + head_dim :]
        gain = joined[part, :, 2 * LANES :].astype(jnp.float32)
        total = gain if total is None else total + gain
    gain_ref[...] = total


def joined_out(scalars, came, head_dim):
    parts, (rows, width) = len(came), came[0].shape
    outs = [shape_of((rows, parts * size), jnp.float32) for size in (LANES, head_dim, head_dim)]
    outs.append(shape_of((rows, width - 2 * LANES), jnp.float32))
    return kernel_call(
        lambda *refs: joined_body(parts, head_dim, *refs),
        scalars,
        came,
        outs,
        [pltpu.VMEM((parts, rows, width), jnp.bfloat16), pltpu.SemaphoreType.DMA((parts,))],
        0,
        "joined_out",
    )


def cut_body(parts, scalars, mine_ref, got_ref, gain_ref, *refs):
    outs, (joined, signals) = refs[:parts], refs[parts:]
    each = joined.shape[1]
    width = mine_ref.shape[1]
    total = mine_ref[...].astype(jnp.float32) + got_ref[...].astype(jnp.float32)
    joined[:, :, :width] = total.astype(jnp.bfloat16).reshape(parts, each, width)
    for part in range(parts):
        joined[part, :, width:] = gain_ref[...]
    copies = [
        pltpu.make_async_copy(joined.at[(scalars[0] + at) % parts], out, signals.at[at])
        for at, out in enumerate(outs)
    ]
    for copy in copies:
        copy.start()
    for copy in copies:
        copy.wait()


def cut_blocks(scalars, mine, got, gains, parts):
    rows, width = mine.shape
    each = rows // parts
    total = width + gains.shape[1]
    outs = [shape_of((each, total), jnp.bfloat16)] * parts
    return kernel_call(
        lambda *refs: cut_body(parts, *refs),
        scalars,
        [mine, got, gains],
        [],
        [pltpu.VMEM((parts, each, total), jnp.bfloat16), pltpu.SemaphoreType.DMA((parts,))],
        0,
        "cut_blocks",
        (),
        outs,
    )


def swapped(value, axis, by):
    count = lax.axis_size(axis)
    return lax.ppermute(value, axis, [(i, i ^ by) for i in range(count)])


def after(value, *others):
    return lax.optimization_barrier((value, *others))[0]


def split_form(
    tokens,
    lengths,
    attn_gain,
    q_gain,
    k_gain,
    w_query,
    w_key,
    w_value,
    w_out,
    ffn_gain,
    w_gate,
    w_up,
    w_down,
    cotangent,
):
    _, rows, width = tokens.shape
    head_dim = q_gain.shape[0]
    hidden_width = w_gate.shape[1]
    parts = lax.axis_size("ctx")
    sums = lax.axis_size("dp")
    place = lax.axis_index("ctx").astype(jnp.int32)
    row = lax.axis_index("dp").astype(jnp.int32)
    core, line = row % 2, row // 2
    length = lengths[0]
    columns = hidden_width // parts
    each = width // (sums * parts)
    steps = parts // 2
    sources = [((place - 2 * (slot // 2)) % parts) ^ (slot % 2) for slot in range(parts)]
    freq = THETA ** (-(jnp.arange(head_dim // 2, dtype=jnp.float32) * 2.0 / head_dim))
    sign = jnp.ones_like(freq)
    freq = jnp.stack([jnp.concatenate([freq] * 4), jnp.concatenate([-sign, sign, -sign, sign])])
    base = jnp.arange(rows, dtype=jnp.float32)[:, None] * freq[0:1]
    base = jnp.stack([jnp.cos(base), jnp.sin(base)])
    attn_row, ffn_row = attn_gain[None], ffn_gain[None]
    q_row = jnp.concatenate([q_gain, q_gain])[None]
    k_row = jnp.concatenate([k_gain, k_gain])[None]
    x_own, cot_own = tokens[0], cotangent[0]

    def own_columns(weights, size, axis):
        return lax.dynamic_slice_in_dim(weights, place * size, size, axis)

    w_head = jnp.concatenate(
        [
            own_columns(w_query, LANES, 1),
            own_columns(w_key, head_dim, 1),
            own_columns(w_value, head_dim, 1),
        ],
        axis=-1,
    )
    spare = -columns % LANES
    wide = columns + spare
    gate_up = jnp.concatenate(
        [
            jnp.pad(own_columns(w_gate, columns, 1), ((0, 0), (0, spare))),
            jnp.pad(own_columns(w_up, columns, 1), ((0, 0), (0, spare))),
        ],
        axis=-1,
    )
    down = jnp.pad(own_columns(w_down, columns, 0), ((0, spare), (0, 0)))

    half = parts // 2
    kv_weights = [w_key, w_value, attn_row, k_row, freq, base]

    def key_values(low, high, held):
        return key_value_part(
            jnp.stack(sources[low:high]), x_shards[low:high], kv_weights, parts, head_dim, held
        )

    held, x_shards, early = x_own, [], None
    for step in range(steps):
        if step:
            held = from_behind(held, "ctx", 2)
        other = held
        if step == steps - 1:
            early = key_values(0, half, ())
            other = after(held, early[0], gate_up, down, w_head, x_shards[-1])
        x_shards += [held, swapped(other, "ctx", 1)]
    fresh = 2 if parts - 2 > half else parts - half
    if parts - fresh > half:
        early = key_values(half, parts - fresh, early)
    attn_low, acts = attend(
        jnp.stack(sources + [place, length]),
        x_shards[parts - fresh :],
        x_own,
        early,
        kv_weights,
        w_query,
        q_row,
        head_dim,
    )
    where = jnp.stack([place, length])

    def along(shard):
        return [shard] + [from_behind(shard, "ctx", 2 * step) for step in range(1, steps)]

    def across(shards):
        if len(shards) == 1:
            return [swapped(shards[0], "ctx", 1)]
        joined = swapped(jnp.stack(shards), "ctx", 1)
        return [Part(joined, at) for at in range(len(shards))]

    def arrays_of(shards):
        return [shard.array if isinstance(shard, Part) else shard for shard in shards]

    cot_ready = after(cot_own, *x_shards[-2:])
    cot_along = along(cot_ready)
    cot_across = across(cot_along[:1])
    attn_low = after(attn_low, *cot_along, *cot_across)
    att_along = along(attn_low)
    att_across = across(att_along[:1])
    cot_across += across([after(shard, attn_low) for shard in cot_along[1:]])
    chunk = next(c for c in (512, 384, 256, 128) if hidden_width % c == 0)
    turned_to = sources[0::2] + sources[1::2]
    slots = jnp.stack(turned_to + [core, length])
    weights = [w_out, ffn_row, gate_up, down]
    x_along, x_across = x_shards[0::2], x_shards[1::2]
    result, grad_mid, sent, ffn_gain_part = ffn_part(
        where,
        [x_own, attn_low, cot_own, w_out, ffn_row],
        [w_gate, w_up, w_down],
        (0, hidden_width // chunk),
        chunk,
        [],
        True,
        parts,
        sums,
    )
    sent = after(sent, *att_along[1:], *att_across, *arrays_of(cot_across[1:2]))
    came = lax.all_to_all(sent, "ctx", 0, 0, tiled=True)
    att_across += across([after(shard, sent) for shard in att_along[1:]])
    factors = [
        factor_part(
            jnp.stack(turned_to[:steps] + [length]),
            [after(x_along[0], sent)] + x_along[1:],
            att_along,
            cot_along,
            weights,
        )
    ]
    came = after(came, factors[0][0], *arrays_of(att_across[1:2]))
    low, head_gains = head_gradients(
        where, acts, w_head, q_row, k_row, freq, base, came, head_dim
    )
    back = lax.all_to_all(low, "ctx", 0, 0, tiled=True)
    def core_sum(kept, given):
        total = kept.astype(jnp.float32) + swapped(given, "dp", 1).astype(jnp.float32)
        return total.astype(jnp.bfloat16)

    def line_halves(half):
        size = half.shape[0] // 2
        mine = lax.dynamic_slice_in_dim(half, line * size, size, 0)
        return mine, lax.dynamic_slice_in_dim(half, (1 - line) * size, size, 0)

    def line_sum(half):
        mine, other = line_halves(half)
        return mine.astype(jnp.float32) + swapped(other, "dp", 2).astype(jnp.float32)

    kept, given = last_products(
        jnp.stack(turned_to[steps:] + [length, core]),
        [after(x_across[0], low)] + x_across[1:],
        att_across,
        cot_across,
        weights,
        factors,
        columns,
    )
    wide_half = core_sum(kept, after(given, back))
    wide_mine, wide_other = line_halves(wide_half)
    wide_got = swapped(wide_other, "dp", 2)
    attn_part, grad_tokens, head_kept, head_given, out_kept, out_given = head_products(
        slots,
        after(low, wide_other),
        acts,
        came,
        w_head,
        att_along + att_across,
        [back, w_query, w_key, w_value, x_own, grad_mid, attn_row],
        head_dim,
    )
    wide_sum = after(wide_mine, head_kept).astype(jnp.float32) + wide_got.astype(jnp.float32)
    wide_sum = wide_sum.astype(jnp.bfloat16).reshape(parts, each, -1)
    wide_came = lax.all_to_all(wide_sum, "ctx", 0, 0, tiled=True)
    head_half = core_sum(head_kept, after(head_given, wide_sum))
    out_half = core_sum(out_kept, after(out_given, wide_sum))
    gains = jnp.concatenate(
        [
            attn_part[:, 0] / attn_gain,
            ffn_gain_part[0],
            head_gains[0, :head_dim] + head_gains[0, head_dim:],
            head_gains[1, :head_dim],
        ]
    )
    gain_count = gains.shape[0]
    gains = after(gains, wide_sum)
    gains = gains + swapped(gains, "dp", 1)
    head_mine, head_other = line_halves(head_half)

    def high_low(values, columns_at):
        high = lax.reduce_precision(values, 8, 7)
        both = jnp.concatenate([high, values - high]).astype(jnp.bfloat16)
        room = -(-both.shape[0] // (16 * columns_at)) * 16
        return jnp.pad(both, (0, room * columns_at - both.shape[0])).reshape(room, columns_at)

    packed = jnp.concatenate([head_other, high_low(gains, head_other.shape[1])])
    got = swapped(packed, "dp", 2)
    head_got, gains_got = got[: head_other.shape[0]], got[head_other.shape[0] :].reshape(-1)
    gains = gains + gains_got[:gain_count].astype(jnp.float32)
    gains = gains + gains_got[gain_count : 2 * gain_count].astype(jnp.float32)
    out_sum = line_sum(out_half)
    pieces = high_low(gains, each * LANES // 32).reshape(-1)
    room = -(-pieces.shape[0] // (each * LANES)) * LANES
    pieces = jnp.pad(pieces, (0, each * room - pieces.shape[0])).reshape(each, room)
    leaving = cut_blocks(place[None], head_mine, head_got, pieces, parts)
    last = [leaving[0]] + [from_behind(leaving[at], "ctx", at) for at in range(1, parts)]
    query_out, key_out, value_out, totals = joined_out(place[None], last, head_dim)
    gate_sum, up_sum, down_out = spread_out(place[None], wide_came, columns, 3)
    totals = totals.reshape(-1)
    totals = totals[:gain_count] + totals[gain_count : 2 * gain_count]
    return (
        result[None],
        grad_tokens[None],
        totals[:width],
        totals[2 * width : 2 * width + head_dim],
        totals[2 * width + head_dim :],
        query_out,
        key_out,
        value_out,
        out_sum.T,
        totals[width : 2 * width],
        gate_sum,
        up_sum,
        down_out.T,
    )


def per_device(*arguments):
    tokens, q_gain, w_query, w_key = (arguments[i] for i in (0, 3, 5, 6))
    parts = lax.axis_size("ctx")
    sums = lax.axis_size("dp")
    head_dim = q_gain.shape[0]
    fits = (
        tokens.shape[0] == 1
        and sums == 4
        and parts % 2 == 0
        and 2 * head_dim == LANES
        and w_query.shape[1] == parts * LANES
        and w_key.shape[1] == parts * head_dim
        and tokens.shape[2] == sums * parts * 32
        and tokens.shape[1] == LANES
        and parts <= 8
    )
    return (split_form if fits else ring_form)(*arguments)


def solution(mesh):
    placed = (
        P("dp", "ctx", None),
        P("dp"),
        P(),
        P(),
        P(),
        P(),
        P(),
        P(),
        P(),
        P(),
        P(),
        P(),
        P(),
        P("dp", "ctx", None),
    )
    return jax.shard_map(
        per_device,
        mesh=mesh,
        in_specs=placed,
        out_specs=(
            P("dp", "ctx", None),
            P("dp", "ctx", None),
            P(),
            P(),
            P(),
            P(("dp", "ctx"), None),
            P(("dp", "ctx"), None),
            P(("dp", "ctx"), None),
            P(None, ("dp", "ctx")),
            P(),
            P(("dp", "ctx"), None),
            P(("dp", "ctx"), None),
            P(None, ("dp", "ctx")),
        ),
        check_vma=False,
    )
```

```python
import math

import jax
import jax.numpy as jnp
from jax import lax
from jax.experimental import pallas as pl
from jax.experimental.pallas import tpu as pltpu
from jax.sharding import PartitionSpec as P

EPS = 1e-05
THETA = 1000000.0
MASKED = -1e30


def passed_along(shard, axis, by):
    count = lax.axis_size(axis)
    pairs = [(i, i + by) for i in range(count) if 0 <= i + by < count]
    return lax.ppermute(shard, axis, pairs)


def from_behind(value, axis, steps):
    count = lax.axis_size(axis)
    pairs = [(source, (source + steps) % count) for source in range(count)]
    return lax.ppermute(value, axis, pairs)


def root_norm(values, gain):
    return values * lax.rsqrt(jnp.mean(values * values, axis=-1, keepdims=True) + EPS) * gain


def rotate(values, cosine, sine):
    half = values.shape[-1] // 2
    first_half = values[..., :half]
    second_half = values[..., half:]
    return jnp.concatenate(
        [first_half * cosine - second_half * sine, second_half * cosine + first_half * sine],
        axis=-1,
    )


def angles(positions, width):
    freqs = THETA ** (-(jnp.arange(width // 2, dtype=jnp.float32) * 2.0 / width))
    turned = positions.astype(jnp.float32)[:, None] * freqs[None, :]
    return (jnp.cos(turned), jnp.sin(turned))


def query_form(flat, gain, cosine, sine, groups):
    seq_count, row_count, width = flat.shape
    head_dim = gain.shape[0]
    normed = root_norm(flat.reshape(seq_count, row_count, width // head_dim, head_dim), gain)
    turned = rotate(normed, cosine, sine)
    return turned.reshape(seq_count, row_count, -1, groups, head_dim).transpose(0, 2, 3, 1, 4)


def key_form(flat, gain, cosine, sine):
    seq_count, row_count, width = flat.shape
    head_dim = gain.shape[0]
    normed = root_norm(flat.reshape(seq_count, row_count, width // head_dim, head_dim), gain)
    return rotate(normed, cosine, sine)


def ring_form(
    tokens,
    lengths,
    attn_gain,
    q_gain,
    k_gain,
    w_query,
    w_key,
    w_value,
    w_out,
    ffn_gain,
    w_gate,
    w_up,
    w_down,
    cotangent,
):
    seq_count, row_count, width = tokens.shape
    head_dim = q_gain.shape[0]
    heads = w_query.shape[1] // head_dim
    kv_heads = w_key.shape[1] // head_dim
    groups = heads // kv_heads
    loop_size = lax.axis_size("ctx")
    my_place = lax.axis_index("ctx")
    query_start = my_place * row_count
    query_pos = query_start + jnp.arange(row_count, dtype=jnp.int32)
    longest = jnp.max(lengths)
    cosine, sine = angles(query_pos, head_dim)
    cosine = cosine[None, :, None, :]
    sine = sine[None, :, None, :]
    inputs = tokens.astype(jnp.float32)
    acts = root_norm(inputs, attn_gain).astype(jnp.bfloat16).reshape(-1, width)
    qproj = jnp.dot(acts, w_query, preferred_element_type=jnp.float32).reshape(
        seq_count, row_count, -1
    )
    kproj = jnp.dot(acts, w_key, preferred_element_type=jnp.float32).reshape(
        seq_count, row_count, -1
    )
    vproj = jnp.dot(acts, w_value, preferred_element_type=jnp.float32)
    queries = query_form(qproj, q_gain, cosine, sine, groups).astype(jnp.bfloat16)
    keys = key_form(kproj, k_gain, cosine, sine).astype(jnp.bfloat16)
    values = vproj.astype(jnp.bfloat16).reshape(seq_count, row_count, kv_heads, head_dim)
    key_values = jnp.stack([keys, values])

    def block_mask(key_start, count):
        key_pos = key_start + jnp.arange(count, dtype=jnp.int32)
        causal = key_pos[None, None, :] <= query_pos[None, :, None]
        inside = key_pos[None, None, :] < lengths[:, None, None]
        return (causal & inside)[:, None, None, :, :]

    def needed(key_start):
        return (key_start < query_start + row_count) & (key_start < longest)

    def scores_of(key_piece):
        return 0.125 * jnp.einsum(
            "scgtd,sucd->scgtu", queries, key_piece, preferred_element_type=jnp.float32
        )

    def absorb(state, pair, key_start):

        def absorb_work(current):
            top_row, row_total, summed = current
            counted = block_mask(key_start, pair.shape[2])
            masked = jnp.where(counted, scores_of(pair[0]), MASKED)
            top_new = jnp.maximum(top_row, jnp.max(masked, axis=-1))
            weights = jnp.where(counted, jnp.exp(masked - top_new[..., None]), 0.0)
            factor = jnp.exp(top_row - top_new)
            row_total = row_total * factor + jnp.sum(weights, axis=-1)
            summed = summed * factor[..., None] + jnp.einsum(
                "scgtu,sucd->scgtd",
                weights.astype(jnp.bfloat16),
                pair[1],
                preferred_element_type=jnp.float32,
            )
            return (top_new, row_total, summed)

        return lax.cond(needed(key_start), absorb_work, lambda current: current, state)

    stat_shape = (seq_count, kv_heads, groups, row_count)
    start_state = (
        jnp.full(stat_shape, MASKED, jnp.float32),
        jnp.zeros(stat_shape, jnp.float32),
        jnp.zeros(stat_shape + (head_dim,), jnp.float32),
    )
    first_state = absorb(start_state, key_values, query_start)

    def forward_turn(step, carry):
        held, state = carry
        held = passed_along(held, "ctx", 1)
        source = (my_place - step) % loop_size
        return (held, absorb(state, held, source * row_count))

    _, (top_row, row_total, summed) = lax.fori_loop(
        1, loop_size, forward_turn, (key_values, first_state)
    )
    attended = summed / row_total[..., None]
    attn_low = attended.astype(jnp.bfloat16)
    out_heads = w_out.reshape(kv_heads, groups, head_dim, width)
    attn_branch = jnp.einsum(
        "scgtd,cgde->ste", attn_low, out_heads, preferred_element_type=jnp.float32
    )
    middle = inputs + attn_branch
    inner = root_norm(middle, ffn_gain).astype(jnp.bfloat16).reshape(-1, width)
    gate_proj = jnp.dot(inner, w_gate, preferred_element_type=jnp.float32)
    up_proj = jnp.dot(inner, w_up, preferred_element_type=jnp.float32)
    hidden = (jax.nn.silu(gate_proj) * up_proj).astype(jnp.bfloat16)
    output = middle + jnp.dot(hidden, w_down, preferred_element_type=jnp.float32).reshape(
        seq_count, row_count, width
    )
    result = output.astype(jnp.bfloat16)
    valid = (query_pos[None, :] < lengths[:, None]).astype(jnp.float32)
    grad_out = cotangent.astype(jnp.float32) * valid[..., None]
    grad_low = grad_out.astype(jnp.bfloat16).reshape(-1, width)
    down_turned = jnp.einsum("nd,nf->df", grad_low, hidden, preferred_element_type=jnp.float32)
    grad_hidden = jnp.einsum("nd,fd->nf", grad_low, w_down, preferred_element_type=jnp.float32)
    _, pull_gate = jax.vjp(lambda gate_in, up_in: jax.nn.silu(gate_in) * up_in, gate_proj, up_proj)
    grad_gate, grad_up = pull_gate(grad_hidden)
    gate_low = grad_gate.astype(jnp.bfloat16)
    up_low = grad_up.astype(jnp.bfloat16)
    gate_local = jnp.einsum("nd,nf->df", inner, gate_low, preferred_element_type=jnp.float32)
    up_local = jnp.einsum("nd,nf->df", inner, up_low, preferred_element_type=jnp.float32)
    grad_inner = jnp.einsum("nf,df->nd", gate_low, w_gate, preferred_element_type=jnp.float32)
    grad_inner = grad_inner + jnp.einsum(
        "nf,df->nd", up_low, w_up, preferred_element_type=jnp.float32
    )
    _, pull_second = jax.vjp(root_norm, middle, ffn_gain)
    grad_middle, ffn_local = pull_second(grad_inner.reshape(seq_count, row_count, width))
    grad_middle = grad_middle + grad_out
    branch_low = grad_middle.astype(jnp.bfloat16)
    out_turned = jnp.einsum(
        "std,scgte->dcge", branch_low, attn_low, preferred_element_type=jnp.float32
    ).reshape(width, -1)
    grad_attended = jnp.einsum(
        "ste,cgde->scgtd", branch_low, out_heads, preferred_element_type=jnp.float32
    ).astype(jnp.bfloat16)
    grad_wide = grad_attended.astype(jnp.float32)
    delta = jnp.sum(grad_wide * attended, axis=-1)
    grad_scaled = grad_wide / row_total[..., None]

    def block_back(pair, key_start):
        counted = block_mask(key_start, pair.shape[2])
        weights = jnp.where(counted, jnp.exp(scores_of(pair[0]) - top_row[..., None]), 0.0)
        probs = weights / row_total[..., None]
        grad_values = jnp.einsum(
            "scgtu,scgtd->sucd",
            weights.astype(jnp.bfloat16),
            grad_scaled,
            preferred_element_type=jnp.float32,
        )
        grad_probs = jnp.einsum(
            "scgtd,sucd->scgtu", grad_attended, pair[1], preferred_element_type=jnp.float32
        )
        grad_scores = (probs * (grad_probs - delta[..., None])).astype(jnp.bfloat16)
        more_queries = 0.125 * jnp.einsum(
            "scgtu,sucd->scgtd", grad_scores, pair[0], preferred_element_type=jnp.float32
        )
        grad_keys = 0.125 * jnp.einsum(
            "scgtu,scgtd->sucd", grad_scores, queries, preferred_element_type=jnp.float32
        )
        return (more_queries, jnp.stack([grad_keys, grad_values]))

    start_queries = jnp.zeros(stat_shape + (head_dim,), jnp.float32)

    def backward_turn(step, carry):
        held, held_grads, grad_queries = carry
        key_start = (my_place - step) % loop_size * row_count

        def backward_work(current):
            query_acc, pair_acc = current
            more_queries, more_pair = block_back(held, key_start)
            return (query_acc + more_queries, pair_acc + more_pair)

        grad_queries, held_grads = lax.cond(
            needed(key_start), backward_work, lambda current: current, (grad_queries, held_grads)
        )
        held = passed_along(held, "ctx", 1)
        held_grads = from_behind(held_grads.astype(jnp.bfloat16), "ctx", 1).astype(held_grads.dtype)
        return (held, held_grads, grad_queries)

    start_grads = jnp.zeros((2, seq_count, row_count, kv_heads, head_dim), jnp.float32)
    _, pair_grads, grad_queries = lax.fori_loop(
        0, loop_size, backward_turn, (key_values, start_grads, start_queries)
    )
    _, pull_query = jax.vjp(
        lambda proj_in, gain_in: query_form(proj_in, gain_in, cosine, sine, groups), qproj, q_gain
    )
    grad_qproj, q_local = pull_query(grad_queries)
    _, pull_key = jax.vjp(
        lambda proj_in, gain_in: key_form(proj_in, gain_in, cosine, sine), kproj, k_gain
    )
    grad_kproj, k_local = pull_key(pair_grads[0])
    query_low = grad_qproj.reshape(-1, heads * head_dim).astype(jnp.bfloat16)
    key_low = grad_kproj.reshape(-1, kv_heads * head_dim).astype(jnp.bfloat16)
    value_low = pair_grads[1].reshape(-1, kv_heads * head_dim).astype(jnp.bfloat16)
    query_local = jnp.einsum("nd,ne->de", acts, query_low, preferred_element_type=jnp.float32)
    key_local = jnp.einsum("nd,ne->de", acts, key_low, preferred_element_type=jnp.float32)
    value_local = jnp.einsum("nd,ne->de", acts, value_low, preferred_element_type=jnp.float32)
    grad_acts = jnp.einsum("ne,de->nd", query_low, w_query, preferred_element_type=jnp.float32)
    grad_acts = grad_acts + jnp.einsum(
        "ne,de->nd", key_low, w_key, preferred_element_type=jnp.float32
    )
    grad_acts = grad_acts + jnp.einsum(
        "ne,de->nd", value_low, w_value, preferred_element_type=jnp.float32
    )
    _, pull_first = jax.vjp(root_norm, inputs, attn_gain)
    grad_inputs, attn_local = pull_first(grad_acts.reshape(seq_count, row_count, width))
    grad_inputs = grad_inputs + grad_middle
    query_sum, key_sum, value_sum, out_sum, gate_sum, up_sum, down_sum = (
        lax.psum_scatter(query_local, ("dp", "ctx"), scatter_dimension=0, tiled=True),
        lax.psum_scatter(key_local, ("dp", "ctx"), scatter_dimension=0, tiled=True),
        lax.psum_scatter(value_local, ("dp", "ctx"), scatter_dimension=0, tiled=True),
        lax.psum_scatter(out_turned, ("dp", "ctx"), scatter_dimension=0, tiled=True),
        lax.psum_scatter(gate_local, ("dp", "ctx"), scatter_dimension=0, tiled=True),
        lax.psum_scatter(up_local, ("dp", "ctx"), scatter_dimension=0, tiled=True),
        lax.psum_scatter(down_turned, ("dp", "ctx"), scatter_dimension=0, tiled=True),
    )
    attn_sum, q_sum, k_sum, ffn_sum = lax.psum(
        (attn_local, q_local, k_local, ffn_local), ("dp", "ctx")
    )
    return (
        result,
        grad_inputs,
        attn_sum,
        q_sum,
        k_sum,
        query_sum,
        key_sum,
        value_sum,
        out_sum.T,
        ffn_sum,
        gate_sum,
        up_sum,
        down_sum.T,
    )


LANES = 128
VMEM_LIMIT = 60 << 20
NN = ((1,), (0,))
NT = ((1,), (1,))
TN = ((0,), (0,))


def bf16_dot(left, right, dims):
    return lax.dot_general(left, right, (dims, ((), ())), preferred_element_type=jnp.float32)


def inverse_root(values):
    return lax.rsqrt(jnp.mean(values * values, axis=-1, keepdims=True) + EPS)


def lane_of(shape):
    return lax.broadcasted_iota(jnp.int32, shape, len(shape) - 1)


def head_mean(values, head_dim):
    rows = lax.broadcasted_iota(jnp.int32, (LANES, LANES), 0) // head_dim
    columns = lane_of((LANES, LANES)) // head_dim
    spread = jnp.where(rows == columns, 1.0 / head_dim, 0.0).astype(jnp.bfloat16)
    return bf16_dot(values.astype(jnp.bfloat16), spread, NN)


def partner(values, head_dim):
    half = head_dim // 2
    first = lane_of(values.shape) % head_dim < half
    return jnp.where(
        first, pltpu.roll(values, LANES - half, axis=1), pltpu.roll(values, half, axis=1)
    )


def head_turn(flat, gain, cosine, sine, head_dim):
    normed = flat * lax.rsqrt(head_mean(flat * flat, head_dim) + EPS) * gain
    return normed * cosine + partner(normed, head_dim) * sine


def head_turn_back(grad, flat, gain, cosine, sine, head_dim):
    back = grad * cosine + partner(grad * sine, head_dim)
    root = lax.rsqrt(head_mean(flat * flat, head_dim) + EPS)
    scaled = gain * back
    mean = head_mean(scaled * flat, head_dim)
    return (
        root * scaled - flat * (root * root * root * mean),
        jnp.sum(back * flat * root, axis=0, keepdims=True),
    )


def turns(freq, base_ref, starts):
    base_cos, base_sin = base_ref[0], base_ref[1]
    cosines, sines = [], []
    for start in starts:
        angle = jnp.asarray(start, jnp.float32) * freq[0:1, :]
        cos, sin = jnp.cos(angle), jnp.sin(angle)
        cosines.append(base_cos * cos - base_sin * sin)
        sines.append((base_sin * cos + base_cos * sin) * freq[1:2, :])
    return jnp.concatenate(cosines, axis=0), jnp.concatenate(sines, axis=0)


def whole_spec(shape):
    return pl.BlockSpec(shape, lambda *_: (0,) * len(shape))


def cost_of(inputs, outs, flops):
    moved = sum(item.size * item.dtype.itemsize for item in (*inputs, *outs))
    return pl.CostEstimate(flops=flops, bytes_accessed=moved, transcendentals=0)


class Arriving:
    def __init__(self, sources, targets, signals, ref):
        self.copies = [pltpu.make_async_copy(*item) for item in zip(sources, targets, signals)]
        self.ref, self.shape = ref, ref.shape
        for copy in self.copies:
            copy.start()

    def ready(self):
        for copy in self.copies:
            copy.wait()
        self.copies = []
        return self.ref

    def __getitem__(self, at):
        return self.ready()[at]


class Leaving:
    def __init__(self, ref, target, signal):
        self.ref, self.target, self.signal, self.shape = ref, target, signal, ref.shape
        self.copy = None

    def __setitem__(self, at, value):
        self.ref[at] = value

    def __getitem__(self, at):
        return self.ref[at]

    def leave(self):
        if self.copy is None:
            self.copy = pltpu.make_async_copy(self.ref, self.target, self.signal)
            self.copy.start()


class Part:
    def __init__(self, array, index):
        self.array, self.index = array, index
        self.shape = array.shape if index is None else array.shape[1:]


class Stack:
    def __init__(self, arrays):
        self.parts = [item if isinstance(item, Part) else Part(item, None) for item in arrays]
        self.arrays, self.dtype = [item.array for item in self.parts], self.parts[0].array.dtype
        self.shape = (len(arrays),) + self.parts[0].shape
        self.size = len(arrays) * math.prod(self.parts[0].shape)

    def of(self, refs):
        return [ref if item.index is None else ref.at[item.index] for ref, item in zip(refs, self.parts)]


class Rows:
    def __init__(self, array, scalar, rows=0):
        self.array, self.scalar, self.rows = array, scalar, rows
        self.shape = (rows,) + array.shape[1:] if rows else array.shape[1:]
        self.dtype, self.size = array.dtype, array.size

    def of(self, ref, scalars):
        at = scalars[self.scalar]
        if not self.rows:
            return ref.at[at]
        return ref.at[pl.ds(pl.multiple_of(at * self.rows, self.rows), self.rows)]


def kernel_call(body, scalars, inputs, outs, scratch, flops, name, held=(), stacks=()):
    arrays = [item.arrays if isinstance(item, Stack) else [getattr(item, "array", item)] for item in inputs]
    count, kept = sum(map(len, arrays)), len(held)

    def run(scalars_ref, *refs):
        given, refs = refs[:count], refs[count + kept :]
        targets, refs = refs[: len(outs)], refs[len(outs) :]
        stack_refs, refs = refs[: len(stacks)], refs[len(stacks) :]
        buffers, refs = refs[: len(inputs)], refs[len(inputs) :]
        results, refs = refs[: len(outs)], refs[len(outs) :]
        signals, own = refs[0], refs[1:]
        arriving, used = [], 0
        for item, group, buffer in zip(inputs, arrays, buffers):
            sources = list(given[used : used + len(group)])
            places = [buffer.at[at] for at in range(len(group))] if isinstance(item, Stack) else [buffer]
            if isinstance(item, Rows):
                sources = [item.of(sources[0], scalars_ref)]
            if isinstance(item, Stack):
                sources = item.of(sources)
            slots = [signals.at[used + at] for at in range(len(group))]
            arriving.append(Arriving(sources, places, slots, buffer))
            used += len(group)
        leaving = [
            Leaving(result, target, signals.at[count + at])
            for at, (result, target) in enumerate(zip(results, targets))
        ]
        body(scalars_ref, *arriving, *leaving, *stack_refs, *own)
        for item in arriving:
            item.ready()
        for item in leaving:
            item.leave()
        for item in leaving:
            item.copy.wait()

    near = pl.BlockSpec(memory_space=pl.ANY)
    far = pl.BlockSpec(memory_space=pltpu.HBM)
    return pl.pallas_call(
        run,
        in_specs=[pl.BlockSpec(memory_space=pltpu.SMEM)] + [near] * count + [far] * kept,
        out_specs=[far] * (len(outs) + len(stacks)),
        out_shape=[*outs, *stacks],
        scratch_shapes=[pltpu.VMEM(item.shape, item.dtype) for item in (*inputs, *outs)]
        + [pltpu.SemaphoreType.DMA((count + len(outs),))]
        + list(scratch),
        input_output_aliases={1 + count + at: len(outs) + at for at in range(kept)},
        cost_estimate=cost_of(inputs, (*outs, *stacks), flops),
        compiler_params=pltpu.CompilerParams(vmem_limit_bytes=VMEM_LIMIT),
        name=name,
    )(scalars, *[array for group in arrays for array in group], *held)


def shape_of(shape, dtype):
    return jax.ShapeDtypeStruct(shape, dtype)


def stacked(values):
    return jnp.concatenate(
        [values[:, at : at + LANES] for at in range(0, values.shape[1], LANES)], axis=0
    )


def key_value_rows(scalars, shard_refs, wk_ref, wv_ref, gain_ref, k_gain_ref, freq, base_ref, acts, kv, head_dim):
    count, rows = len(shard_refs), shard_refs[0].shape[0]
    for at, ref in enumerate(shard_refs):
        values = ref[...].astype(jnp.float32)
        acts[at] = (values * inverse_root(values) * gain_ref[...]).astype(jnp.bfloat16)
    cosine, sine = turns(freq, base_ref, [scalars[at] * rows for at in range(count)])
    flat = acts[...].reshape(count * rows, -1)
    left = lane_of((count * rows, LANES)) < head_dim
    keys = bf16_dot(flat, wk_ref[...], NN)
    values = bf16_dot(flat, wv_ref[...], NN)
    for chunk in range(wk_ref.shape[1] // LANES):
        at = slice(chunk * LANES, (chunk + 1) * LANES)
        turned = head_turn(keys[:, at], k_gain_ref[...], cosine, sine, head_dim)
        value = values[:, at]
        for odd in range(2):
            pair = jnp.where(
                left,
                pltpu.roll(turned, head_dim, axis=1) if odd else turned,
                value if odd else pltpu.roll(value, head_dim, axis=1),
            )
            start = (2 * chunk + odd) * LANES
            kv[:, :, start : start + LANES] = pair.astype(jnp.bfloat16).reshape(count, rows, LANES)


def key_value_body(count, head_dim, scalars, *refs):
    shard_ref, wk_ref, wv_ref, gain_ref, k_gain_ref, freq_ref, base_ref = refs[:7]
    acts_out, kv_out, acts, kv, signals = refs[7:]
    shards, freq = shard_ref.ready(), freq_ref[...]
    for ref in (wk_ref, wv_ref, gain_ref, k_gain_ref, base_ref):
        ref.ready()

    def one_pair(pair, carry):
        both = pl.ds(2 * pair, 2)
        key_value_rows(
            [scalars[2 * pair], scalars[2 * pair + 1]],
            [shards.at[2 * pair], shards.at[2 * pair + 1]],
            wk_ref,
            wv_ref,
            gain_ref,
            k_gain_ref,
            freq,
            base_ref,
            acts.at[both],
            kv.at[both],
            head_dim,
        )
        return carry

    lax.fori_loop(0, count // 2, one_pair, 0)
    leaving = [
        pltpu.make_async_copy(buffer.at[at], out.at[scalars[at]], signals.at[2 * at + turn])
        for at in range(count)
        for turn, (buffer, out) in enumerate(((acts, acts_out), (kv, kv_out)))
    ]
    for copy in leaving:
        copy.start()
    for copy in leaving:
        copy.wait()


def key_value_part(scalars, shards, weights, parts, head_dim, held):
    rows, width = shards[0].shape
    kv_width = 2 * weights[0].shape[1]
    count = len(shards)
    return kernel_call(
        lambda *refs: key_value_body(count, head_dim, *refs),
        scalars,
        [Stack(shards), *weights],
        [],
        [
            pltpu.VMEM((count, rows, width), jnp.bfloat16),
            pltpu.VMEM((count, rows, kv_width), jnp.bfloat16),
            pltpu.SemaphoreType.DMA((2 * count,)),
        ],
        2 * count * rows * width * kv_width,
        "key_value_part",
        held,
        [
            shape_of((parts, rows, width), jnp.bfloat16),
            shape_of((parts, rows, kv_width), jnp.bfloat16),
        ],
    )


def attend_body(known, fresh, head_dim, scalars, *refs):
    shard_refs, refs = refs[:fresh], refs[fresh:]
    wk_ref, wv_ref, gain_ref, k_gain_ref, freq_ref, base_ref, x_ref, wq_ref, q_gain_ref = refs[:9]
    kv_refs, refs = refs[9 : 9 + known], refs[9 + known :]
    out_ref, acts_out, acts, kv, bias, turned, signals = refs
    place, length = scalars[known + fresh], scalars[known + fresh + 1]
    rows = x_ref.shape[0]
    count = (known + fresh) * rows
    chunks = wq_ref.shape[1] // LANES
    freq = freq_ref[...]
    key_value_rows(
        [scalars[known + at] for at in range(fresh)],
        shard_refs,
        wk_ref,
        wv_ref,
        gain_ref,
        k_gain_ref,
        freq,
        base_ref,
        acts,
        kv.at[pl.ds(known, fresh)],
        head_dim,
    )
    leaving = [
        pltpu.make_async_copy(acts.at[at], acts_out.at[scalars[known + at]], signals.at[at])
        for at in range(fresh)
    ]
    for copy in leaving:
        copy.start()
    values = x_ref[...].astype(jnp.float32)
    own = (values * inverse_root(values) * gain_ref[...]).astype(jnp.bfloat16)
    tables = turns(freq, base_ref, [place * rows])
    cosine, sine = (jnp.concatenate([table] * chunks, axis=0) for table in tables)
    flat = stacked(bf16_dot(own, wq_ref[...], NN))
    turned[...] = (0.125 * head_turn(flat, q_gain_ref[...], cosine, sine, head_dim)).reshape(
        chunks, rows, LANES
    )
    query_pos = place * rows + lane_of((rows, 2 * rows)) % rows
    for slot in range(known + fresh):
        key_pos = scalars[slot] * rows + lax.broadcasted_iota(jnp.int32, (rows, 2 * rows), 0)
        bias[slot * rows : (slot + 1) * rows, :] = jnp.where(
            (key_pos <= query_pos) & (key_pos < length), 0.0, MASKED
        )
        if slot < known:
            kv[slot] = kv_refs[slot][...]
    left = lane_of((rows, LANES)) < head_dim

    def one_head(index, carry):
        at = pl.ds(pl.multiple_of(index * LANES, LANES), LANES)
        mine = turned[index]
        both = jnp.concatenate(
            [jnp.where(left, mine, 0.0), jnp.where(left, pltpu.roll(mine, head_dim, axis=1), 0.0)],
            axis=0,
        ).astype(jnp.bfloat16)
        head_kv = kv[:, :, at].reshape(count, LANES)
        scores = bf16_dot(head_kv, both, NT) + bias[...]
        top = jnp.max(scores, axis=0, keepdims=True)
        weights = jnp.exp(scores - top)
        total = jnp.sum(weights, axis=0, keepdims=True)
        summed = bf16_dot(head_kv, weights.astype(jnp.bfloat16), TN)[head_dim:] / total
        heads = jnp.concatenate([summed[:, :rows], summed[:, rows:]], axis=0)
        out_ref[:, at] = heads.T.astype(jnp.bfloat16)
        return carry

    lax.fori_loop(0, chunks, one_head, 0, unroll=2)
    for copy in leaving:
        copy.wait()


def attend(scalars, shards, x_own, early, weights, w_query, q_gain, head_dim):
    parts, rows, width = early[0].shape
    q_width, kv_width = w_query.shape[1], 2 * weights[0].shape[1]
    fresh = len(shards)
    known = parts - fresh
    blocks = [Rows(early[1], at) for at in range(known)]
    return kernel_call(
        lambda *refs: attend_body(known, fresh, head_dim, *refs),
        scalars,
        [*shards, *weights, x_own, w_query, q_gain, *blocks],
        [shape_of((rows, q_width), jnp.bfloat16)],
        [
            pltpu.VMEM((fresh, rows, width), jnp.bfloat16),
            pltpu.VMEM((parts, rows, kv_width), jnp.bfloat16),
            pltpu.VMEM((parts * rows, 2 * rows), jnp.float32),
            pltpu.VMEM((q_width // LANES, rows, LANES), jnp.float32),
            pltpu.SemaphoreType.DMA((fresh,)),
        ],
        2 * rows * width * (q_width + fresh * kv_width) + 4 * rows * parts * rows * q_width,
        "attend",
        [early[0]],
        [shape_of((parts, rows, width), jnp.bfloat16)],
    )


def ffn_terms(gate, up, grad_hidden):
    sig = 1.0 / (1.0 + jnp.exp(-gate))
    swish = gate * sig
    hidden = (swish * up).astype(jnp.bfloat16)
    grad_gate = (grad_hidden * up * (sig * (1.0 + gate * (1.0 - sig)))).astype(jnp.bfloat16)
    grad_up = (grad_hidden * swish).astype(jnp.bfloat16)
    return hidden, grad_gate, grad_up


def valid_rows(values, start, length):
    pos = start + lax.broadcasted_iota(jnp.int32, (values.shape[0], 1), 0)
    return jnp.where(pos < length, values.astype(jnp.float32), 0.0).astype(jnp.bfloat16)


def ffn_body(
    sums,
    first,
    last,
    scalars,
    x_ref,
    att_ref,
    cot_ref,
    w_out_ref,
    gain_ref,
    gate_ref,
    up_ref,
    down_ref,
    *refs,
):
    if not first:
        before, refs = refs[:2], refs[2:]
    outs, (mid, inner, grad_low, out_acc, inner_acc) = refs[:-5], refs[-5:]
    step = pl.program_id(0)
    gain = gain_ref[...]
    rows = x_ref.shape[0]

    @pl.when(step == 0)
    def _():
        middle = x_ref[...].astype(jnp.float32) + bf16_dot(att_ref[...], w_out_ref[...], NN)
        mid[...] = middle
        inner[...] = (middle * inverse_root(middle) * gain).astype(jnp.bfloat16)
        grad_low[...] = valid_rows(cot_ref[...], scalars[0] * rows, scalars[1])
        out_acc[...] = middle if first else before[0][...]
        inner_acc[...] = jnp.zeros_like(inner_acc) if first else before[1][...]

    gate_w, up_w, down_w = gate_ref[...], up_ref[...], down_ref[...]
    hidden, grad_gate, grad_up = ffn_terms(
        bf16_dot(inner[...], gate_w, NN),
        bf16_dot(inner[...], up_w, NN),
        bf16_dot(grad_low[...], down_w, NT),
    )
    out_acc[...] += bf16_dot(hidden, down_w, NN)
    inner_acc[...] += bf16_dot(grad_gate, gate_w, NT) + bf16_dot(grad_up, up_w, NT)

    @pl.when(step == pl.num_programs(0) - 1)
    def _():
        if not last:
            outs[0][...] = out_acc[...]
            outs[1][...] = inner_acc[...]
            return
        result_ref, grad_mid_ref, sent_ref, gain_grad_ref = outs
        result_ref[...] = out_acc[...].astype(jnp.bfloat16)
        middle = mid[...]
        grad_inner = inner_acc[...]
        root = inverse_root(middle)
        scaled = grad_inner * gain
        mean = jnp.mean(scaled * middle, axis=-1, keepdims=True)
        grad_mid = (
            grad_low[...].astype(jnp.float32) + root * scaled - middle * (root * root * root * mean)
        )
        grad_mid_ref[...] = grad_mid
        gain_grad_ref[...] = jnp.sum(grad_inner * middle * root, axis=0, keepdims=True)
        branch = grad_mid.astype(jnp.bfloat16)
        grad_att = bf16_dot(branch, w_out_ref[...], NT)
        parts = sent_ref.shape[0]
        each = grad_mid.shape[1] // (parts * sums)
        lane = lane_of((rows, LANES))
        for part in range(parts):
            head_at = slice(part * LANES, (part + 1) * LANES)
            sent_ref[part, :, :LANES] = grad_att[:, head_at].astype(jnp.bfloat16)
            picked = jnp.zeros((rows, LANES), jnp.float32)
            for block in range(sums):
                start = (block * parts + part) * each
                chunk = grad_mid[:, start // LANES * LANES : start // LANES * LANES + LANES]
                turn = (block * each - start % LANES) % LANES
                moved = pltpu.roll(chunk, turn, axis=1) if turn else chunk
                picked = jnp.where(lane // each == block, moved, picked)
            sent_ref[part, :, LANES:] = picked.astype(jnp.bfloat16)


def ffn_part(scalars, own, weights, blocks, chunk, before, last, parts, sums):
    rows, width = own[0].shape
    low, high = blocks
    w_gate, w_up, w_down = weights
    inputs = [*own, *weights, *before]
    specs = [whole_spec(item.shape) for item in own] + [
        pl.BlockSpec((width, chunk), lambda i, s: (0, i + low)),
        pl.BlockSpec((width, chunk), lambda i, s: (0, i + low)),
        pl.BlockSpec((chunk, width), lambda i, s: (i + low, 0)),
    ]
    specs += [whole_spec(item.shape) for item in before]
    outs = [shape_of((rows, width), jnp.float32)] * 2
    if last:
        outs = [
            shape_of((rows, width), jnp.bfloat16),
            shape_of((rows, width), jnp.float32),
            shape_of((parts, rows, 2 * LANES), jnp.bfloat16),
            shape_of((1, width), jnp.float32),
        ]
    return pl.pallas_call(
        lambda *refs: ffn_body(sums, not before, last, *refs),
        grid_spec=pltpu.PrefetchScalarGridSpec(
            num_scalar_prefetch=1,
            grid=(high - low,),
            in_specs=specs,
            out_specs=[whole_spec(item.shape) for item in outs],
            scratch_shapes=[
                pltpu.VMEM((rows, width), jnp.float32),
                pltpu.VMEM((rows, width), jnp.bfloat16),
                pltpu.VMEM((rows, width), jnp.bfloat16),
                pltpu.VMEM((rows, width), jnp.float32),
                pltpu.VMEM((rows, width), jnp.float32),
            ],
        ),
        out_shape=outs,
        cost_estimate=pl.CostEstimate(
            flops=12 * rows * width * chunk * (high - low),
            bytes_accessed=6 * width * chunk * (high - low),
            transcendentals=0,
        ),
        compiler_params=pltpu.CompilerParams(vmem_limit_bytes=VMEM_LIMIT),
        name="ffn_part",
    )(scalars, *inputs)


def factor_loop(count, scalars, refs, inner_ref, grad_ref, gate_ref, up_ref, hidden_ref):
    x_ref, att_ref, cot_ref, w_out_ref, gain_ref, gate_up_ref, down_ref = refs
    x_all, att_all, cot_all = x_ref.ready(), att_ref.ready(), cot_ref.ready()
    w_out, gain, gate_up, down = w_out_ref[...], gain_ref[...], gate_up_ref[...], down_ref[...]
    rows, padded = x_ref.shape[1], down_ref.shape[0]

    def one_pair(pair, carry):
        at = pl.ds(pl.multiple_of(2 * pair * rows, 2 * rows), 2 * rows)
        both = pl.ds(2 * pair, 2)
        middle = x_all[both].reshape(2 * rows, -1).astype(jnp.float32)
        middle = middle + bf16_dot(att_all[both].reshape(2 * rows, -1), w_out, NN)
        inner = (middle * inverse_root(middle) * gain).astype(jnp.bfloat16)
        grad_low = jnp.concatenate(
            [
                valid_rows(cot_all[2 * pair + odd], scalars[2 * pair + odd] * rows, scalars[count])
                for odd in range(2)
            ],
            axis=0,
        )
        wide = bf16_dot(inner, gate_up, NN)
        grad_hidden = bf16_dot(grad_low, down, NT)
        hidden, grad_gate, grad_up = ffn_terms(wide[:, :padded], wide[:, padded:], grad_hidden)
        inner_ref[at, :], grad_ref[at, :], hidden_ref[at, :] = inner, grad_low, hidden
        gate_ref[at, :], up_ref[at, :] = grad_gate, grad_up
        return carry

    lax.fori_loop(0, count // 2, one_pair, 0)


def factor_body(count, scalars, *refs):
    factor_loop(count, scalars, refs[:7], *[ref.ref for ref in refs[7:]])


def factor_part(scalars, x_shards, att_shards, cot_shards, weights):
    rows, width = x_shards[0].shape
    columns = weights[-1].shape[0]
    count = len(x_shards)
    outs = [shape_of((count * rows, width), jnp.bfloat16)] * 2
    outs += [shape_of((count * rows, columns), jnp.bfloat16)] * 3
    return kernel_call(
        lambda *refs: factor_body(count, *refs),
        scalars,
        [Stack(x_shards), Stack(att_shards), Stack(cot_shards), *weights],
        outs,
        [],
        2 * count * rows * width * (width + 3 * columns),
        "factor_part",
    )


def cut_copies(whole, kept_out, given_out, core, signals):
    size = whole.shape[0] // 4
    copies = []
    for index, (out, bit) in enumerate(((kept_out, core), (given_out, 1 - core))):
        for half in range(2):
            start = pl.multiple_of((2 * half + bit) * size, size)
            copies.append(
                pltpu.make_async_copy(
                    whole.at[pl.ds(start, size)],
                    out.at[pl.ds(half * size, size)],
                    signals.at[2 * index + half],
                )
            )
    for copy in copies:
        copy.start()
    return copies


def last_body(count, known, columns, scalars, *refs):
    left_ref, right_ref, kept_out, given_out, lefts, rights, found, whole, signals = refs[7:]
    core = scalars[count + 1]
    factor_loop(
        count, scalars, refs[:7], lefts.at[0], lefts.at[1], rights.at[0], rights.at[1], rights.at[2]
    )
    lefts_known, rights_known = left_ref.ready(), right_ref.ready()

    def product(index, carry):
        side = index // 2
        total = bf16_dot(rights[index], lefts[side], TN)
        for at in range(known):
            total = total + bf16_dot(rights_known[index * known + at], lefts_known[side * known + at], TN)
        found[index] = total.T.astype(jnp.bfloat16)
        return carry

    lax.fori_loop(0, 3, product, 0)
    for index in range(3):
        whole[:, index * columns : (index + 1) * columns] = found[index, :, :columns]
    for copy in cut_copies(whole, kept_out, given_out, core, signals):
        copy.wait()


def last_products(scalars, x_shards, att_shards, cot_shards, weights, before, columns):
    rows, width = x_shards[0].shape
    padded = weights[-1].shape[0]
    count = len(x_shards)
    total = 3 * columns + -3 * columns % LANES
    return kernel_call(
        lambda *refs: last_body(count, len(before), columns, *refs),
        scalars,
        [
            Stack(x_shards),
            Stack(att_shards),
            Stack(cot_shards),
            *weights,
            Stack([item[side] for side in (0, 1) for item in before]),
            Stack([item[side] for side in (2, 3, 4) for item in before]),
        ],
        [],
        [
            pltpu.VMEM((2, count * rows, width), jnp.bfloat16),
            pltpu.VMEM((3, count * rows, padded), jnp.bfloat16),
            pltpu.VMEM((3, width, padded), jnp.bfloat16),
            pltpu.VMEM((width, total), jnp.bfloat16),
            pltpu.SemaphoreType.DMA((4,)),
        ],
        2 * count * rows * width * (width + 3 * padded) + 12 * count * rows * width * columns,
        "last_products",
        (),
        [shape_of((width // 2, total), jnp.bfloat16)] * 2,
    )


def head_body(head_dim, scalars, *refs):
    w_ref, q_gain_ref, k_gain_ref, freq_ref, base_ref, acts_ref, came_ref, low_ref, gains_ref = refs[:9]
    flat_q, flat_kv, cosines, sines, queries, keys, values, query_grad, key_grad, value_grad = refs[9:]
    parts, rows, width = acts_ref.shape
    count = parts * rows
    length = scalars[1]
    span = 2 * rows
    blocks = count // span
    q_gain, k_gain, freq, w = q_gain_ref[...], k_gain_ref[...], freq_ref[...], w_ref[...]
    acts, base = acts_ref.ready(), base_ref.ready()
    left = lane_of((span, LANES)) < head_dim

    def rows_of(block):
        return pl.ds(pl.multiple_of(block * span, span), span)

    def project(block, carry):
        at = rows_of(block)
        cosine, sine = turns(freq, base, [block * span, block * span + rows])
        flat = bf16_dot(acts[pl.ds(2 * block, 2)].reshape(span, width), w, NN)
        query, kv = flat[:, :LANES], flat[:, LANES:]
        flat_q[at, :], flat_kv[at, :], cosines[at, :], sines[at, :] = query, kv, cosine, sine
        queries[at, :] = (0.125 * head_turn(query, q_gain, cosine, sine, head_dim)).astype(jnp.bfloat16)
        turned = head_turn(kv, k_gain, cosine, sine, head_dim)
        keys[at, :] = jnp.where(left, turned, pltpu.roll(turned, head_dim, axis=1)).astype(jnp.bfloat16)
        values[at, :] = jnp.where(left, pltpu.roll(kv, head_dim, axis=1), kv).astype(jnp.bfloat16)
        key_grad[at, :] = jnp.zeros((span, LANES), jnp.float32)
        value_grad[at, :] = jnp.zeros((span, LANES), jnp.float32)
        return carry

    lax.fori_loop(0, blocks, project, 0)
    came = came_ref.ready()
    nothing = jnp.zeros((span, LANES), jnp.bfloat16)
    for block in range(blocks):
        extent = (block + 1) * span
        at = slice(block * span, extent)
        query_grad[...] = jnp.zeros_like(query_grad)

        def one_head(head, carry, extent=extent, at=at, block=block):
            key_pos = lax.broadcasted_iota(jnp.int32, (extent, span), 0)
            query_pos = block * span + lane_of((extent, span))
            counted = (key_pos <= query_pos) & (key_pos < length)
            mine = (lane_of((span, LANES)) // head_dim) == head
            query = jnp.where(mine, queries[at, :], nothing)
            grad = jnp.where(mine, came[2 * block : 2 * block + 2, :, :LANES].reshape(span, LANES), nothing)
            scores = jnp.where(counted, bf16_dot(keys[:extent, :], query, NT), MASKED)
            top = jnp.max(scores, axis=0, keepdims=True)
            weights = jnp.exp(scores - top)
            probs = weights * (1.0 / jnp.sum(weights, axis=0, keepdims=True))
            grad_probs = bf16_dot(values[:extent, :], grad, NT)
            delta = jnp.sum(probs * grad_probs, axis=0, keepdims=True)
            grad_scores = (probs * (grad_probs - delta)).astype(jnp.bfloat16)
            value_grad[:extent, :] += bf16_dot(probs.astype(jnp.bfloat16), grad, NN)
            key_grad[:extent, :] += bf16_dot(grad_scores, query, NN)
            own = (lane_of((extent, LANES)) // head_dim) == head
            key = jnp.where(own, keys[:extent, :], jnp.zeros((extent, LANES), jnp.bfloat16))
            query_grad[...] += bf16_dot(key, grad_scores, TN)
            return carry

        lax.fori_loop(0, 2, one_head, 0, unroll=2)
        sines_at, cosines_at = sines[at, :], cosines[at, :]
        low, q_part = head_turn_back(
            0.125 * query_grad[...].T, flat_q[at, :], q_gain, cosines_at, sines_at, head_dim
        )
        low_ref[2 * block : 2 * block + 2, :, :LANES] = low.astype(jnp.bfloat16).reshape(2, rows, LANES)
        gains_ref[0:1, :] = q_part if block == 0 else gains_ref[0:1, :] + q_part

    def finish(block, total):
        at = rows_of(block)
        key, value = key_grad[at, :], value_grad[at, :]
        key = key + pltpu.roll(key, head_dim, axis=1)
        value = value + pltpu.roll(value, head_dim, axis=1)
        low, part = head_turn_back(key, flat_kv[at, :], k_gain, cosines[at, :], sines[at, :], head_dim)
        both = jnp.where(left, low, value).astype(jnp.bfloat16).reshape(2, rows, LANES)
        low_ref.ref[pl.ds(2 * block, 2), :, LANES:] = both
        return total + part

    gains_ref[1:2, :] = lax.fori_loop(0, blocks, finish, jnp.zeros((1, LANES), jnp.float32))


def head_gradients(scalars, acts, w_head, q_gain, k_gain, freq, base, came, head_dim):
    parts, rows, width = acts.shape
    count = parts * rows
    return kernel_call(
        lambda *refs: head_body(head_dim, *refs),
        scalars,
        [w_head, q_gain, k_gain, freq, base, acts, came],
        [
            shape_of((parts, rows, 2 * LANES), jnp.bfloat16),
            shape_of((8, LANES), jnp.float32),
        ],
        [pltpu.VMEM((count, LANES), jnp.float32)] * 4
        + [pltpu.VMEM((count, LANES), jnp.bfloat16)] * 3
        + [pltpu.VMEM((LANES, 2 * rows), jnp.float32)]
        + [pltpu.VMEM((count, LANES), jnp.float32)] * 2,
        4 * count * width * LANES + 14 * count * count * head_dim,
        "head_gradients",
    )


def token_grad_body(head_dim, *refs):
    back_ref, wq_ref, wk_ref, wv_ref, x_ref, grad_mid_ref, gain_ref, out_ref = refs
    parts = back_ref.shape[0]
    back = back_ref.ready()
    left = lane_of((back.shape[1], LANES)) < head_dim
    keys, values = [], []
    for part in range(0, parts, 2):
        even = back[part, :, LANES:].astype(jnp.float32)
        odd = back[part + 1, :, LANES:].astype(jnp.float32)
        keys.append(jnp.where(left, even, pltpu.roll(odd, head_dim, axis=1)).astype(jnp.bfloat16))
        values.append(jnp.where(left, pltpu.roll(even, head_dim, axis=1), odd).astype(jnp.bfloat16))
    queries = [back[part, :, :LANES] for part in range(parts)]
    grad = (
        bf16_dot(jnp.concatenate(queries, axis=1), wq_ref[...], NT)
        + bf16_dot(jnp.concatenate(keys, axis=1), wk_ref[...], NT)
        + bf16_dot(jnp.concatenate(values, axis=1), wv_ref[...], NT)
    )
    values = x_ref[...].astype(jnp.float32)
    root = inverse_root(values)
    scaled = grad * gain_ref[...]
    mean = jnp.mean(scaled * values, axis=-1, keepdims=True)
    out_ref[...] = grad_mid_ref[...] + root * scaled - values * (root * root * root * mean)


def head_products_body(sources, head_dim, scalars, *refs):
    low_ref, acts_ref, w_ref, came_ref = refs[:4]
    att_ref, refs = refs[4], refs[5:]
    token_refs, refs = refs[:7], refs[7:]
    gain_ref, grad_tokens_ref, kept_out, given_out, out_kept, out_given, proj, outer, signals = refs
    parts, rows, width = acts_ref.shape
    count = parts * rows
    core = scalars[sources]
    low = low_ref[...].reshape(count, 2 * LANES)
    turned = bf16_dot(low, acts_ref[...].reshape(count, width), TN).T
    proj[...] = turned.astype(jnp.bfloat16)
    copies = cut_copies(proj, kept_out, given_out, core, signals.at[pl.ds(0, 4)])
    gain_ref[...] = jnp.sum(turned * w_ref[...].astype(jnp.float32), axis=-1, keepdims=True)
    total = None
    came = came_ref.ready()
    for slot in range(sources):
        branch = came[scalars[slot], :, LANES:]
        term = bf16_dot(branch, att_ref[slot], TN)
        total = term if total is None else total + term
    outer[...] = total.astype(jnp.bfloat16)
    copies += cut_copies(outer, out_kept, out_given, core, signals.at[pl.ds(4, 4)])
    token_grad_body(head_dim, *token_refs, grad_tokens_ref)
    for copy in copies:
        copy.wait()


def head_products(scalars, low, acts, came, w_head, att_shards, token_inputs, head_dim):
    parts, rows, width = acts.shape
    out_width = att_shards[0].shape[1]
    return kernel_call(
        lambda *refs: head_products_body(len(att_shards), head_dim, *refs),
        scalars,
        [low, acts, w_head, came, Stack(att_shards), *token_inputs],
        [
            shape_of((width, 1), jnp.float32),
            shape_of((rows, width), jnp.float32),
        ],
        [
            pltpu.VMEM((width, 2 * LANES), jnp.bfloat16),
            pltpu.VMEM((LANES, out_width), jnp.bfloat16),
            pltpu.SemaphoreType.DMA((8,)),
        ],
        6 * parts * rows * width * LANES + 4 * rows * width * width,
        "head_products",
        (),
        [shape_of((width // 2, 2 * LANES), jnp.bfloat16)] * 2
        + [shape_of((LANES // 2, out_width), jnp.bfloat16)] * 2,
    )


def spread_body(columns, count, scalars, came_ref, *outs):
    for part in range(came_ref.shape[0]):
        for index in range(count):
            piece = came_ref[part, :, index * columns : (index + 1) * columns].astype(jnp.float32)
            outs[index][:, part * columns : (part + 1) * columns] = piece


def spread_out(scalars, came, columns, count):
    parts, rows, width = came.shape
    outs = [shape_of((rows, parts * columns), jnp.float32)] * count
    return kernel_call(
        lambda *refs: spread_body(columns, count, *refs),
        scalars,
        [came],
        outs,
        [],
        0,
        "spread_out",
    )


def joined_body(parts, head_dim, scalars, *refs):
    came_refs, outs = refs[:parts], refs[parts:-2]
    joined, signals = refs[-2:]
    copies = [
        pltpu.make_async_copy(ref.ready(), joined.at[(scalars[0] + parts - at) % parts], signals.at[at])
        for at, ref in enumerate(came_refs)
    ]
    for copy in copies:
        copy.start()
    for copy in copies:
        copy.wait()
    query_ref, key_ref, value_ref, gain_ref = outs
    total = None
    for part in range(parts):
        piece = joined[part, :, : 2 * LANES].astype(jnp.float32)
        query_ref[:, part * LANES : (part + 1) * LANES] = piece[:, :LANES]
        at = slice(part * head_dim, (part + 1) * head_dim)
        key_ref[:, at] = piece[:, LANES : LANES + head_dim]
        value_ref[:, at] = piece[:, LANES + head_dim :]
        gain = joined[part, :, 2 * LANES :].astype(jnp.float32)
        total = gain if total is None else total + gain
    gain_ref[...] = total


def joined_out(scalars, came, head_dim):
    parts, (rows, width) = len(came), came[0].shape
    outs = [shape_of((rows, parts * size), jnp.float32) for size in (LANES, head_dim, head_dim)]
    outs.append(shape_of((rows, width - 2 * LANES), jnp.float32))
    return kernel_call(
        lambda *refs: joined_body(parts, head_dim, *refs),
        scalars,
        came,
        outs,
        [pltpu.VMEM((parts, rows, width), jnp.bfloat16), pltpu.SemaphoreType.DMA((parts,))],
        0,
        "joined_out",
    )


def cut_body(parts, scalars, mine_ref, got_ref, gain_ref, *refs):
    outs, (joined, signals) = refs[:parts], refs[parts:]
    each = joined.shape[1]
    width = mine_ref.shape[1]
    total = mine_ref[...].astype(jnp.float32) + got_ref[...].astype(jnp.float32)
    joined[:, :, :width] = total.astype(jnp.bfloat16).reshape(parts, each, width)
    for part in range(parts):
        joined[part, :, width:] = gain_ref[...]
    copies = [
        pltpu.make_async_copy(joined.at[(scalars[0] + at) % parts], out, signals.at[at])
        for at, out in enumerate(outs)
    ]
    for copy in copies:
        copy.start()
    for copy in copies:
        copy.wait()


def cut_blocks(scalars, mine, got, gains, parts):
    rows, width = mine.shape
    each = rows // parts
    total = width + gains.shape[1]
    outs = [shape_of((each, total), jnp.bfloat16)] * parts
    return kernel_call(
        lambda *refs: cut_body(parts, *refs),
        scalars,
        [mine, got, gains],
        [],
        [pltpu.VMEM((parts, each, total), jnp.bfloat16), pltpu.SemaphoreType.DMA((parts,))],
        0,
        "cut_blocks",
        (),
        outs,
    )


def swapped(value, axis, by):
    count = lax.axis_size(axis)
    return lax.ppermute(value, axis, [(i, i ^ by) for i in range(count)])


def after(value, *others):
    return lax.optimization_barrier((value, *others))[0]


def split_form(
    tokens,
    lengths,
    attn_gain,
    q_gain,
    k_gain,
    w_query,
    w_key,
    w_value,
    w_out,
    ffn_gain,
    w_gate,
    w_up,
    w_down,
    cotangent,
):
    _, rows, width = tokens.shape
    head_dim = q_gain.shape[0]
    hidden_width = w_gate.shape[1]
    parts = lax.axis_size("ctx")
    sums = lax.axis_size("dp")
    place = lax.axis_index("ctx").astype(jnp.int32)
    row = lax.axis_index("dp").astype(jnp.int32)
    core, line = row % 2, row // 2
    length = lengths[0]
    columns = hidden_width // parts
    each = width // (sums * parts)
    steps = parts // 2
    sources = [((place - 2 * (slot // 2)) % parts) ^ (slot % 2) for slot in range(parts)]
    freq = THETA ** (-(jnp.arange(head_dim // 2, dtype=jnp.float32) * 2.0 / head_dim))
    sign = jnp.ones_like(freq)
    freq = jnp.stack([jnp.concatenate([freq] * 4), jnp.concatenate([-sign, sign, -sign, sign])])
    base = jnp.arange(rows, dtype=jnp.float32)[:, None] * freq[0:1]
    base = jnp.stack([jnp.cos(base), jnp.sin(base)])
    attn_row, ffn_row = attn_gain[None], ffn_gain[None]
    q_row = jnp.concatenate([q_gain, q_gain])[None]
    k_row = jnp.concatenate([k_gain, k_gain])[None]
    x_own, cot_own = tokens[0], cotangent[0]

    def own_columns(weights, size, axis):
        return lax.dynamic_slice_in_dim(weights, place * size, size, axis)

    w_head = jnp.concatenate(
        [
            own_columns(w_query, LANES, 1),
            own_columns(w_key, head_dim, 1),
            own_columns(w_value, head_dim, 1),
        ],
        axis=-1,
    )
    spare = -columns % LANES
    wide = columns + spare
    gate_up = jnp.concatenate(
        [
            jnp.pad(own_columns(w_gate, columns, 1), ((0, 0), (0, spare))),
            jnp.pad(own_columns(w_up, columns, 1), ((0, 0), (0, spare))),
        ],
        axis=-1,
    )
    down = jnp.pad(own_columns(w_down, columns, 0), ((0, spare), (0, 0)))

    half = parts // 2
    kv_weights = [w_key, w_value, attn_row, k_row, freq, base]

    def key_values(low, high, held):
        return key_value_part(
            jnp.stack(sources[low:high]), x_shards[low:high], kv_weights, parts, head_dim, held
        )

    held, x_shards, early = x_own, [], None
    for step in range(steps):
        if step:
            held = from_behind(held, "ctx", 2)
        other = held
        if step == steps - 1:
            early = key_values(0, half, ())
            other = after(held, early[0], gate_up, down, w_head, x_shards[-1])
        x_shards += [held, swapped(other, "ctx", 1)]
    fresh = 2 if parts - 2 > half else parts - half
    if parts - fresh > half:
        early = key_values(half, parts - fresh, early)
    attn_low, acts = attend(
        jnp.stack(sources + [place, length]),
        x_shards[parts - fresh :],
        x_own,
        early,
        kv_weights,
        w_query,
        q_row,
        head_dim,
    )
    where = jnp.stack([place, length])

    def along(shard):
        return [shard] + [from_behind(shard, "ctx", 2 * step) for step in range(1, steps)]

    def across(shards):
        if len(shards) == 1:
            return [swapped(shards[0], "ctx", 1)]
        joined = swapped(jnp.stack(shards), "ctx", 1)
        return [Part(joined, at) for at in range(len(shards))]

    def arrays_of(shards):
        return [shard.array if isinstance(shard, Part) else shard for shard in shards]

    cot_ready = after(cot_own, *x_shards[-2:], early[0])
    cot_along = along(cot_ready)
    cot_across = across(cot_along[:1])
    attn_low = after(attn_low, *cot_along, *cot_across)
    att_along = along(attn_low)
    att_across = across(att_along[:1])
    cot_across += across([after(shard, attn_low) for shard in cot_along[1:]])
    chunk = next(c for c in (512, 384, 256, 128) if hidden_width % c == 0)
    turned_to = sources[0::2] + sources[1::2]
    slots = jnp.stack(turned_to + [core, length])
    weights = [w_out, ffn_row, gate_up, down]
    x_along, x_across = x_shards[0::2], x_shards[1::2]
    result, grad_mid, sent, ffn_gain_part = ffn_part(
        where,
        [x_own, attn_low, cot_own, w_out, ffn_row],
        [w_gate, w_up, w_down],
        (0, hidden_width // chunk),
        chunk,
        [],
        True,
        parts,
        sums,
    )
    sent = after(sent, *att_along[1:], *att_across, *arrays_of(cot_across[1:2]))
    came = lax.all_to_all(sent, "ctx", 0, 0, tiled=True)
    att_across += across([after(shard, sent) for shard in att_along[1:]])
    factors = [
        factor_part(
            jnp.stack(turned_to[:steps] + [length]),
            [after(x_along[0], sent)] + x_along[1:],
            att_along,
            cot_along,
            weights,
        )
    ]
    came = after(came, factors[0][0])
    low, head_gains = head_gradients(
        where, acts, w_head, q_row, k_row, freq, base, came, head_dim
    )
    low = after(low, *arrays_of(att_across[1:2]))
    back = lax.all_to_all(low, "ctx", 0, 0, tiled=True)
    def core_sum(kept, given):
        total = kept.astype(jnp.float32) + swapped(given, "dp", 1).astype(jnp.float32)
        return total.astype(jnp.bfloat16)

    def line_halves(half):
        size = half.shape[0] // 2
        mine = lax.dynamic_slice_in_dim(half, line * size, size, 0)
        return mine, lax.dynamic_slice_in_dim(half, (1 - line) * size, size, 0)

    def line_sum(half):
        mine, other = line_halves(half)
        return mine.astype(jnp.float32) + swapped(other, "dp", 2).astype(jnp.float32)

    kept, given = last_products(
        jnp.stack(turned_to[steps:] + [length, core]),
        [after(x_across[0], low)] + x_across[1:],
        att_across,
        cot_across,
        weights,
        factors,
        columns,
    )
    wide_half = core_sum(kept, after(given, back))
    wide_mine, wide_other = line_halves(wide_half)
    wide_got = swapped(wide_other, "dp", 2)
    attn_part, grad_tokens, head_kept, head_given, out_kept, out_given = head_products(
        slots,
        after(low, wide_other),
        acts,
        came,
        w_head,
        att_along + att_across,
        [back, w_query, w_key, w_value, x_own, grad_mid, attn_row],
        head_dim,
    )
    wide_sum = after(wide_mine, head_kept).astype(jnp.float32) + wide_got.astype(jnp.float32)
    wide_sum = wide_sum.astype(jnp.bfloat16).reshape(parts, each, -1)
    wide_came = lax.all_to_all(wide_sum, "ctx", 0, 0, tiled=True)
    head_half = core_sum(head_kept, after(head_given, wide_sum))
    out_half = core_sum(out_kept, after(out_given, wide_sum))
    gains = jnp.concatenate(
        [
            attn_part[:, 0] / attn_gain,
            ffn_gain_part[0],
            head_gains[0, :head_dim] + head_gains[0, head_dim:],
            head_gains[1, :head_dim],
        ]
    )
    gain_count = gains.shape[0]
    gains = after(gains, wide_sum)
    gains = gains + swapped(gains, "dp", 1)
    head_mine, head_other = line_halves(head_half)

    def high_low(values, columns_at):
        high = lax.reduce_precision(values, 8, 7)
        both = jnp.concatenate([high, values - high]).astype(jnp.bfloat16)
        room = -(-both.shape[0] // (16 * columns_at)) * 16
        return jnp.pad(both, (0, room * columns_at - both.shape[0])).reshape(room, columns_at)

    packed = jnp.concatenate([head_other, high_low(gains, head_other.shape[1])])
    got = swapped(packed, "dp", 2)
    head_got, gains_got = got[: head_other.shape[0]], got[head_other.shape[0] :].reshape(-1)
    gains = gains + gains_got[:gain_count].astype(jnp.float32)
    gains = gains + gains_got[gain_count : 2 * gain_count].astype(jnp.float32)
    out_sum = line_sum(out_half)
    pieces = high_low(gains, each * LANES // 32).reshape(-1)
    room = -(-pieces.shape[0] // (each * LANES)) * LANES
    pieces = jnp.pad(pieces, (0, each * room - pieces.shape[0])).reshape(each, room)
    leaving = cut_blocks(place[None], head_mine, head_got, pieces, parts)
    last = [leaving[0]] + [from_behind(leaving[at], "ctx", at) for at in range(1, parts)]
    query_out, key_out, value_out, totals = joined_out(place[None], last, head_dim)
    gate_sum, up_sum, down_out = spread_out(place[None], wide_came, columns, 3)
    totals = totals.reshape(-1)
    totals = totals[:gain_count] + totals[gain_count : 2 * gain_count]
    return (
        result[None],
        grad_tokens[None],
        totals[:width],
        totals[2 * width : 2 * width + head_dim],
        totals[2 * width + head_dim :],
        query_out,
        key_out,
        value_out,
        out_sum.T,
        totals[width : 2 * width],
        gate_sum,
        up_sum,
        down_out.T,
    )


def per_device(*arguments):
    tokens, q_gain, w_query, w_key = (arguments[i] for i in (0, 3, 5, 6))
    parts = lax.axis_size("ctx")
    sums = lax.axis_size("dp")
    head_dim = q_gain.shape[0]
    fits = (
        tokens.shape[0] == 1
        and sums == 4
        and parts % 2 == 0
        and 2 * head_dim == LANES
        and w_query.shape[1] == parts * LANES
        and w_key.shape[1] == parts * head_dim
        and tokens.shape[2] == sums * parts * 32
        and tokens.shape[1] == LANES
        and parts <= 8
    )
    return (split_form if fits else ring_form)(*arguments)


def solution(mesh):
    placed = (
        P("dp", "ctx", None),
        P("dp"),
        P(),
        P(),
        P(),
        P(),
        P(),
        P(),
        P(),
        P(),
        P(),
        P(),
        P(),
        P("dp", "ctx", None),
    )
    return jax.shard_map(
        per_device,
        mesh=mesh,
        in_specs=placed,
        out_specs=(
            P("dp", "ctx", None),
            P("dp", "ctx", None),
            P(),
            P(),
            P(),
            P(("dp", "ctx"), None),
            P(("dp", "ctx"), None),
            P(("dp", "ctx"), None),
            P(None, ("dp", "ctx")),
            P(),
            P(("dp", "ctx"), None),
            P(("dp", "ctx"), None),
            P(None, ("dp", "ctx")),
        ),
        check_vma=False,
    )
```
